32 devices in a mesh: ctx: 16 (over z, y, x), tp: 2 (over core).
Axes of the slice: x: 2, y: 2, z: 4, core: 2. Of those that a mesh axis runs over, the one named last changes fastest.
Arguments:
- ssm_input: bfloat16 [2048, 8192], P('ctx', 'tp'), may hold values from -40 to 40
- ssm_gate: bfloat16 [2048, 8192], P('ctx', 'tp'), may hold values from -4 to 4
- state_write: bfloat16 [2048, 128], P('ctx'), may hold values from -0.5 to 0.5
- state_read: bfloat16 [2048, 128], P('ctx'), may hold values from -0.5 to 0.5
- log_decay: float32 [2048, 32], P('ctx', 'tp'), may hold values from -4 to 0
- skip_gain: float32 [32], P('tp'), may hold values from 0.5 to 1.5
- norm_gain: float32 [8192], P('tp'), may hold values from 0.1 to 1.9
- ssm_cotangent: bfloat16 [2048, 8192], P('ctx', 'tp'), may hold values from -6 to 6
- queries: bfloat16 [2048, 8192], P('ctx', 'tp'), may hold values from -5 to 5
- key_states: bfloat16 [2048, 1024], P('ctx', 'tp'), may hold values from -5 to 5
- value_states: bfloat16 [2048, 1024], P('ctx', 'tp'), may hold values from -6 to 6
- attn_cotangent: bfloat16 [2048, 8192], P('ctx', 'tp'), may hold values from -6 to 6
Outputs:
- ssm_output: bfloat16 [2048, 8192], P('ctx', 'tp')
- input_grad: bfloat16 [2048, 8192], P('ctx', 'tp')
- gate_grad: bfloat16 [2048, 8192], P('ctx', 'tp')
- write_grad: float32 [2048, 128], P('ctx')
- read_grad: float32 [2048, 128], P('ctx')
- attn_output: bfloat16 [2048, 8192], P('ctx', 'tp')
- query_grad: bfloat16 [2048, 8192], P('ctx', 'tp')
- key_grad: bfloat16 [2048, 1024], P('ctx', 'tp')
- value_grad: bfloat16 [2048, 1024], P('ctx', 'tp')
The draws below stay inside these ranges and needn't reach their ends.
All inputs are finite; a program needn't handle non-finite values.
Results may differ from the reference program's by a relative error of at most 0.035.
Values may be sent and summed in bfloat16 or wider, within the bound.
A program may use at most 192 MiB of HBM per device.

```python
import math
from functools import partial
import jax
import jax.numpy as jnp
from jax import lax

STATE_HEADS = 32
P_SIZE = 256
NS = 128
QH = 64
KVH = 8
HD = 128
TOK_DEV = 128
HF = 64
TOKEN_COUNT = 2048
CH = 8192
N_CTX = 16


def draw_ssm_input(key, part):
    random_subkeys = jax.random.split(key, 3)
    column = jnp.arange(CH, dtype=jnp.float32) / CH
    col_scale = 0.5 * jnp.exp(math.log(3.0) * column + jax.random.uniform(random_subkeys[2], (CH,), minval=-0.7, maxval=0.7))
    base_draw = jnp.clip(jax.random.normal(random_subkeys[0], (TOKEN_COUNT, CH)), -4.0, 4.0)
    row_scale = jnp.exp(jax.random.uniform(random_subkeys[1], (TOKEN_COUNT, 1), minval=math.log(0.3), maxval=math.log(3.0)))
    return (base_draw * row_scale * col_scale[None, :]).astype(jnp.bfloat16)


def draw_log_decay(key, part):
    random_subkeys = jax.random.split(key, 7)
    order = jax.random.permutation(random_subkeys[0], STATE_HEADS)
    fast_heads = order < STATE_HEADS // 2
    fast_rate = jax.random.uniform(random_subkeys[1], (STATE_HEADS,), minval=2.0, maxval=3.0) / HF
    slow_rate = jnp.exp(jax.random.uniform(random_subkeys[2], (STATE_HEADS,), minval=math.log(1.0 / (16 * TOKEN_COUNT)), maxval=math.log(1.0 / (4 * TOKEN_COUNT))))
    decay_speed = jnp.where(fast_heads, fast_rate, slow_rate)
    coarse_estimate = jax.random.uniform(random_subkeys[3], (TOKEN_COUNT, STATE_HEADS), minval=0.5, maxval=2.0)
    block_draw = jax.random.uniform(random_subkeys[4], (TOKEN_COUNT // HF, STATE_HEADS), minval=0.5, maxval=2.0)
    block_multiplier = jnp.repeat(block_draw, HF, axis=0)
    spike_positions = jax.random.randint(random_subkeys[5], (3,), 0, TOKEN_COUNT)
    spike_rows = jnp.any(jnp.arange(TOKEN_COUNT)[:, None] == spike_positions[None, :], axis=1)
    spike_loss = jnp.log(jax.random.uniform(random_subkeys[6], (TOKEN_COUNT, STATE_HEADS), minval=0.5, maxval=0.8))
    return -decay_speed[None, :] * coarse_estimate * block_multiplier + jnp.where(spike_rows[:, None], spike_loss, 0.0)


def draw_queries(key, part):
    return jnp.clip(jax.random.normal(jax.random.fold_in(key, 11), (TOKEN_COUNT, QH * HD)), -4.0, 4.0).astype(jnp.bfloat16)


def draw_key_states(key, part):
    return jnp.clip(jax.random.normal(jax.random.fold_in(key, 13), (TOKEN_COUNT, KVH * HD)), -4.0, 4.0).astype(jnp.bfloat16)


def block_scale(own_key, dims, cuts, smallest, high):
    def one(axis_at, shards_of):
        steps = jax.random.uniform(jax.random.fold_in(jax.random.fold_in(own_key, 6), axis_at), (shards_of,), jnp.float32, smallest / len(cuts), high / len(cuts))
        return jnp.repeat(jnp.exp(steps), dims[axis_at] // shards_of).reshape((-1,) + (1,) * (len(dims) - axis_at - 1))

    factor_of = one(*cuts[0])
    for cut in cuts[1:]:
        factor_of = factor_of * one(*cut)
    return factor_of


def gaussian(stream_key, shape, deviation, bound, cuts=(), kind=jnp.bfloat16):
    result = jax.random.normal(stream_key, shape, jnp.float32) * deviation
    if len(cuts) > 0:
        result = block_scale(stream_key, shape, cuts, -0.22, 0.18) * result
    return jnp.clip(result, min=-bound, max=bound).astype(kind)


def setup_inputs(seed: int = 0) -> dict:
    arg_keys = jax.random.split(jax.random.key(seed), 13)
    ssm_input = draw_ssm_input(jax.random.fold_in(arg_keys[12], 71), 0)
    ssm_gate = gaussian(arg_keys[1], (TOKEN_COUNT, CH), 1.0, 4.0, ((0, 16), (1, 2)))
    state_write = gaussian(arg_keys[2], (TOKEN_COUNT, NS), NS ** -0.5, 0.5, ((0, 16),))
    state_read = gaussian(arg_keys[3], (TOKEN_COUNT, NS), NS ** -0.5, 0.5, ((0, 16),))
    log_decay = draw_log_decay(jax.random.fold_in(arg_keys[12], 71), 0)
    skip_gain = jnp.clip(0.5 + 1.0 * jax.random.uniform(arg_keys[5], (STATE_HEADS,), jnp.float32) ** block_scale(arg_keys[5], (STATE_HEADS,), ((0, 2),), -0.2, 0.2), 0.5, 1.5)
    norm_gain = jnp.clip(1.0 + 0.18 * jax.random.normal(arg_keys[6], (CH,), jnp.float32), 0.1, 1.9)
    ssm_cotangent = gaussian(arg_keys[7], (TOKEN_COUNT, CH), 1.0, 6.0, ((0, 16), (1, 2)))
    queries = draw_queries(jax.random.fold_in(arg_keys[12], 71), 0)
    key_states = draw_key_states(jax.random.fold_in(arg_keys[12], 71), 0)
    value_states = gaussian(arg_keys[10], (TOKEN_COUNT, KVH * HD), 1.0, 6.0, ((0, 16), (1, 2)))
    attn_cotangent = gaussian(arg_keys[11], (TOKEN_COUNT, QH * HD), 1.0, 6.0, ((0, 16), (1, 2)))
    return dict(ssm_input=ssm_input, ssm_gate=ssm_gate, state_write=state_write, state_read=state_read, log_decay=log_decay, skip_gain=skip_gain, norm_gain=norm_gain, ssm_cotangent=ssm_cotangent, queries=queries, key_states=key_states, value_states=value_states, attn_cotangent=attn_cotangent)


PRECISE = lax.Precision.HIGHEST
NEGATIVE = -1e+30
EPSILON = 1e-05

def sequence_rows():
    position = jnp.arange(TOKEN_COUNT, dtype=jnp.int32)
    block_id = position // HF
    device_id = jnp.where(block_id < N_CTX, block_id, 2 * N_CTX - 1 - block_id)
    second = jnp.where(block_id < N_CTX, 0, 1)
    return (device_id * TOK_DEV + second * HF + position % HF).astype(jnp.int32)

def folded_rows():
    row_id = jnp.arange(TOKEN_COUNT, dtype=jnp.int32)
    device_id = row_id // TOK_DEV
    local_id = row_id % TOK_DEV
    block_id = jnp.where(local_id < HF, device_id, 2 * N_CTX - 1 - device_id)
    return (block_id * HF + local_id % HF).astype(jnp.int32)

def block_step(zero_state, pieces):
    input_block, write_block, read_block, decay_block = pieces
    log_total = jnp.cumsum(decay_block, axis=0)
    log_gap = log_total[:, None, :] - log_total[None, :, :]
    causal = jnp.arange(HF)[:, None] >= jnp.arange(HF)[None, :]
    decay = jnp.exp(jnp.where(causal[:, :, None], log_gap, NEGATIVE))
    read_write = jnp.dot(read_block, write_block.T, precision=PRECISE)
    weights = decay * read_write[:, :, None]
    mixed = jnp.einsum('tsh,shp->thp', weights, input_block, precision=PRECISE)
    mixed = mixed + jnp.exp(log_total)[:, :, None] * jnp.einsum('hpn,tn->thp', zero_state, read_block, precision=PRECISE)
    log_last = log_total[-1]
    shrink = jnp.exp(log_last[None, :] - log_total)
    new_state = jnp.exp(log_last)[:, None, None] * zero_state + jnp.einsum('shp,sn->hpn', shrink[:, :, None] * input_block, write_block, precision=PRECISE)
    return (new_state, mixed)

def ssm_map(input_seq, gate_seq, write_seq, read_seq, decay_seq, skip_gain, norm_gain):
    blocks = 2 * N_CTX
    initial = jnp.zeros((STATE_HEADS, P_SIZE, NS), dtype=input_seq.dtype)
    pieces = (input_seq.reshape(blocks, HF, STATE_HEADS, P_SIZE), write_seq.reshape(blocks, HF, NS), read_seq.reshape(blocks, HF, NS), decay_seq.reshape(blocks, HF, STATE_HEADS))
    _, mixed = lax.scan(block_step, initial, pieces)
    mixed = mixed.reshape(TOKEN_COUNT, STATE_HEADS, P_SIZE) + skip_gain[None, :, None] * input_seq.reshape(TOKEN_COUNT, STATE_HEADS, P_SIZE)
    gated = mixed.reshape(TOKEN_COUNT, CH) * jax.nn.silu(gate_seq)
    root_mean = jnp.sqrt(lax.optimization_barrier(jnp.mean(gated * gated, axis=1, keepdims=True)) + EPSILON)
    return gated / root_mean * norm_gain

def head_terms(pieces, causal, score_scale):
    query_head, key_head, value_head, cot_head = pieces
    scores = jnp.dot(query_head, key_head.T, preferred_element_type=jnp.float32) * score_scale
    scores = jnp.where(causal, scores, NEGATIVE)
    row_max = lax.optimization_barrier(jnp.max(scores, axis=1, keepdims=True))
    log_norm = row_max + jnp.log(lax.optimization_barrier(jnp.sum(jnp.exp(scores - row_max), axis=1, keepdims=True)))
    probs_full = jnp.exp(scores - log_norm)
    weights = probs_full.astype(jnp.bfloat16)
    output = jnp.dot(weights, value_head, preferred_element_type=jnp.float32).astype(jnp.bfloat16)
    delta_row = lax.optimization_barrier(jnp.sum(cot_head.astype(jnp.float32) * output.astype(jnp.float32), axis=1, keepdims=True))
    d_prob = jnp.dot(cot_head, value_head.T, preferred_element_type=jnp.float32)
    d_score = (probs_full * (d_prob - delta_row) * score_scale).astype(jnp.bfloat16)
    query_g = jnp.dot(d_score, key_head, preferred_element_type=jnp.float32).astype(jnp.bfloat16)
    key_g = jnp.dot(d_score.T, query_head, preferred_element_type=jnp.float32)
    value_g = jnp.dot(weights.T, cot_head, preferred_element_type=jnp.float32)
    return (output, query_g, key_g, value_g)

def reference(ssm_input, ssm_gate, state_write, state_read, log_decay, skip_gain, norm_gain, ssm_cotangent, queries, key_states, value_states, attn_cotangent):
    to_seq = sequence_rows()
    to_fold = folded_rows()

    def ordered(values):
        return jnp.take(values, to_seq, axis=0)

    def folded(values):
        return jnp.take(values, to_fold, axis=0)
    decay_seq = ordered(log_decay).astype(jnp.float32)

    def ssm_local(input_seq, gate_seq, write_seq, read_seq):
        return ssm_map(input_seq, gate_seq, write_seq, read_seq, decay_seq, skip_gain, norm_gain)
    primal = (ordered(ssm_input).astype(jnp.float32), ordered(ssm_gate).astype(jnp.float32), ordered(state_write).astype(jnp.float32), ordered(state_read).astype(jnp.float32))
    ssm_seq, pullback = jax.vjp(ssm_local, *primal)
    input_g, gate_g, write_g, read_g = pullback(ordered(ssm_cotangent).astype(jnp.float32))
    ssm_output = folded(ssm_seq).astype(jnp.bfloat16)
    input_grad = folded(input_g).astype(jnp.bfloat16)
    gate_grad = folded(gate_g).astype(jnp.bfloat16)
    write_grad = folded(write_g).astype(jnp.float32)
    read_grad = folded(read_g).astype(jnp.float32)
    group_size = QH // KVH
    query_heads = jnp.transpose(ordered(queries).reshape(TOKEN_COUNT, QH, HD), (1, 0, 2))
    cot_heads = jnp.transpose(ordered(attn_cotangent).reshape(TOKEN_COUNT, QH, HD), (1, 0, 2))
    key_heads = jnp.repeat(jnp.transpose(ordered(key_states).reshape(TOKEN_COUNT, KVH, HD), (1, 0, 2)), group_size, axis=0)
    value_heads = jnp.repeat(jnp.transpose(ordered(value_states).reshape(TOKEN_COUNT, KVH, HD), (1, 0, 2)), group_size, axis=0)
    causal = jnp.arange(TOKEN_COUNT)[:, None] >= jnp.arange(TOKEN_COUNT)[None, :]
    outputs, query_g, key_g, value_g = lax.map(partial(head_terms, causal=causal, score_scale=HD ** (-0.5)), (query_heads, key_heads, value_heads, cot_heads))
    attn_output = folded(jnp.transpose(outputs, (1, 0, 2)).reshape(TOKEN_COUNT, QH * HD))
    query_grad = folded(jnp.transpose(query_g, (1, 0, 2)).reshape(TOKEN_COUNT, QH * HD))
    key_sum = lax.optimization_barrier(jnp.sum(key_g.reshape(KVH, group_size, TOKEN_COUNT, HD), axis=1))
    value_sum = lax.optimization_barrier(jnp.sum(value_g.reshape(KVH, group_size, TOKEN_COUNT, HD), axis=1))
    key_grad = folded(jnp.transpose(key_sum, (1, 0, 2)).reshape(TOKEN_COUNT, KVH * HD)).astype(jnp.bfloat16)
    value_grad = folded(jnp.transpose(value_sum, (1, 0, 2)).reshape(TOKEN_COUNT, KVH * HD)).astype(jnp.bfloat16)
    return (ssm_output, input_grad, gate_grad, write_grad, read_grad, attn_output, query_grad, key_grad, value_grad)
```

```python
import functools

import jax
import jax.numpy as jnp
from jax import lax
from jax.experimental import pallas as pl
from jax.experimental.pallas import tpu as pltpu
from jax.sharding import PartitionSpec as P

HD = 128
CH = 8192
PRECISE = lax.Precision.HIGHEST
NEGATIVE = -1e30
EPSILON = 1e-05
TILE_KEYS = 256
CHUNK = 256
VMEM_BYTES = 48 * 1024 * 1024


def dot(a, b, a_dim, b_dim):
    return lax.dot_general(
        a, b, (((a_dim,), (b_dim,)), ((), ())), preferred_element_type=jnp.float32
    )


def attention_kernel(
    place_ref, q_ref, kv_ref, cot_ref, out_ref, dq_ref, dkv_ref,
    keys, values, dk_sum, dv_sum, scores, q_rows, cot_rows, acc,
):
    count, _, _, half_rows, _ = kv_ref.shape
    group = q_ref.shape[1] // HD
    rows = group * half_rows
    scale = HD ** (-0.5)
    place = place_ref[0]
    for j in range(count):
        near = pl.ds(j * half_rows, half_rows)
        far = pl.ds((2 * count - 1 - j) * half_rows, half_rows)
        keys[near] = kv_ref[j, 0, 0]
        keys[far] = kv_ref[j, 0, 1]
        values[near] = kv_ref[j, 1, 0]
        values[far] = kv_ref[j, 1, 1]
    dk_sum[...] = jnp.zeros_like(dk_sum)
    dv_sum[...] = jnp.zeros_like(dv_sum)
    for half in range(2):
        block = place if half == 0 else 2 * count - 1 - place
        tiles = block // (TILE_KEYS // half_rows) + 1
        for h in range(group):
            there = (pl.ds(half * half_rows, half_rows), pl.ds(h * HD, HD))
            q_rows[pl.ds(h * half_rows, half_rows)] = q_ref[there]
            cot_rows[pl.ds(h * half_rows, half_rows)] = cot_ref[there]
        q_pos = block * half_rows + lax.broadcasted_iota(jnp.int32, (1, rows), 1) % half_rows

        def score_turn(tile, top):
            at = pl.ds(pl.multiple_of(tile * TILE_KEYS, TILE_KEYS), TILE_KEYS)
            s = dot(keys[at], q_rows[...], 1, 1) * scale
            key_pos = tile * TILE_KEYS + lax.broadcasted_iota(jnp.int32, s.shape, 0)
            s = jnp.where(key_pos <= q_pos, s, NEGATIVE)
            scores[at] = s
            return jnp.maximum(top, jnp.max(s, axis=0, keepdims=True))

        top = lax.fori_loop(0, tiles, score_turn, jnp.full((1, rows), NEGATIVE, jnp.float32))
        acc[...] = jnp.zeros_like(acc)

        def value_turn(tile, total):
            at = pl.ds(pl.multiple_of(tile * TILE_KEYS, TILE_KEYS), TILE_KEYS)
            p = jnp.exp(scores[at] - top)
            scores[at] = p
            acc[...] += dot(values[at], p.astype(jnp.bfloat16), 0, 0)
            return total + jnp.sum(p, axis=0, keepdims=True)

        total = lax.fori_loop(0, tiles, value_turn, jnp.zeros((1, rows), jnp.float32))
        inverse = 1.0 / total
        out_t = acc[...] * inverse
        out_rows = out_t.T.astype(jnp.bfloat16)
        cot_t = cot_rows[...].astype(jnp.float32).T
        delta = jnp.sum(
            cot_t * out_t.astype(jnp.bfloat16).astype(jnp.float32), axis=0, keepdims=True
        )
        acc[...] = jnp.zeros_like(acc)

        def grad_turn(tile, carry):
            at = pl.ds(pl.multiple_of(tile * TILE_KEYS, TILE_KEYS), TILE_KEYS)
            w = scores[at] * inverse
            d_prob = dot(values[at], cot_rows[...], 1, 1)
            d_score = (w * (d_prob - delta) * scale).astype(jnp.bfloat16)
            acc[...] += dot(keys[at], d_score, 0, 0)
            dk_sum[at] += dot(d_score, q_rows[...], 1, 0)
            dv_sum[at] += dot(w.astype(jnp.bfloat16), cot_rows[...], 1, 0)
            return carry

        lax.fori_loop(0, tiles, grad_turn, 0)
        dq_rows = acc[...].T.astype(jnp.bfloat16)
        for h in range(group):
            there = (pl.ds(half * half_rows, half_rows), pl.ds(h * HD, HD))
            out_ref[there] = out_rows[h * half_rows : (h + 1) * half_rows]
            dq_ref[there] = dq_rows[h * half_rows : (h + 1) * half_rows]
    for j in range(count):
        near = pl.ds(j * half_rows, half_rows)
        far = pl.ds((2 * count - 1 - j) * half_rows, half_rows)
        dkv_ref[j, 0, 0] = dk_sum[near].astype(jnp.bfloat16)
        dkv_ref[j, 0, 1] = dk_sum[far].astype(jnp.bfloat16)
        dkv_ref[j, 1, 0] = dv_sum[near].astype(jnp.bfloat16)
        dkv_ref[j, 1, 1] = dv_sum[far].astype(jnp.bfloat16)


def attention_core(queries, kv_all, attn_cotangent, place):
    tok_rows, q_cols = queries.shape
    count, _, _, half_rows, kv_cols = kv_all.shape
    kv_heads = kv_cols // HD
    width = q_cols // kv_heads
    rows = width // HD * half_rows
    total = count * tok_rows
    wide = pl.BlockSpec((tok_rows, width), lambda g, place: (0, g))
    pair = pl.BlockSpec((count, 2, 2, half_rows, HD), lambda g, place: (0, 0, 0, 0, g))
    like_q = jax.ShapeDtypeStruct(queries.shape, jnp.bfloat16)
    flops = 7 * 2 * tok_rows * q_cols * total // 2
    return pl.pallas_call(
        attention_kernel,
        out_shape=(like_q, like_q, jax.ShapeDtypeStruct(kv_all.shape, jnp.bfloat16)),
        grid_spec=pltpu.PrefetchScalarGridSpec(
            num_scalar_prefetch=1,
            grid=(kv_heads,),
            in_specs=[wide, pair, wide],
            out_specs=(wide, wide, pair),
            scratch_shapes=[
                pltpu.VMEM((total, HD), jnp.bfloat16),
                pltpu.VMEM((total, HD), jnp.bfloat16),
                pltpu.VMEM((total, HD), jnp.float32),
                pltpu.VMEM((total, HD), jnp.float32),
                pltpu.VMEM((total, rows), jnp.float32),
                pltpu.VMEM((rows, HD), jnp.bfloat16),
                pltpu.VMEM((rows, HD), jnp.bfloat16),
                pltpu.VMEM((HD, rows), jnp.float32),
            ],
        ),
        compiler_params=pltpu.CompilerParams(vmem_limit_bytes=VMEM_BYTES),
        cost_estimate=pl.CostEstimate(
            flops=3 * flops, bytes_accessed=16 * 1024 * 1024, transcendentals=total * q_cols // 2
        ),
        name="attention_both",
    )(place.reshape(1).astype(jnp.int32), queries, kv_all, attn_cotangent)


def gather_pair(kv):
    _, tok_rows, kv_cols = kv.shape
    return lax.all_gather(kv, "ctx", axis=0).reshape(
        lax.axis_size("ctx"), 2, 2, tok_rows // 2, kv_cols
    )


def scatter_pair(dkv):
    count, _, _, half_rows, kv_cols = dkv.shape
    mine = lax.psum_scatter(
        dkv.reshape(count, 2, 2 * half_rows, kv_cols), "ctx", scatter_dimension=0, tiled=False
    )
    return (mine[0], mine[1])


def in_order(ref, step, steps):
    pieces = ref.shape[0]
    early = step < steps // 2
    return [ref[jnp.where(early, j, pieces - 1 - j)] for j in range(pieces)]


def put_in_order(ref, value, step, steps):
    pieces, rows = ref.shape[0], ref.shape[1]
    early = step < steps // 2
    for j in range(pieces):
        ref[jnp.where(early, j, pieces - 1 - j)] = value[j * rows : (j + 1) * rows].astype(
            ref.dtype
        )


def whole(ref, step, steps):
    return jnp.concatenate(in_order(ref, step, steps), axis=0)


def causal_decay(col, row, flip):
    shape = (col.shape[0], row.shape[1])
    down = lax.broadcasted_iota(jnp.int32, shape, 0)
    across = lax.broadcasted_iota(jnp.int32, shape, 1)
    if flip:
        return jnp.exp(jnp.where(across >= down, row - col, NEGATIVE))
    return jnp.exp(jnp.where(down >= across, col - row, NEGATIVE))


def forward_kernel(steps, x_ref, b_ref, c_ref, col_ref, row_ref, mixed_ref, state_ref, state):
    step = pl.program_id(0)

    @pl.when(step == 0)
    def _():
        state[...] = jnp.zeros_like(state)

    x = whole(x_ref, step, steps)
    b = whole(b_ref, step, steps)
    c = whole(c_ref, step, steps)
    col, row = col_ref[...], row_ref[0]
    last = col[CHUNK - 1 : CHUNK]
    weights = (causal_decay(col, row, False) * dot(c, b, 1, 1)).astype(jnp.bfloat16)
    entering = state[...]
    entering_short = entering.astype(jnp.bfloat16)
    state_ref[0] = entering_short
    mixed = dot(weights, x, 1, 0) + jnp.exp(col) * dot(c, entering_short, 1, 0)
    put_in_order(mixed_ref, mixed, step, steps)
    shrunk = (b.astype(jnp.float32) * jnp.exp(last - col)).astype(jnp.bfloat16)
    state[...] = jnp.exp(last) * entering + dot(shrunk, x, 0, 0)


def backward_kernel(
    steps, x_ref, dm_ref, b_ref, c_ref, col_ref, row_ref, state_ref,
    input_ref, write_ref, read_ref, adjoint,
):
    step = steps - 1 - pl.program_id(0)

    @pl.when(pl.program_id(0) == 0)
    def _():
        adjoint[...] = jnp.zeros_like(adjoint)

    x = whole(x_ref, step, steps)
    dm = whole(dm_ref, step, steps)
    b = whole(b_ref, step, steps)
    c = whole(c_ref, step, steps)
    col, row = col_ref[...], row_ref[0]
    last = col[CHUNK - 1 : CHUNK]
    shrink, grow = jnp.exp(last - col), jnp.exp(col)
    entering = adjoint[...]
    entering_short = entering.astype(jnp.bfloat16)
    decay_t = causal_decay(col, row, True)
    weights_t = (decay_t * dot(b, c, 1, 1)).astype(jnp.bfloat16)
    input_g = dot(weights_t, dm, 1, 0) + shrink * dot(b, entering_short, 1, 0)
    put_in_order(input_ref, input_g, step, steps)
    pairs_t = (decay_t * dot(x, dm, 1, 1)).astype(jnp.bfloat16)
    write_g = dot(pairs_t, c, 1, 0) + shrink * dot(x, entering_short, 1, 1)
    pairs = (causal_decay(col, row, False) * dot(dm, x, 1, 1)).astype(jnp.bfloat16)
    read_g = dot(pairs, b, 1, 0) + grow * dot(dm, state_ref[0], 1, 1)
    put_in_order(write_ref, write_g, step, steps)
    put_in_order(read_ref, read_g, step, steps)
    grown = (c.astype(jnp.float32) * grow).astype(jnp.bfloat16)
    adjoint[...] = jnp.exp(last) * entering + dot(grown, dm, 0, 0)


def ssm_specs(count, half_rows, steps, order):
    per = CHUNK // half_rows

    def rows_spec(cols):
        def place(i):
            step = order(i)
            early = step < steps // 2
            return (
                jnp.where(early, step, steps - 1 - step), jnp.where(early, 0, 1), 0, 0
            )

        return pl.BlockSpec((per, pl.Squeezed(), half_rows, cols), place)

    return (
        rows_spec,
        pl.BlockSpec((CHUNK, 1), lambda i: (order(i), 0)),
        pl.BlockSpec((1, 1, CHUNK), lambda i: (order(i), 0, 0)),
    )


def scan_forward(x, b, c, col, row):
    count, _, half_rows, cols = x.shape
    states = b.shape[-1]
    steps = count * 2 * half_rows // CHUNK
    rows_spec, col_spec, row_spec = ssm_specs(count, half_rows, steps, lambda i: i)
    return pl.pallas_call(
        functools.partial(forward_kernel, steps),
        grid=(steps,),
        in_specs=[rows_spec(cols), rows_spec(states), rows_spec(states), col_spec, row_spec],
        out_specs=(rows_spec(cols), pl.BlockSpec((1, states, cols), lambda i: (i, 0, 0))),
        out_shape=(
            jax.ShapeDtypeStruct(x.shape, jnp.bfloat16),
            jax.ShapeDtypeStruct((steps, states, cols), jnp.bfloat16),
        ),
        scratch_shapes=[pltpu.VMEM((states, cols), jnp.float32)],
        compiler_params=pltpu.CompilerParams(vmem_limit_bytes=VMEM_BYTES),
        cost_estimate=pl.CostEstimate(
            flops=10**9, bytes_accessed=6 * 1024 * 1024, transcendentals=5 * 10**5
        ),
        name="scan_forward",
    )(x, b, c, col, row)


def scan_backward(x, dm, b, c, col, row, state):
    count, _, half_rows, cols = x.shape
    states = b.shape[-1]
    steps = count * 2 * half_rows // CHUNK
    rows_spec, col_spec, row_spec = ssm_specs(
        count, half_rows, steps, lambda i: steps - 1 - i
    )
    return pl.pallas_call(
        functools.partial(backward_kernel, steps),
        grid=(steps,),
        in_specs=[
            rows_spec(cols), rows_spec(cols), rows_spec(states), rows_spec(states),
            col_spec, row_spec,
            pl.BlockSpec((1, states, cols), lambda i: (steps - 1 - i, 0, 0)),
        ],
        out_specs=(rows_spec(cols), rows_spec(states), rows_spec(states)),
        out_shape=(
            jax.ShapeDtypeStruct(x.shape, jnp.bfloat16),
            jax.ShapeDtypeStruct(b.shape, jnp.bfloat16),
            jax.ShapeDtypeStruct(b.shape, jnp.bfloat16),
        ),
        scratch_shapes=[pltpu.VMEM((states, cols), jnp.float32)],
        compiler_params=pltpu.CompilerParams(vmem_limit_bytes=VMEM_BYTES),
        cost_estimate=pl.CostEstimate(
            flops=2 * 10**9, bytes_accessed=6 * 1024 * 1024, transcendentals=10**6
        ),
        name="scan_backward",
    )(x, dm, b, c, col, row, state)


def to_channels(values, extra=None):
    count = lax.axis_size("ctx")
    parts = values.reshape(values.shape[0], count, -1)
    if extra is not None:
        shape = (values.shape[0], count, extra.shape[1])
        parts = jnp.concatenate([parts, jnp.broadcast_to(extra[:, None, :], shape)], axis=2)
    blocks = jnp.transpose(parts, (1, 0, 2))
    return lax.all_to_all(blocks, "ctx", split_axis=0, concat_axis=0)


def to_owners(blocks):
    return lax.all_to_all(blocks, "ctx", split_axis=0, concat_axis=0)


def side_by_side(blocks):
    return jnp.transpose(blocks, (1, 0, 2)).reshape(blocks.shape[1], -1)


def from_other_core(values):
    return lax.ppermute(values, "tp", [(0, 1), (1, 0)])


def both_layers(
    ssm_input, ssm_gate, state_write, state_read, log_decay, skip_gain, norm_gain, ssm_cotangent,
    queries, key_states, value_states, attn_cotangent,
):
    tok_rows, channel_count = ssm_input.shape
    head_count = log_decay.shape[1]
    half_rows = tok_rows // 2
    head_dim = channel_count // head_count
    count = lax.axis_size("ctx")
    own_cols = channel_count // count
    states = state_write.shape[1]
    folded = (count, 2, half_rows)
    share_maps = lax.axis_size("tp") == 2
    kv = jnp.stack([key_states, value_states])
    kv, sent_input, log_decay = lax.optimization_barrier((kv, ssm_input, log_decay))
    kv_all = gather_pair(kv)
    if share_maps:
        first = lax.axis_index("tp") == 0
        arrived = to_channels(sent_input, jnp.where(first, state_write, state_read))
        own_map = arrived[:, :, own_cols:]
        other_map = from_other_core(own_map)
        b_all = jnp.where(first, own_map, other_map).reshape(*folded, states)
        c_all = jnp.where(first, other_map, own_map).reshape(*folded, states)
    else:
        arrived = to_channels(sent_input, jnp.concatenate([state_write, state_read], axis=1))
        b_all = arrived[:, :, own_cols : own_cols + states].reshape(*folded, states)
        c_all = arrived[:, :, own_cols + states :].reshape(*folded, states)
    x_all = arrived[:, :, :own_cols].reshape(*folded, own_cols)
    decay_rows = jnp.repeat(log_decay.T, head_dim // own_cols, axis=0)
    own_decay = to_owners(decay_rows[:, None, :]).reshape(*folded)
    ordered = jnp.concatenate([own_decay[:, 0], own_decay[::-1, 1]]).reshape(-1, CHUNK)
    upto = jnp.triu(jnp.ones((CHUNK, CHUNK), jnp.float32))
    log_total = jnp.dot(ordered, upto, precision=PRECISE)
    col = log_total.reshape(-1, 1)
    row = log_total[:, None, :]
    mixed_all, state_all = scan_forward(x_all, b_all, c_all, col, row)
    mixed_all, kv_all = lax.optimization_barrier((mixed_all, kv_all))
    attn_output, query_grad, dkv = attention_core(
        queries, kv_all, attn_cotangent, lax.axis_index("ctx")
    )
    mixed_back = to_owners(mixed_all.reshape(count, tok_rows, own_cols))
    dkv, mixed_back = lax.optimization_barrier((dkv, mixed_back))
    key_grad, value_grad = scatter_pair(dkv)
    skip = jnp.repeat(skip_gain, head_dim)[None, :]
    mixed = side_by_side(mixed_back)
    mixed = mixed.astype(jnp.float32) + skip * ssm_input.astype(jnp.float32)
    gate = ssm_gate.astype(jnp.float32)
    sigmoid = jax.nn.sigmoid(gate)
    gated = mixed * gate * sigmoid
    d_normed = ssm_cotangent.astype(jnp.float32) * norm_gain
    sums = lax.psum(
        jnp.stack([jnp.sum(gated * gated, axis=1), jnp.sum(d_normed * gated, axis=1)]), "tp"
    )
    root_mean = jnp.sqrt(sums[0] / CH + EPSILON)[:, None]
    inner_mean = (sums[1] / CH)[:, None] / root_mean
    normed = gated / root_mean
    ssm_output = (normed * norm_gain).astype(jnp.bfloat16)
    d_gated = (d_normed - normed * inner_mean) / root_mean
    d_mixed = d_gated * gate * sigmoid
    gate_grad = (d_gated * mixed * sigmoid * (1.0 + gate * (1.0 - sigmoid))).astype(jnp.bfloat16)
    dm_all = to_channels(d_mixed.astype(jnp.bfloat16)).reshape(*folded, own_cols)
    input_all, write_all, read_all = scan_backward(
        x_all, dm_all, b_all, c_all, col, row, state_all
    )
    blocks = (count, tok_rows)
    input_all = input_all.reshape(*blocks, own_cols)
    write_all, read_all = write_all.reshape(*blocks, states), read_all.reshape(*blocks, states)
    if share_maps:
        kept = jnp.where(first, write_all, read_all)
        passed = from_other_core(jnp.where(first, read_all, write_all))
        maps_all = (kept.astype(jnp.float32) + passed.astype(jnp.float32)).astype(jnp.bfloat16)
    else:
        maps_all = jnp.concatenate([write_all, read_all], axis=2)
    back = to_owners(jnp.concatenate([input_all, maps_all], axis=2))
    input_g = side_by_side(back[:, :, :own_cols]).astype(jnp.float32)
    input_grad = (input_g + skip * d_mixed).astype(jnp.bfloat16)
    maps = jnp.sum(back[:, :, own_cols:].astype(jnp.float32), axis=0)
    if share_maps:
        other = from_other_core(maps)
        write_grad, read_grad = jnp.where(first, maps, other), jnp.where(first, other, maps)
    else:
        maps = lax.psum(maps.astype(jnp.bfloat16), "tp").astype(jnp.float32)
        write_grad, read_grad = maps[:, :states], maps[:, states:]
    return (
        ssm_output, input_grad, gate_grad, write_grad, read_grad,
        attn_output, query_grad, key_grad, value_grad,
    )


MESH = pl.DeviceIdType.MESH


def remote(src, dst, send, recv, **to):
    return pltpu.make_async_remote_copy(
        src_ref=src, dst_ref=dst, send_sem=send, recv_sem=recv,
        device_id=to, device_id_type=MESH,
    )


def ring(at, step, size):
    return lax.rem(at + step, size)


def spot():
    me = lax.axis_index("ctx")
    return me, lax.div(me, 4), lax.rem(lax.div(me, 2), 2), lax.rem(me, 2)


def greet(count, me, core=None):
    barrier = pltpu.get_barrier_semaphore()
    for k in range(1, count):
        pl.semaphore_signal(
            barrier, inc=1, device_id={"ctx": ring(me, k, count)}, device_id_type=MESH
        )
    if core is not None:
        pl.semaphore_signal(barrier, inc=1, device_id={"tp": 1 - core}, device_id_type=MESH)
    pl.semaphore_wait(barrier, count - 1 if core is None else count)


def columns(p, width):
    return pl.ds(pl.multiple_of(p * width, width), width)


def spread(count, me, pick, place, send, recv):
    local = pltpu.make_async_copy(pick(me), place(me), send.at[0])
    local.start()
    copies = []
    for k in range(1, count):
        p = ring(me, k, count)
        copy = remote(pick(p), place(me), send.at[k], recv.at[k], ctx=p)
        copy.start()
        copies.append(copy)
    return local, copies


def settle(pieces):
    local, copies = pieces
    for copy in copies:
        copy.wait_recv()
    for copy in copies:
        copy.wait_send()
    local.wait()


def index_of(z, y, x):
    return z * 4 + y * 2 + x


def gather_turns(own, dest, where, send, recv, local):
    _, z, y, x = where
    depth = dest.shape[0]
    used = []

    def post(src, dst, to):
        copy = remote(src, dst, send.at[len(used)], recv.at[len(used)], ctx=to)
        copy.start()
        used.append(copy)
        return copy

    mine = [pltpu.make_async_copy(own.at[c], dest.at[z, y, x, c], local.at[c]) for c in range(2)]
    for copy in mine:
        copy.start()
    over_x, over_y = index_of(z, y, 1 - x), index_of(z, 1 - y, x)
    first = [
        post(own.at[0], dest.at[z, y, x, 0], over_x),
        post(own.at[1], dest.at[z, y, x, 1], over_y),
    ]
    along = {}
    for k in range(1, depth):
        to = index_of(ring(z, k, depth), y, x)
        along[k] = [post(own.at[c], dest.at[z, y, x, c], to) for c in range(2)]
    yield
    for copy in mine:
        copy.wait()

    def pair(at, arrived):
        arrived[0].wait_recv()
        keys = dest.at[at, y, :, 0]
        a = post(keys, keys, over_y)
        arrived[1].wait_recv()
        values = dest.at[at, :, x, 1]
        return a, post(values, values, over_x)

    ends = list(pair(z, first))
    yield
    onward = {}
    for k in range(1, depth):
        at = ring(z, depth - k, depth)
        for copy in along[k]:
            copy.wait_recv()
        onward[k] = [
            post(dest.at[at, y, x, 0], dest.at[at, y, x, 0], over_x),
            post(dest.at[at, y, x, 1], dest.at[at, y, x, 1], over_y),
        ]
        yield
    for k in range(1, depth):
        ends += pair(ring(z, depth - k, depth), onward[k])
        yield
    for copy in ends:
        copy.wait_recv()
    for copy in used:
        copy.wait_send()


def gather_copies(depth):
    return 2 + 2 * (depth - 1) * 3 + 2


def scatter_turns(terms, out, half_way, next_way, last_way, where, send, recv):
    _, z, y, x = where
    depth = terms.shape[0]
    used = []

    def post(src, dst, to):
        copy = remote(src, dst, send.at[len(used)], recv.at[len(used)], ctx=to)
        copy.start()
        used.append(copy)
        return copy

    def wide(value):
        return value.astype(jnp.float32)

    over_x, over_y = index_of(z, y, 1 - x), index_of(z, 1 - y, x)
    order = list(range(1, depth)) + [0]
    first, second, third = {}, {}, []
    for k in order:
        at = ring(z, k, depth)
        first[k] = (
            post(terms.at[at, 1 - y, :, 0], half_way.at[0, at], over_y),
            post(terms.at[at, :, 1 - x, 1], half_way.at[1, at], over_x),
        )
    yield
    for k in order:
        at = ring(z, k, depth)
        first[k][0].wait_recv()
        half_way[0, at, 1 - x] = (
            wide(half_way[0, at, 1 - x]) + wide(terms[at, y, 1 - x, 0])
        ).astype(jnp.bfloat16)
        a = post(half_way.at[0, at, 1 - x], next_way.at[0, at], over_x)
        first[k][1].wait_recv()
        half_way[1, at, 1 - y] = (
            wide(half_way[1, at, 1 - y]) + wide(terms[at, 1 - y, x, 1])
        ).astype(jnp.bfloat16)
        second[k] = (a, post(half_way.at[1, at, 1 - y], next_way.at[1, at], over_y))
        yield
    for k in order:
        at = ring(z, k, depth)
        for c in range(2):
            second[k][c].wait_recv()
            total = (
                wide(next_way[c, at]) + wide(half_way[c, at, y if c else x])
                + wide(terms[at, y, x, c])
            )
            next_way[c, at] = total.astype(jnp.bfloat16)
            if k:
                third.append(
                    post(next_way.at[c, at], last_way.at[c, k - 1], index_of(at, y, x))
                )
        yield
    for copy in third:
        copy.wait_recv()
    for c in range(2):
        total = wide(next_way[c, z])
        for k in range(1, depth):
            total = total + wide(last_way[c, k - 1])
        out[c] = total.astype(jnp.bfloat16)
    for copy in used:
        copy.wait_send()


def scatter_copies(depth):
    return 4 * depth + 2 * (depth - 1)


def running_decay(decay, rows, half_rows):
    per = CHUNK // half_rows
    groups = decay.shape[0] // per
    width = 2 * half_rows
    side = jnp.concatenate(
        [decay[pl.ds(j, groups, stride=per)] for j in range(per)], axis=1
    )
    shape = (per * width, 2 * CHUNK)
    r = lax.broadcasted_iota(jnp.int32, shape, 0)
    u = lax.broadcasted_iota(jnp.int32, shape, 1)
    j, t = r // width, r % width
    near = (t < half_rows) & (u < CHUNK) & (j * half_rows + t <= u)
    far = (t >= half_rows) & (u >= CHUNK)
    far = far & ((per - 1 - j) * half_rows + t - half_rows <= u - CHUNK)
    ones = jnp.where(near | far, 1.0, 0.0)
    sums = lax.dot_general(
        side, ones, (((1,), (0,)), ((), ())), precision=PRECISE,
        preferred_element_type=jnp.float32,
    )
    rows[0:groups] = sums[:, :CHUNK]
    rows[groups : 2 * groups] = sums[:, CHUNK:]


def members(group, half, per):
    return [per * group + (j if half == 0 else per - 1 - j) for j in range(per)]


def chunk_of(ref, ids, half, half_rows):
    return jnp.concatenate(
        [ref[d, half * half_rows : (half + 1) * half_rows] for d in ids], axis=0
    )


def put_chunk(ref, ids, half, half_rows, value):
    value = value.astype(ref.dtype)
    for j, d in enumerate(ids):
        ref[d, half * half_rows : (half + 1) * half_rows] = value[
            j * half_rows : (j + 1) * half_rows
        ]


def as_column(row):
    shape = (row.shape[1], row.shape[1])
    same = lax.broadcasted_iota(jnp.int32, shape, 0) == lax.broadcasted_iota(jnp.int32, shape, 1)
    return jnp.sum(jnp.where(same, row, 0.0), axis=1, keepdims=True)


def first_kernel(
    x_ref, map_ref, decay_ref, kv_ref,
    x_all, maps, rows, states, mixed_back, kv_all,
    decay, mixed, state,
    x_send, x_recv, d_send, d_recv, m_send, m_recv, kv_send, kv_recv, kv_local, b_send, b_recv,
):
    where = spot()
    me, z, y, x = where
    core = lax.axis_index("tp")
    count, tok_rows, own_cols = x_all.shape
    half_rows = tok_rows // 2
    depth = count // 4
    greet(count, me, core)
    decays = spread(
        count, me, lambda p: decay_ref.at[pl.ds(p, 1)], lambda p: decay.at[pl.ds(p, 1)],
        d_send, d_recv,
    )
    own_map = pltpu.make_async_copy(map_ref, maps.at[core, z, y, x], m_send.at[0])
    own_map.start()
    used = []

    def post(src, dst, **to):
        copy = remote(src, dst, m_send.at[len(used) + 1], m_recv.at[len(used) + 1], **to)
        copy.start()
        used.append(copy)
        return copy

    for k in range(1, depth):
        post(map_ref, maps.at[core, z, y, x], ctx=index_of(ring(z, k, depth), y, x))
    inputs = spread(
        count, me, lambda p: x_ref.at[:, columns(p, own_cols)], lambda p: x_all.at[p],
        x_send, x_recv,
    )
    turns = gather_turns(kv_ref, kv_all, where, kv_send, kv_recv, kv_local)
    next(turns)
    for copy in used:
        copy.wait_recv()
    own_map.wait()
    part = maps.at[core, :, y, x]
    post(part, part, ctx=index_of(z, y, 1 - x)).wait_recv()
    part = maps.at[core, :, y]
    post(part, part, ctx=index_of(z, 1 - y, x)).wait_recv()
    part = maps.at[core]
    over = post(part, part, tp=1 - core)
    next(turns)
    settle(decays)
    running_decay(decay, rows, half_rows)
    over.wait_recv()
    for copy in used:
        copy.wait_send()
    settle(inputs)
    per = CHUNK // half_rows
    groups = count // per
    state[...] = jnp.zeros_like(state)

    def turn(group, half):
        ids = members(group, half, per)
        step = group if half == 0 else 2 * groups - 1 - group
        value = chunk_of(x_all, ids, half, half_rows)
        b, c = [
            jnp.concatenate(
                [
                    maps[which, lax.div(d, 4), lax.rem(lax.div(d, 2), 2), lax.rem(d, 2),
                         half * half_rows : (half + 1) * half_rows]
                    for d in ids
                ],
                axis=0,
            )
            for which in range(2)
        ]
        row = rows[pl.ds(half * groups + group, 1)]
        col = as_column(row)
        last = col[CHUNK - 1 : CHUNK]
        weights = (causal_decay(col, row, False) * dot(c, b, 1, 1)).astype(jnp.bfloat16)
        entering = state[...]
        entering_short = entering.astype(jnp.bfloat16)
        states[step] = entering_short
        result = dot(weights, value, 1, 0) + jnp.exp(col) * dot(c, entering_short, 1, 0)
        put_chunk(mixed, ids, half, half_rows, result)
        shrunk = (b.astype(jnp.float32) * jnp.exp(last - col)).astype(jnp.bfloat16)
        state[...] = jnp.exp(last) * entering + dot(shrunk, value, 0, 0)

    @pl.loop(0, groups)
    def _(group):
        turn(group, 0)

    next(turns)

    @pl.loop(0, groups)
    def _(group):
        turn(groups - 1 - group, 1)

    back = spread(
        count, me, lambda p: mixed.at[p], lambda p: mixed_back.at[:, columns(p, own_cols)],
        b_send, b_recv,
    )
    for _ in turns:
        pass
    settle(back)


def first_stage(x, own_map, decay_rows, kv):
    count = lax.axis_size("ctx")
    tok_rows, channels = x.shape
    own_cols = channels // count
    states = own_map.shape[1]
    depth = count // 4
    steps = count * tok_rows // CHUNK
    short = jnp.bfloat16
    hbm = pl.BlockSpec(memory_space=pl.ANY)
    vmem = pl.BlockSpec(memory_space=pltpu.VMEM)
    dma = pltpu.SemaphoreType.DMA
    kv_count = gather_copies(depth)
    return pl.pallas_call(
        first_kernel,
        in_specs=[hbm, vmem, vmem, hbm],
        out_specs=(vmem, vmem, vmem, vmem, hbm, hbm),
        out_shape=(
            jax.ShapeDtypeStruct((count, tok_rows, own_cols), short),
            jax.ShapeDtypeStruct((2, depth, 2, 2, tok_rows, states), short),
            jax.ShapeDtypeStruct((steps, CHUNK), jnp.float32),
            jax.ShapeDtypeStruct((steps, states, own_cols), short),
            jax.ShapeDtypeStruct(x.shape, short),
            jax.ShapeDtypeStruct((depth, 2, 2) + kv.shape, short),
        ),
        scratch_shapes=[
            pltpu.VMEM((count, tok_rows), jnp.float32),
            pltpu.VMEM((count, tok_rows, own_cols), short),
            pltpu.VMEM((states, own_cols), jnp.float32),
            dma((count,)), dma((count,)), dma((count,)), dma((count,)),
            dma((depth + 3,)), dma((depth + 3,)), dma((kv_count,)), dma((kv_count,)), dma((2,)),
            dma((count,)), dma((count,)),
        ],
        compiler_params=pltpu.CompilerParams(
            collective_id=0, has_side_effects=True, vmem_limit_bytes=VMEM_BYTES
        ),
        cost_estimate=pl.CostEstimate(
            flops=10**9, bytes_accessed=16 * 1024 * 1024, transcendentals=5 * 10**5
        ),
        name="gather_and_scan",
    )(x, own_map, decay_rows, kv)


def attention_with_exchange(
    q_ref, kv_ref, cot_ref, dm_ref, out_ref, dq_ref, dkv_ref, dm_all,
    keys, values, dk_sum, dv_sum, scores, q_rows, cot_rows, acc, send, recv,
):
    me = lax.axis_index("ctx")
    count, _, own_cols = dm_all.shape

    def pieces():
        copies = []
        for k in range(1, count):
            p = ring(me, k, count)
            copies.append(
                remote(
                    dm_ref.at[:, columns(p, own_cols)], dm_all.at[me], send.at[k], recv.at[k],
                    ctx=p,
                )
            )
        own = pltpu.make_async_copy(
            dm_ref.at[:, columns(me, own_cols)], dm_all.at[me], send.at[0]
        )
        return own, copies

    @pl.when(pl.program_id(0) == 0)
    def _():
        greet(count, me)
        own, copies = pieces()
        own.start()
        for copy in copies:
            copy.start()

    attention_kernel(
        (me,), q_ref, kv_ref, cot_ref, out_ref, dq_ref, dkv_ref,
        keys, values, dk_sum, dv_sum, scores, q_rows, cot_rows, acc,
    )

    @pl.when(pl.program_id(0) == pl.num_programs(0) - 1)
    def _():
        settle(pieces())


def second_stage(queries, kv_all, attn_cotangent, d_mixed):
    tok_rows, q_cols = queries.shape
    count, _, _, half_rows, kv_cols = kv_all.shape
    kv_heads = kv_cols // HD
    width = q_cols // kv_heads
    rows = width // HD * half_rows
    total = count * tok_rows
    wide = pl.BlockSpec((tok_rows, width), lambda g: (0, g))
    pair = pl.BlockSpec((count, 2, 2, half_rows, HD), lambda g: (0, 0, 0, 0, g))
    hbm = pl.BlockSpec(memory_space=pl.ANY)
    like_q = jax.ShapeDtypeStruct(queries.shape, jnp.bfloat16)
    flops = 7 * 2 * tok_rows * q_cols * total // 2
    return pl.pallas_call(
        attention_with_exchange,
        out_shape=(
            like_q, like_q, jax.ShapeDtypeStruct(kv_all.shape, jnp.bfloat16),
            jax.ShapeDtypeStruct((count, tok_rows, d_mixed.shape[1] // count), jnp.bfloat16),
        ),
        grid=(kv_heads,),
        in_specs=[wide, pair, wide, hbm],
        out_specs=(wide, wide, pair, hbm),
        scratch_shapes=[
            pltpu.VMEM((total, HD), jnp.bfloat16),
            pltpu.VMEM((total, HD), jnp.bfloat16),
            pltpu.VMEM((total, HD), jnp.float32),
            pltpu.VMEM((total, HD), jnp.float32),
            pltpu.VMEM((total, rows), jnp.float32),
            pltpu.VMEM((rows, HD), jnp.bfloat16),
            pltpu.VMEM((rows, HD), jnp.bfloat16),
            pltpu.VMEM((HD, rows), jnp.float32),
            pltpu.SemaphoreType.DMA((count,)),
            pltpu.SemaphoreType.DMA((count,)),
        ],
        compiler_params=pltpu.CompilerParams(
            collective_id=1, has_side_effects=True, vmem_limit_bytes=VMEM_BYTES
        ),
        cost_estimate=pl.CostEstimate(
            flops=3 * flops, bytes_accessed=16 * 1024 * 1024, transcendentals=total * q_cols // 2
        ),
        name="attention_both",
    )(queries, kv_all, attn_cotangent, d_mixed)


def third_kernel(
    x_all, dm_all, maps, rows, states, terms,
    input_back, kv_out, write_out, read_out,
    inputs, map_terms, map_in, map_back, map_mine, map_theirs, adjoint,
    half_way, next_way, last_way,
    i_send, i_recv, m_send, m_recv, s_send, s_recv, t_send, t_recv,
):
    where = spot()
    me, z, y, x = where
    core = lax.axis_index("tp")
    count, tok_rows, own_cols = x_all.shape
    half_rows = tok_rows // 2
    per = CHUNK // half_rows
    groups = count // per
    greet(count, me, core)
    turns = scatter_turns(
        terms, kv_out, half_way, next_way, last_way, where, s_send, s_recv
    )
    next(turns)
    adjoint[...] = jnp.zeros_like(adjoint)

    def turn(group, half):
        ids = members(group, half, per)
        step = group if half == 0 else 2 * groups - 1 - group
        value = chunk_of(x_all, ids, half, half_rows)
        dm = chunk_of(dm_all, ids, half, half_rows)
        b = chunk_of(maps.at[0], ids, half, half_rows)
        c = chunk_of(maps.at[1], ids, half, half_rows)
        row = rows[pl.ds(half * groups + group, 1)]
        col = as_column(row)
        last = col[CHUNK - 1 : CHUNK]
        shrink, grow = jnp.exp(last - col), jnp.exp(col)
        entering = adjoint[...]
        entering_short = entering.astype(jnp.bfloat16)
        decay_t = causal_decay(col, row, True)
        weights_t = (decay_t * dot(b, c, 1, 1)).astype(jnp.bfloat16)
        input_g = dot(weights_t, dm, 1, 0) + shrink * dot(b, entering_short, 1, 0)
        put_chunk(inputs, ids, half, half_rows, input_g)
        pairs_t = (decay_t * dot(value, dm, 1, 1)).astype(jnp.bfloat16)
        write_g = dot(pairs_t, c, 1, 0) + shrink * dot(value, entering_short, 1, 1)
        pairs = (causal_decay(col, row, False) * dot(dm, value, 1, 1)).astype(jnp.bfloat16)
        read_g = dot(pairs, b, 1, 0) + grow * dot(dm, states[step], 1, 1)
        put_chunk(map_terms.at[0], ids, half, half_rows, write_g)
        put_chunk(map_terms.at[1], ids, half, half_rows, read_g)
        grown = (c.astype(jnp.float32) * grow).astype(jnp.bfloat16)
        adjoint[...] = jnp.exp(last) * entering + dot(grown, dm, 0, 0)

    @pl.loop(0, groups)
    def _(group):
        turn(group, 1)

    @pl.loop(0, groups)
    def _(group):
        turn(groups - 1 - group, 0)

    over = remote(map_terms.at[1 - core], map_in, t_send.at[0], t_recv.at[0], tp=1 - core)
    over.start()
    back = spread(
        count, me, lambda p: inputs.at[p], lambda p: input_back.at[:, columns(p, own_cols)],
        i_send, i_recv,
    )
    next(turns)
    over.wait_recv()

    @pl.loop(0, count)
    def _(d):
        map_in[d] = (
            map_in[d].astype(jnp.float32) + map_terms[core, d].astype(jnp.float32)
        ).astype(jnp.bfloat16)

    map_pieces = spread(
        count, me, lambda p: map_in.at[p], lambda p: map_back.at[p], m_send, m_recv
    )
    for _ in turns:
        pass
    settle(map_pieces)
    total = map_back[0].astype(jnp.float32)
    for d in range(1, count):
        total = total + map_back[d].astype(jnp.float32)
    map_mine[...] = total
    other = remote(map_mine, map_theirs, t_send.at[1], t_recv.at[1], tp=1 - core)
    other.start()
    other.wait_recv()
    first = core == 0
    write_out[...] = jnp.where(first, map_mine[...], map_theirs[...])
    read_out[...] = jnp.where(first, map_theirs[...], map_mine[...])
    other.wait_send()
    over.wait_send()
    settle(back)


def third_stage(x_all, dm_all, maps, rows, states, terms):
    count, tok_rows, own_cols = x_all.shape
    size = maps.shape[-1]
    kv_cols = terms.shape[-1]
    depth = count // 4
    short = jnp.bfloat16
    hbm = pl.BlockSpec(memory_space=pl.ANY)
    vmem = pl.BlockSpec(memory_space=pltpu.VMEM)
    dma = pltpu.SemaphoreType.DMA
    copies = scatter_copies(depth)
    map_shape = (count, tok_rows, size)
    grad = jax.ShapeDtypeStruct((tok_rows, size), jnp.float32)
    return pl.pallas_call(
        third_kernel,
        in_specs=[vmem] * 6,
        out_specs=(hbm, vmem, vmem, vmem),
        out_shape=(
            jax.ShapeDtypeStruct((tok_rows, count * own_cols), short),
            jax.ShapeDtypeStruct((2, tok_rows, kv_cols), short),
            grad, grad,
        ),
        scratch_shapes=[
            pltpu.VMEM((count, tok_rows, own_cols), short),
            pltpu.VMEM((2,) + map_shape, short),
            pltpu.VMEM(map_shape, short),
            pltpu.VMEM(map_shape, short),
            pltpu.VMEM((tok_rows, size), jnp.float32),
            pltpu.VMEM((tok_rows, size), jnp.float32),
            pltpu.VMEM((size, own_cols), jnp.float32),
            pltpu.VMEM((2, depth, 2, tok_rows, kv_cols), short),
            pltpu.VMEM((2, depth, tok_rows, kv_cols), short),
            pltpu.VMEM((2, depth - 1, tok_rows, kv_cols), short),
            dma((count,)), dma((count,)), dma((count,)), dma((count,)),
            dma((copies,)), dma((copies,)), dma((2,)), dma((2,)),
        ],
        compiler_params=pltpu.CompilerParams(
            collective_id=2, has_side_effects=True, vmem_limit_bytes=VMEM_BYTES
        ),
        cost_estimate=pl.CostEstimate(
            flops=2 * 10**9, bytes_accessed=16 * 1024 * 1024, transcendentals=10**6
        ),
        name="scatter_and_scan",
    )(x_all, dm_all, maps, rows, states, terms)


def both_layers_direct(
    ssm_input, ssm_gate, state_write, state_read, log_decay, skip_gain, norm_gain, ssm_cotangent,
    queries, key_states, value_states, attn_cotangent,
):
    tok_rows, channel_count = ssm_input.shape
    head_count = log_decay.shape[1]
    head_dim = channel_count // head_count
    count = lax.axis_size("ctx")
    own_cols = channel_count // count
    states = state_write.shape[1]
    kv_cols = key_states.shape[1]
    kv = jnp.stack([key_states, value_states])
    own_map = jnp.where(lax.axis_index("tp") == 0, state_write, state_read)
    decay_rows = jnp.repeat(log_decay.T, head_dim // own_cols, axis=0)
    x_all, maps, rows, state_all, mixed_back, kv_all = first_stage(
        ssm_input, own_map, decay_rows, kv
    )
    skip = jnp.repeat(skip_gain, head_dim)[None, :]
    mixed = mixed_back.astype(jnp.float32) + skip * ssm_input.astype(jnp.float32)
    gate = ssm_gate.astype(jnp.float32)
    sigmoid = jax.nn.sigmoid(gate)
    gated = mixed * gate * sigmoid
    d_normed = ssm_cotangent.astype(jnp.float32) * norm_gain
    sums = lax.psum(
        jnp.stack([jnp.sum(gated * gated, axis=1), jnp.sum(d_normed * gated, axis=1)]), "tp"
    )
    root_mean = jnp.sqrt(sums[0] / CH + EPSILON)[:, None]
    inner_mean = (sums[1] / CH)[:, None] / root_mean
    normed = gated / root_mean
    ssm_output = (normed * norm_gain).astype(jnp.bfloat16)
    d_gated = (d_normed - normed * inner_mean) / root_mean
    d_mixed = d_gated * gate * sigmoid
    gate_grad = (d_gated * mixed * sigmoid * (1.0 + gate * (1.0 - sigmoid))).astype(jnp.bfloat16)
    attn_output, query_grad, dkv, dm_all = second_stage(
        queries, kv_all.reshape(count, 2, 2, tok_rows // 2, kv_cols), attn_cotangent,
        d_mixed.astype(jnp.bfloat16),
    )
    input_back, dkv_own, write_grad, read_grad = third_stage(
        x_all, dm_all, maps.reshape(2, count, tok_rows, states), rows, state_all,
        dkv.reshape(kv_all.shape),
    )
    input_grad = (input_back.astype(jnp.float32) + skip * d_mixed).astype(jnp.bfloat16)
    return (
        ssm_output, input_grad, gate_grad, write_grad, read_grad,
        attn_output, query_grad, dkv_own[0], dkv_own[1],
    )


def direct(mesh):
    count = mesh.shape["ctx"]
    return mesh.shape["tp"] == 2 and count % 4 == 0 and count >= 8 and CH // 2 // count % HD == 0


def solution(mesh):
    placed = (
        P("ctx", "tp"),
        P("ctx", "tp"),
        P("ctx", None),
        P("ctx", None),
        P("ctx", "tp"),
        P("tp"),
        P("tp"),
        P("ctx", "tp"),
        P("ctx", "tp"),
        P("ctx", "tp"),
        P("ctx", "tp"),
        P("ctx", "tp"),
    )
    return jax.shard_map(
        both_layers_direct if direct(mesh) else both_layers,
        mesh=mesh,
        in_specs=placed,
        out_specs=(
            P("ctx", "tp"),
            P("ctx", "tp"),
            P("ctx", "tp"),
            P("ctx", None),
            P("ctx", None),
            P("ctx", "tp"),
            P("ctx", "tp"),
            P("ctx", "tp"),
            P("ctx", "tp"),
        ),
        check_vma=False,
    )
```

```python
import functools

import jax
import jax.numpy as jnp
from jax import lax
from jax.experimental import pallas as pl
from jax.experimental.pallas import tpu as pltpu
from jax.sharding import PartitionSpec as P

HD = 128
CH = 8192
PRECISE = lax.Precision.HIGHEST
NEGATIVE = -1e30
EPSILON = 1e-05
TILE_KEYS = 256
CHUNK = 256
VMEM_BYTES = 48 * 1024 * 1024
VMEM_LARGE = 58 * 1024 * 1024


def dot(a, b, a_dim, b_dim):
    return lax.dot_general(
        a, b, (((a_dim,), (b_dim,)), ((), ())), preferred_element_type=jnp.float32
    )


def attention_kernel(
    place_ref, q_ref, kv_ref, cot_ref, out_ref, dq_ref, dkv_ref,
    keys, values, dk_sum, dv_sum, scores, q_rows, cot_rows, acc,
):
    count, _, _, half_rows, _ = kv_ref.shape
    group = q_ref.shape[1] // HD
    rows = group * half_rows
    scale = HD ** (-0.5)
    place = place_ref[0]
    for j in range(count):
        near = pl.ds(j * half_rows, half_rows)
        far = pl.ds((2 * count - 1 - j) * half_rows, half_rows)
        keys[near] = kv_ref[j, 0, 0]
        keys[far] = kv_ref[j, 0, 1]
        values[near] = kv_ref[j, 1, 0]
        values[far] = kv_ref[j, 1, 1]
    dk_sum[...] = jnp.zeros_like(dk_sum)
    dv_sum[...] = jnp.zeros_like(dv_sum)
    for half in range(2):
        block = place if half == 0 else 2 * count - 1 - place
        tiles = block // (TILE_KEYS // half_rows) + 1
        for h in range(group):
            there = (pl.ds(half * half_rows, half_rows), pl.ds(h * HD, HD))
            q_rows[pl.ds(h * half_rows, half_rows)] = q_ref[there]
            cot_rows[pl.ds(h * half_rows, half_rows)] = cot_ref[there]
        q_pos = block * half_rows + lax.broadcasted_iota(jnp.int32, (1, rows), 1) % half_rows

        def score_turn(tile, top):
            at = pl.ds(pl.multiple_of(tile * TILE_KEYS, TILE_KEYS), TILE_KEYS)
            s = dot(keys[at], q_rows[...], 1, 1) * scale
            key_pos = tile * TILE_KEYS + lax.broadcasted_iota(jnp.int32, s.shape, 0)
            s = jnp.where(key_pos <= q_pos, s, NEGATIVE)
            scores[at] = s
            return jnp.maximum(top, jnp.max(s, axis=0, keepdims=True))

        top = lax.fori_loop(0, tiles, score_turn, jnp.full((1, rows), NEGATIVE, jnp.float32))
        acc[...] = jnp.zeros_like(acc)

        def value_turn(tile, total):
            at = pl.ds(pl.multiple_of(tile * TILE_KEYS, TILE_KEYS), TILE_KEYS)
            p = jnp.exp(scores[at] - top)
            scores[at] = p
            acc[...] += dot(values[at], p.astype(jnp.bfloat16), 0, 0)
            return total + jnp.sum(p, axis=0, keepdims=True)

        total = lax.fori_loop(0, tiles, value_turn, jnp.zeros((1, rows), jnp.float32))
        inverse = 1.0 / total
        out_t = acc[...] * inverse
        out_rows = out_t.T.astype(jnp.bfloat16)
        cot_t = cot_rows[...].astype(jnp.float32).T
        delta = jnp.sum(
            cot_t * out_t.astype(jnp.bfloat16).astype(jnp.float32), axis=0, keepdims=True
        )
        acc[...] = jnp.zeros_like(acc)

        def grad_turn(tile, carry):
            at = pl.ds(pl.multiple_of(tile * TILE_KEYS, TILE_KEYS), TILE_KEYS)
            w = scores[at] * inverse
            d_prob = dot(values[at], cot_rows[...], 1, 1)
            d_score = (w * (d_prob - delta) * scale).astype(jnp.bfloat16)
            acc[...] += dot(keys[at], d_score, 0, 0)
            dk_sum[at] += dot(d_score, q_rows[...], 1, 0)
            dv_sum[at] += dot(w.astype(jnp.bfloat16), cot_rows[...], 1, 0)
            return carry

        lax.fori_loop(0, tiles, grad_turn, 0)
        dq_rows = acc[...].T.astype(jnp.bfloat16)
        for h in range(group):
            there = (pl.ds(half * half_rows, half_rows), pl.ds(h * HD, HD))
            out_ref[there] = out_rows[h * half_rows : (h + 1) * half_rows]
            dq_ref[there] = dq_rows[h * half_rows : (h + 1) * half_rows]
    for j in range(count):
        near = pl.ds(j * half_rows, half_rows)
        far = pl.ds((2 * count - 1 - j) * half_rows, half_rows)
        dkv_ref[j, 0, 0] = dk_sum[near].astype(jnp.bfloat16)
        dkv_ref[j, 0, 1] = dk_sum[far].astype(jnp.bfloat16)
        dkv_ref[j, 1, 0] = dv_sum[near].astype(jnp.bfloat16)
        dkv_ref[j, 1, 1] = dv_sum[far].astype(jnp.bfloat16)


def attention_core(queries, kv_all, attn_cotangent, place):
    tok_rows, q_cols = queries.shape
    count, _, _, half_rows, kv_cols = kv_all.shape
    kv_heads = kv_cols // HD
    width = q_cols // kv_heads
    rows = width // HD * half_rows
    total = count * tok_rows
    wide = pl.BlockSpec((tok_rows, width), lambda g, place: (0, g))
    pair = pl.BlockSpec((count, 2, 2, half_rows, HD), lambda g, place: (0, 0, 0, 0, g))
    like_q = jax.ShapeDtypeStruct(queries.shape, jnp.bfloat16)
    flops = 7 * 2 * tok_rows * q_cols * total // 2
    return pl.pallas_call(
        attention_kernel,
        out_shape=(like_q, like_q, jax.ShapeDtypeStruct(kv_all.shape, jnp.bfloat16)),
        grid_spec=pltpu.PrefetchScalarGridSpec(
            num_scalar_prefetch=1,
            grid=(kv_heads,),
            in_specs=[wide, pair, wide],
            out_specs=(wide, wide, pair),
            scratch_shapes=[
                pltpu.VMEM((total, HD), jnp.bfloat16),
                pltpu.VMEM((total, HD), jnp.bfloat16),
                pltpu.VMEM((total, HD), jnp.float32),
                pltpu.VMEM((total, HD), jnp.float32),
                pltpu.VMEM((total, rows), jnp.float32),
                pltpu.VMEM((rows, HD), jnp.bfloat16),
                pltpu.VMEM((rows, HD), jnp.bfloat16),
                pltpu.VMEM((HD, rows), jnp.float32),
            ],
        ),
        compiler_params=pltpu.CompilerParams(vmem_limit_bytes=VMEM_BYTES),
        cost_estimate=pl.CostEstimate(
            flops=3 * flops, bytes_accessed=16 * 1024 * 1024, transcendentals=total * q_cols // 2
        ),
        name="attention_both",
    )(place.reshape(1).astype(jnp.int32), queries, kv_all, attn_cotangent)


def gather_pair(kv):
    _, tok_rows, kv_cols = kv.shape
    return lax.all_gather(kv, "ctx", axis=0).reshape(
        lax.axis_size("ctx"), 2, 2, tok_rows // 2, kv_cols
    )


def scatter_pair(dkv):
    count, _, _, half_rows, kv_cols = dkv.shape
    mine = lax.psum_scatter(
        dkv.reshape(count, 2, 2 * half_rows, kv_cols), "ctx", scatter_dimension=0, tiled=False
    )
    return (mine[0], mine[1])


def in_order(ref, step, steps):
    pieces = ref.shape[0]
    early = step < steps // 2
    return [ref[jnp.where(early, j, pieces - 1 - j)] for j in range(pieces)]


def put_in_order(ref, value, step, steps):
    pieces, rows = ref.shape[0], ref.shape[1]
    early = step < steps // 2
    for j in range(pieces):
        ref[jnp.where(early, j, pieces - 1 - j)] = value[j * rows : (j + 1) * rows].astype(
            ref.dtype
        )


def whole(ref, step, steps):
    return jnp.concatenate(in_order(ref, step, steps), axis=0)


def causal_decay(col, row, flip):
    shape = (col.shape[0], row.shape[1])
    down = lax.broadcasted_iota(jnp.int32, shape, 0)
    across = lax.broadcasted_iota(jnp.int32, shape, 1)
    if flip:
        return jnp.exp(jnp.where(across >= down, row - col, NEGATIVE))
    return jnp.exp(jnp.where(down >= across, col - row, NEGATIVE))


def forward_kernel(steps, x_ref, b_ref, c_ref, col_ref, row_ref, mixed_ref, state_ref, state):
    step = pl.program_id(0)

    @pl.when(step == 0)
    def _():
        state[...] = jnp.zeros_like(state)

    x = whole(x_ref, step, steps)
    b = whole(b_ref, step, steps)
    c = whole(c_ref, step, steps)
    col, row = col_ref[...], row_ref[0]
    last = col[CHUNK - 1 : CHUNK]
    weights = (causal_decay(col, row, False) * dot(c, b, 1, 1)).astype(jnp.bfloat16)
    entering = state[...]
    entering_short = entering.astype(jnp.bfloat16)
    state_ref[0] = entering_short
    mixed = dot(weights, x, 1, 0) + jnp.exp(col) * dot(c, entering_short, 1, 0)
    put_in_order(mixed_ref, mixed, step, steps)
    shrunk = (b.astype(jnp.float32) * jnp.exp(last - col)).astype(jnp.bfloat16)
    state[...] = jnp.exp(last) * entering + dot(shrunk, x, 0, 0)


def backward_kernel(
    steps, x_ref, dm_ref, b_ref, c_ref, col_ref, row_ref, state_ref,
    input_ref, write_ref, read_ref, adjoint,
):
    step = steps - 1 - pl.program_id(0)

    @pl.when(pl.program_id(0) == 0)
    def _():
        adjoint[...] = jnp.zeros_like(adjoint)

    x = whole(x_ref, step, steps)
    dm = whole(dm_ref, step, steps)
    b = whole(b_ref, step, steps)
    c = whole(c_ref, step, steps)
    col, row = col_ref[...], row_ref[0]
    last = col[CHUNK - 1 : CHUNK]
    shrink, grow = jnp.exp(last - col), jnp.exp(col)
    entering = adjoint[...]
    entering_short = entering.astype(jnp.bfloat16)
    decay_t = causal_decay(col, row, True)
    weights_t = (decay_t * dot(b, c, 1, 1)).astype(jnp.bfloat16)
    input_g = dot(weights_t, dm, 1, 0) + shrink * dot(b, entering_short, 1, 0)
    put_in_order(input_ref, input_g, step, steps)
    pairs_t = (decay_t * dot(x, dm, 1, 1)).astype(jnp.bfloat16)
    write_g = dot(pairs_t, c, 1, 0) + shrink * dot(x, entering_short, 1, 1)
    pairs = (causal_decay(col, row, False) * dot(dm, x, 1, 1)).astype(jnp.bfloat16)
    read_g = dot(pairs, b, 1, 0) + grow * dot(dm, state_ref[0], 1, 1)
    put_in_order(write_ref, write_g, step, steps)
    put_in_order(read_ref, read_g, step, steps)
    grown = (c.astype(jnp.float32) * grow).astype(jnp.bfloat16)
    adjoint[...] = jnp.exp(last) * entering + dot(grown, dm, 0, 0)


def ssm_specs(count, half_rows, steps, order):
    per = CHUNK // half_rows

    def rows_spec(cols):
        def place(i):
            step = order(i)
            early = step < steps // 2
            return (
                jnp.where(early, step, steps - 1 - step), jnp.where(early, 0, 1), 0, 0
            )

        return pl.BlockSpec((per, pl.Squeezed(), half_rows, cols), place)

    return (
        rows_spec,
        pl.BlockSpec((CHUNK, 1), lambda i: (order(i), 0)),
        pl.BlockSpec((1, 1, CHUNK), lambda i: (order(i), 0, 0)),
    )


def scan_forward(x, b, c, col, row):
    count, _, half_rows, cols = x.shape
    states = b.shape[-1]
    steps = count * 2 * half_rows // CHUNK
    rows_spec, col_spec, row_spec = ssm_specs(count, half_rows, steps, lambda i: i)
    return pl.pallas_call(
        functools.partial(forward_kernel, steps),
        grid=(steps,),
        in_specs=[rows_spec(cols), rows_spec(states), rows_spec(states), col_spec, row_spec],
        out_specs=(rows_spec(cols), pl.BlockSpec((1, states, cols), lambda i: (i, 0, 0))),
        out_shape=(
            jax.ShapeDtypeStruct(x.shape, jnp.bfloat16),
            jax.ShapeDtypeStruct((steps, states, cols), jnp.bfloat16),
        ),
        scratch_shapes=[pltpu.VMEM((states, cols), jnp.float32)],
        compiler_params=pltpu.CompilerParams(vmem_limit_bytes=VMEM_BYTES),
        cost_estimate=pl.CostEstimate(
            flops=10**9, bytes_accessed=6 * 1024 * 1024, transcendentals=5 * 10**5
        ),
        name="scan_forward",
    )(x, b, c, col, row)


def scan_backward(x, dm, b, c, col, row, state):
    count, _, half_rows, cols = x.shape
    states = b.shape[-1]
    steps = count * 2 * half_rows // CHUNK
    rows_spec, col_spec, row_spec = ssm_specs(
        count, half_rows, steps, lambda i: steps - 1 - i
    )
    return pl.pallas_call(
        functools.partial(backward_kernel, steps),
        grid=(steps,),
        in_specs=[
            rows_spec(cols), rows_spec(cols), rows_spec(states), rows_spec(states),
            col_spec, row_spec,
            pl.BlockSpec((1, states, cols), lambda i: (steps - 1 - i, 0, 0)),
        ],
        out_specs=(rows_spec(cols), rows_spec(states), rows_spec(states)),
        out_shape=(
            jax.ShapeDtypeStruct(x.shape, jnp.bfloat16),
            jax.ShapeDtypeStruct(b.shape, jnp.bfloat16),
            jax.ShapeDtypeStruct(b.shape, jnp.bfloat16),
        ),
        scratch_shapes=[pltpu.VMEM((states, cols), jnp.float32)],
        compiler_params=pltpu.CompilerParams(vmem_limit_bytes=VMEM_BYTES),
        cost_estimate=pl.CostEstimate(
            flops=2 * 10**9, bytes_accessed=6 * 1024 * 1024, transcendentals=10**6
        ),
        name="scan_backward",
    )(x, dm, b, c, col, row, state)


def to_channels(values, extra=None):
    count = lax.axis_size("ctx")
    parts = values.reshape(values.shape[0], count, -1)
    if extra is not None:
        shape = (values.shape[0], count, extra.shape[1])
        parts = jnp.concatenate([parts, jnp.broadcast_to(extra[:, None, :], shape)], axis=2)
    blocks = jnp.transpose(parts, (1, 0, 2))
    return lax.all_to_all(blocks, "ctx", split_axis=0, concat_axis=0)


def to_owners(blocks):
    return lax.all_to_all(blocks, "ctx", split_axis=0, concat_axis=0)


def side_by_side(blocks):
    return jnp.transpose(blocks, (1, 0, 2)).reshape(blocks.shape[1], -1)


def from_other_core(values):
    return lax.ppermute(values, "tp", [(0, 1), (1, 0)])


def both_layers(
    ssm_input, ssm_gate, state_write, state_read, log_decay, skip_gain, norm_gain, ssm_cotangent,
    queries, key_states, value_states, attn_cotangent,
):
    tok_rows, channel_count = ssm_input.shape
    head_count = log_decay.shape[1]
    half_rows = tok_rows // 2
    head_dim = channel_count // head_count
    count = lax.axis_size("ctx")
    own_cols = channel_count // count
    states = state_write.shape[1]
    folded = (count, 2, half_rows)
    share_maps = lax.axis_size("tp") == 2
    kv = jnp.stack([key_states, value_states])
    kv, sent_input, log_decay = lax.optimization_barrier((kv, ssm_input, log_decay))
    kv_all = gather_pair(kv)
    if share_maps:
        first = lax.axis_index("tp") == 0
        arrived = to_channels(sent_input, jnp.where(first, state_write, state_read))
        own_map = arrived[:, :, own_cols:]
        other_map = from_other_core(own_map)
        b_all = jnp.where(first, own_map, other_map).reshape(*folded, states)
        c_all = jnp.where(first, other_map, own_map).reshape(*folded, states)
    else:
        arrived = to_channels(sent_input, jnp.concatenate([state_write, state_read], axis=1))
        b_all = arrived[:, :, own_cols : own_cols + states].reshape(*folded, states)
        c_all = arrived[:, :, own_cols + states :].reshape(*folded, states)
    x_all = arrived[:, :, :own_cols].reshape(*folded, own_cols)
    decay_rows = jnp.repeat(log_decay.T, head_dim // own_cols, axis=0)
    own_decay = to_owners(decay_rows[:, None, :]).reshape(*folded)
    ordered = jnp.concatenate([own_decay[:, 0], own_decay[::-1, 1]]).reshape(-1, CHUNK)
    upto = jnp.triu(jnp.ones((CHUNK, CHUNK), jnp.float32))
    log_total = jnp.dot(ordered, upto, precision=PRECISE)
    col = log_total.reshape(-1, 1)
    row = log_total[:, None, :]
    mixed_all, state_all = scan_forward(x_all, b_all, c_all, col, row)
    mixed_all, kv_all = lax.optimization_barrier((mixed_all, kv_all))
    attn_output, query_grad, dkv = attention_core(
        queries, kv_all, attn_cotangent, lax.axis_index("ctx")
    )
    mixed_back = to_owners(mixed_all.reshape(count, tok_rows, own_cols))
    dkv, mixed_back = lax.optimization_barrier((dkv, mixed_back))
    key_grad, value_grad = scatter_pair(dkv)
    skip = jnp.repeat(skip_gain, head_dim)[None, :]
    mixed = side_by_side(mixed_back)
    mixed = mixed.astype(jnp.float32) + skip * ssm_input.astype(jnp.float32)
    gate = ssm_gate.astype(jnp.float32)
    sigmoid = jax.nn.sigmoid(gate)
    gated = mixed * gate * sigmoid
    d_normed = ssm_cotangent.astype(jnp.float32) * norm_gain
    sums = lax.psum(
        jnp.stack([jnp.sum(gated * gated, axis=1), jnp.sum(d_normed * gated, axis=1)]), "tp"
    )
    root_mean = jnp.sqrt(sums[0] / CH + EPSILON)[:, None]
    inner_mean = (sums[1] / CH)[:, None] / root_mean
    normed = gated / root_mean
    ssm_output = (normed * norm_gain).astype(jnp.bfloat16)
    d_gated = (d_normed - normed * inner_mean) / root_mean
    d_mixed = d_gated * gate * sigmoid
    gate_grad = (d_gated * mixed * sigmoid * (1.0 + gate * (1.0 - sigmoid))).astype(jnp.bfloat16)
    dm_all = to_channels(d_mixed.astype(jnp.bfloat16)).reshape(*folded, own_cols)
    input_all, write_all, read_all = scan_backward(
        x_all, dm_all, b_all, c_all, col, row, state_all
    )
    blocks = (count, tok_rows)
    input_all = input_all.reshape(*blocks, own_cols)
    write_all, read_all = write_all.reshape(*blocks, states), read_all.reshape(*blocks, states)
    if share_maps:
        kept = jnp.where(first, write_all, read_all)
        passed = from_other_core(jnp.where(first, read_all, write_all))
        maps_all = (kept.astype(jnp.float32) + passed.astype(jnp.float32)).astype(jnp.bfloat16)
    else:
        maps_all = jnp.concatenate([write_all, read_all], axis=2)
    back = to_owners(jnp.concatenate([input_all, maps_all], axis=2))
    input_g = side_by_side(back[:, :, :own_cols]).astype(jnp.float32)
    input_grad = (input_g + skip * d_mixed).astype(jnp.bfloat16)
    maps = jnp.sum(back[:, :, own_cols:].astype(jnp.float32), axis=0)
    if share_maps:
        other = from_other_core(maps)
        write_grad, read_grad = jnp.where(first, maps, other), jnp.where(first, other, maps)
    else:
        maps = lax.psum(maps.astype(jnp.bfloat16), "tp").astype(jnp.float32)
        write_grad, read_grad = maps[:, :states], maps[:, states:]
    return (
        ssm_output, input_grad, gate_grad, write_grad, read_grad,
        attn_output, query_grad, key_grad, value_grad,
    )


MESH = pl.DeviceIdType.MESH


def remote(src, dst, send, recv, **to):
    return pltpu.make_async_remote_copy(
        src_ref=src, dst_ref=dst, send_sem=send, recv_sem=recv,
        device_id=to, device_id_type=MESH,
    )


def ring(at, step, size):
    return lax.rem(at + step, size)


def spot():
    me = lax.axis_index("ctx")
    return me, lax.div(me, 4), lax.rem(lax.div(me, 2), 2), lax.rem(me, 2)


def greet(count, me, core=None):
    barrier = pltpu.get_barrier_semaphore()
    for k in range(1, count):
        pl.semaphore_signal(
            barrier, inc=1, device_id={"ctx": ring(me, k, count)}, device_id_type=MESH
        )
    if core is not None:
        pl.semaphore_signal(barrier, inc=1, device_id={"tp": 1 - core}, device_id_type=MESH)
    pl.semaphore_wait(barrier, count - 1 if core is None else count)


def columns(p, width):
    return pl.ds(pl.multiple_of(p * width, width), width)


def spread(count, me, pick, place, send, recv):
    local = pltpu.make_async_copy(pick(me), place(me), send.at[0])
    local.start()
    copies = []
    for k in range(1, count):
        p = ring(me, k, count)
        copy = remote(pick(p), place(me), send.at[k], recv.at[k], ctx=p)
        copy.start()
        copies.append(copy)
    return local, copies


def settle(pieces):
    local, copies = pieces
    for copy in copies:
        copy.wait_recv()
    for copy in copies:
        copy.wait_send()
    local.wait()


def index_of(z, y, x):
    return z * 4 + y * 2 + x


def gather_turns(own, dest, cols, where, send, recv, local):
    _, z, y, x = where
    depth = dest.shape[0]
    used = []

    def post(src, dst, to):
        copy = remote(src, dst, send.at[len(used)], recv.at[len(used)], ctx=to)
        copy.start()
        used.append(copy)
        return copy

    def block(at, c):
        return dest.at[at, y, x, c, :, cols]

    mine = [
        pltpu.make_async_copy(own[c].at[:, cols], block(z, c), local.at[c]) for c in range(2)
    ]
    for copy in mine:
        copy.start()
    over_x, over_y = index_of(z, y, 1 - x), index_of(z, 1 - y, x)
    first = [
        post(own[0].at[:, cols], block(z, 0), over_x),
        post(own[1].at[:, cols], block(z, 1), over_y),
    ]
    along = {}
    for k in range(1, depth):
        to = index_of(ring(z, k, depth), y, x)
        along[k] = [post(own[c].at[:, cols], block(z, c), to) for c in range(2)]
    yield
    for copy in mine:
        copy.wait()

    def pair(at, arrived):
        arrived[0].wait_recv()
        keys = dest.at[at, y, :, 0, :, cols]
        a = post(keys, keys, over_y)
        arrived[1].wait_recv()
        values = dest.at[at, :, x, 1, :, cols]
        return a, post(values, values, over_x)

    ends = list(pair(z, first))
    yield
    onward = {}
    for k in range(1, depth):
        at = ring(z, depth - k, depth)
        for copy in along[k]:
            copy.wait_recv()
        onward[k] = [post(block(at, 0), block(at, 0), over_x), post(block(at, 1), block(at, 1), over_y)]
        yield
    for k in range(1, depth):
        ends += pair(ring(z, depth - k, depth), onward[k])
        yield
    for copy in ends:
        copy.wait_recv()
    for copy in used:
        copy.wait_send()


def gather_copies(depth):
    return 2 + 2 * (depth - 1) * 3 + 2


def scatter_turns(terms, cols, out, half_way, next_way, last_way, where, send, recv):
    _, z, y, x = where
    depth = terms.shape[0]
    used = []

    def post(src, dst, to):
        copy = remote(src, dst, send.at[len(used)], recv.at[len(used)], ctx=to)
        copy.start()
        used.append(copy)
        return copy

    def wide(value):
        return value.astype(jnp.float32)

    over_x, over_y = index_of(z, y, 1 - x), index_of(z, 1 - y, x)
    order = list(range(1, depth)) + [0]
    first, second, third = {}, {}, []
    for k in order:
        at = ring(z, k, depth)
        first[k] = (
            post(terms.at[at, 1 - y, :, 0, :, cols], half_way.at[0, at], over_y),
            post(terms.at[at, :, 1 - x, 1, :, cols], half_way.at[1, at], over_x),
        )
    yield
    for k in order:
        at = ring(z, k, depth)
        first[k][0].wait_recv()
        half_way[0, at, 1 - x] = (
            wide(half_way[0, at, 1 - x]) + wide(terms[at, y, 1 - x, 0, :, cols])
        ).astype(jnp.bfloat16)
        a = post(half_way.at[0, at, 1 - x], next_way.at[0, at], over_x)
        first[k][1].wait_recv()
        half_way[1, at, 1 - y] = (
            wide(half_way[1, at, 1 - y]) + wide(terms[at, 1 - y, x, 1, :, cols])
        ).astype(jnp.bfloat16)
        second[k] = (a, post(half_way.at[1, at, 1 - y], next_way.at[1, at], over_y))
        yield
    for k in order:
        at = ring(z, k, depth)
        for c in range(2):
            second[k][c].wait_recv()
            total = (
                wide(next_way[c, at]) + wide(half_way[c, at, y if c else x])
                + wide(terms[at, y, x, c, :, cols])
            )
            next_way[c, at] = total.astype(jnp.bfloat16)
            if k:
                third.append(
                    post(next_way.at[c, at], last_way.at[c, k - 1], index_of(at, y, x))
                )
        yield
    for copy in third:
        copy.wait_recv()
    for c in range(2):
        total = wide(next_way[c, z])
        for k in range(1, depth):
            total = total + wide(last_way[c, k - 1])
        out[c][:, cols] = total.astype(jnp.bfloat16)
    for copy in used:
        copy.wait_send()


def scatter_copies(depth):
    return 4 * depth + 2 * (depth - 1)


def running_decay(decay, rows, half_rows):
    per = CHUNK // half_rows
    groups = decay.shape[0] // per
    width = 2 * half_rows
    side = jnp.concatenate(
        [decay[pl.ds(j, groups, stride=per)] for j in range(per)], axis=1
    )
    shape = (per * width, 2 * CHUNK)
    r = lax.broadcasted_iota(jnp.int32, shape, 0)
    u = lax.broadcasted_iota(jnp.int32, shape, 1)
    j, t = r // width, r % width
    near = (t < half_rows) & (u < CHUNK) & (j * half_rows + t <= u)
    far = (t >= half_rows) & (u >= CHUNK)
    far = far & ((per - 1 - j) * half_rows + t - half_rows <= u - CHUNK)
    ones = jnp.where(near | far, 1.0, 0.0)
    sums = lax.dot_general(
        side, ones, (((1,), (0,)), ((), ())), precision=PRECISE,
        preferred_element_type=jnp.float32,
    )
    rows[0:groups] = sums[:, :CHUNK]
    rows[groups : 2 * groups] = sums[:, CHUNK:]


def members(group, half, per):
    return [per * group + (j if half == 0 else per - 1 - j) for j in range(per)]


def chunk_of(ref, ids, half, half_rows):
    return jnp.concatenate(
        [ref[d, half * half_rows : (half + 1) * half_rows] for d in ids], axis=0
    )


def put_chunk(ref, ids, half, half_rows, value):
    value = value.astype(ref.dtype)
    for j, d in enumerate(ids):
        ref[d, half * half_rows : (half + 1) * half_rows] = value[
            j * half_rows : (j + 1) * half_rows
        ]


def as_column(row):
    shape = (row.shape[1], row.shape[1])
    same = lax.broadcasted_iota(jnp.int32, shape, 0) == lax.broadcasted_iota(jnp.int32, shape, 1)
    return jnp.sum(jnp.where(same, row, 0.0), axis=1, keepdims=True)


def layers_kernel(
    x_hbm, gate_hbm, write_hbm, read_hbm, decay_hbm, skip_ref, gain_ref, up_hbm,
    q_hbm, k_hbm, v_hbm, cot_hbm,
    ssm_out, input_out, gate_out, write_out, read_out, attn_out, query_out, key_out, value_out,
    x_ref, gate_ref, up_ref, q_ref, cot_ref, own_map,
    decay, rows, state, states, x_all, maps, mixed_all, mixed_back,
    sums_mine, sums_theirs, dm_ref, dm_wide, dm_all, input_back,
    map_terms, map_in, map_back, map_mine, map_theirs,
    kv_all, terms, half_way, next_way, last_way,
    scores, tops, dk_sum, dv_sum, q_rows, cot_rows, acc,
    ssm_ref, input_ref, gate_grad, attn_ref, dq_ref,
    x_send, x_recv, d_send, d_recv, b_send, b_recv, m_send, m_recv, i_send, i_recv,
    p_send, p_recv, map_send, map_recv, g_send, g_recv, g_local, s_send, s_recv,
    t_send, t_recv, load_sem, store_sem,
):
    where = spot()
    me, z, y, x = where
    core = lax.axis_index("tp")
    count, tok_rows, own_cols = x_all.shape
    channels = x_ref.shape[1]
    half_rows = tok_rows // 2
    depth = count // 4
    per = CHUNK // half_rows
    groups = count // per
    pairs = g_send.shape[0]
    kv_cols = k_hbm.shape[1]
    kv_heads = kv_cols // HD
    group_cols = q_ref.shape[1] // kv_heads
    group_size = group_cols // HD
    q_count = group_size * half_rows
    pair_cols = [slice(i * kv_cols // pairs, (i + 1) * kv_cols // pairs) for i in range(pairs)]
    scale = HD ** (-0.5)
    to_exp2 = scale * 1.4426950408889634

    loads = {}
    for i, (name, src, dst) in enumerate((
        ("q", q_hbm, q_ref), ("cot", cot_hbm, cot_ref), ("x", x_hbm, x_ref),
        ("gate", gate_hbm, gate_ref), ("up", up_hbm, up_ref),
    )):
        loads[name] = pltpu.make_async_copy(src, dst, load_sem.at[i])
        loads[name].start()
    own_map_sem = load_sem.at[len(loads)]

    @pl.when(core == 0)
    def _():
        pltpu.make_async_copy(write_hbm, own_map, own_map_sem).start()

    @pl.when(core != 0)
    def _():
        pltpu.make_async_copy(read_hbm, own_map, own_map_sem).start()

    greet(count, me, core)
    decays = spread(
        count, me, lambda p: decay_hbm.at[pl.ds(p, 1)], lambda p: decay.at[pl.ds(p, 1)],
        d_send, d_recv,
    )
    pltpu.make_async_copy(write_hbm, own_map, own_map_sem).wait()
    copy_map = pltpu.make_async_copy(own_map, maps.at[core, z, y, x], m_send.at[0])
    copy_map.start()
    used = []

    def post(src, dst, **to):
        copy = remote(src, dst, m_send.at[len(used) + 1], m_recv.at[len(used) + 1], **to)
        copy.start()
        used.append(copy)
        return copy

    for k in range(1, depth):
        post(own_map, maps.at[core, z, y, x], ctx=index_of(ring(z, k, depth), y, x))
    inputs = spread(
        count, me, lambda p: x_hbm.at[:, columns(p, own_cols)], lambda p: x_all.at[p],
        x_send, x_recv,
    )
    gathers = [
        gather_turns(
            (k_hbm, v_hbm), kv_all, pair_cols[i], where, g_send.at[i], g_recv.at[i], g_local.at[i]
        )
        for i in range(pairs)
    ]
    scatters = [
        scatter_turns(
            terms, pair_cols[i], (key_out, value_out), half_way.at[i], next_way.at[i],
            last_way.at[i], where, s_send.at[i], s_recv.at[i],
        )
        for i in range(pairs)
    ]

    def turn(turns, times=1):
        for _ in range(times):
            next(turns, None)

    def finish(turns):
        for _ in turns:
            pass

    turn(gathers[0])
    for copy in used:
        copy.wait_recv()
    copy_map.wait()
    part = maps.at[core, :, y, x]
    post(part, part, ctx=index_of(z, y, 1 - x)).wait_recv()
    part = maps.at[core, :, y]
    post(part, part, ctx=index_of(z, 1 - y, x)).wait_recv()
    part = maps.at[core]
    over = post(part, part, tp=1 - core)
    turn(gathers[0])
    settle(decays)
    running_decay(decay, rows, half_rows)
    over.wait_recv()
    for copy in used:
        copy.wait_send()
    settle(inputs)
    state[...] = jnp.zeros_like(state)

    def chunk_map(which, group, half):
        js = range(per) if half == 0 else range(per - 1, -1, -1)
        at = slice(half * half_rows, (half + 1) * half_rows)
        return jnp.concatenate([maps[which, group, j // 2, j % 2, at] for j in js], axis=0)

    def forward(group, half):
        ids = members(group, half, per)
        step = group if half == 0 else 2 * groups - 1 - group
        value = chunk_of(x_all, ids, half, half_rows)
        b, c = chunk_map(0, group, half), chunk_map(1, group, half)
        row = rows[pl.ds(half * groups + group, 1)]
        col = as_column(row)
        last = col[CHUNK - 1 : CHUNK]
        weights = (causal_decay(col, row, False) * dot(c, b, 1, 1)).astype(jnp.bfloat16)
        entering = state[...]
        entering_short = entering.astype(jnp.bfloat16)
        states[step] = entering_short
        result = dot(weights, value, 1, 0) + jnp.exp(col) * dot(c, entering_short, 1, 0)
        put_chunk(mixed_all, ids, half, half_rows, result)
        shrunk = (b.astype(jnp.float32) * jnp.exp(last - col)).astype(jnp.bfloat16)
        state[...] = jnp.exp(last) * entering + dot(shrunk, value, 0, 0)

    def backward(group, half):
        ids = members(group, half, per)
        step = group if half == 0 else 2 * groups - 1 - group
        value = chunk_of(x_all, ids, half, half_rows)
        dm = chunk_of(dm_all, ids, half, half_rows)
        b, c = chunk_map(0, group, half), chunk_map(1, group, half)
        row = rows[pl.ds(half * groups + group, 1)]
        col = as_column(row)
        last = col[CHUNK - 1 : CHUNK]
        shrink, grow = jnp.exp(last - col), jnp.exp(col)
        entering = state[...]
        entering_short = entering.astype(jnp.bfloat16)
        decay_t = causal_decay(col, row, True)
        weights_t = (decay_t * dot(b, c, 1, 1)).astype(jnp.bfloat16)
        input_g = dot(weights_t, dm, 1, 0) + shrink * dot(b, entering_short, 1, 0)
        put_chunk(mixed_all, ids, half, half_rows, input_g)
        pairs_t = (decay_t * dot(value, dm, 1, 1)).astype(jnp.bfloat16)
        write_g = dot(pairs_t, c, 1, 0) + shrink * dot(value, entering_short, 1, 1)
        pairs_f = (causal_decay(col, row, False) * dot(dm, value, 1, 1)).astype(jnp.bfloat16)
        read_g = dot(pairs_f, b, 1, 0) + grow * dot(dm, states[step], 1, 1)
        put_chunk(map_terms.at[0], ids, half, half_rows, write_g)
        put_chunk(map_terms.at[1], ids, half, half_rows, read_g)
        grown = (c.astype(jnp.float32) * grow).astype(jnp.bfloat16)
        state[...] = jnp.exp(last) * entering + dot(grown, dm, 0, 0)

    wide_cols = 1024
    strip = 16

    def pieces_of(r):
        at = pl.ds(pl.multiple_of(r * strip, strip), strip)
        for c in range(channels // wide_cols):
            cols = slice(c * wide_cols, (c + 1) * wide_cols)
            gate = gate_ref[at, cols].astype(jnp.float32)
            sigmoid = 0.5 * jnp.tanh(0.5 * gate) + 0.5
            mixed = mixed_back[at, cols].astype(jnp.float32) + skip_ref[:, cols] * x_ref[
                at, cols
            ].astype(jnp.float32)
            d_normed = up_ref[at, cols].astype(jnp.float32) * gain_ref[:, cols]
            yield at, cols, gate, sigmoid, mixed, d_normed

    def norm():
        @pl.loop(0, tok_rows // strip)
        def _(r):
            squares = jnp.zeros((strip, 1), jnp.float32)
            inner = jnp.zeros((strip, 1), jnp.float32)
            for at, cols, gate, sigmoid, mixed, d_normed in pieces_of(r):
                gated = mixed * gate * sigmoid
                squares = squares + jnp.sum(gated * gated, axis=1, keepdims=True)
                inner = inner + jnp.sum(d_normed * gated, axis=1, keepdims=True)
            sums_mine[0, at] = jnp.broadcast_to(squares, (strip, HD))
            sums_mine[1, at] = jnp.broadcast_to(inner, (strip, HD))

        swap = remote(sums_mine, sums_theirs, t_send.at[0], t_recv.at[0], tp=1 - core)
        swap.start()
        swap.wait()

        @pl.loop(0, tok_rows // strip)
        def _(r):
            at = pl.ds(pl.multiple_of(r * strip, strip), strip)
            squares = sums_mine[0, at] + sums_theirs[0, at]
            inner = sums_mine[1, at] + sums_theirs[1, at]
            inverse = 1.0 / jnp.sqrt(squares[:, :1] / CH + EPSILON)
            inner_mean = inner[:, :1] / CH * inverse
            for at, cols, gate, sigmoid, mixed, d_normed in pieces_of(r):
                silu = gate * sigmoid
                normed = mixed * silu * inverse
                ssm_ref[at, cols] = (normed * gain_ref[:, cols]).astype(jnp.bfloat16)
                d_gated = (d_normed - normed * inner_mean) * inverse
                d_mixed = d_gated * silu
                dm_ref[at, cols] = d_mixed.astype(jnp.bfloat16)
                dm_wide[at, cols] = skip_ref[:, cols] * d_mixed
                gate_grad[at, cols] = (
                    d_gated * mixed * sigmoid * (1.0 + gate * (1.0 - sigmoid))
                ).astype(jnp.bfloat16)

    def attend(head, half):
        cols = slice(head * HD, (head + 1) * HD)
        token_at = slice(half * half_rows, (half + 1) * half_rows)
        for h in range(group_size):
            q_at = slice(head * group_cols + h * HD, head * group_cols + (h + 1) * HD)
            q_rows[h * half_rows : (h + 1) * half_rows] = q_ref[token_at, q_at]
            cot_rows[h * half_rows : (h + 1) * half_rows] = cot_ref[token_at, q_at]
        if half == 1:
            dk_sum[...] = jnp.zeros_like(dk_sum)
            dv_sum[...] = jnp.zeros_like(dv_sum)

        def tile(c, plane, side):
            block = kv_all[
                plane, :, :, c, side * half_rows : (side + 1) * half_rows, cols
            ]
            return block.reshape(4 * half_rows, HD)

        def score_turn(plane, side, carry, edge):
            top, total = carry
            s = dot(tile(0, plane, side), q_rows[...], 1, 1) * to_exp2
            if edge:
                r = lax.broadcasted_iota(jnp.int32, s.shape, 0)
                q = lax.broadcasted_iota(jnp.int32, s.shape, 1) % half_rows
                j, mine = r // half_rows, 2 * y + x
                if side:
                    j, mine = 3 - j, 3 - mine
                s = jnp.where(j * half_rows + r % half_rows <= mine * half_rows + q, s, NEGATIVE)
            higher = jnp.maximum(top, jnp.max(s, axis=0, keepdims=True))
            p = jnp.exp2(s - higher)
            short = p.astype(jnp.bfloat16)
            at = side * depth + plane
            scores[at] = short
            tops[at] = higher
            fade = jnp.exp2(top - higher)
            acc[...] = acc[...] * fade + dot(tile(1, plane, side), short, 0, 0)
            return higher, total * fade + jnp.sum(p, axis=0, keepdims=True)

        acc[...] = jnp.zeros_like(acc)
        start = (jnp.full((1, q_count), NEGATIVE, jnp.float32), jnp.zeros((1, q_count), jnp.float32))
        carry = score_turn(z, half, start, True)
        if half == 0:
            carry = lax.fori_loop(0, z, lambda t, c: score_turn(t, 0, c, False), carry)
        else:
            carry = lax.fori_loop(0, depth, lambda t, c: score_turn(t, 0, c, False), carry)
            carry = lax.fori_loop(z + 1, depth, lambda t, c: score_turn(t, 1, c, False), carry)
        top, total = carry
        inverse = 1.0 / total
        out_t = acc[...] * inverse
        out_rows = out_t.T.astype(jnp.bfloat16)
        cot_t = cot_rows[...].astype(jnp.float32).T
        delta = jnp.sum(
            cot_t * out_t.astype(jnp.bfloat16).astype(jnp.float32), axis=0, keepdims=True
        )
        acc[...] = jnp.zeros_like(acc)

        def grad_turn(plane, side):
            at = side * depth + plane
            w = scores[at].astype(jnp.float32) * (jnp.exp2(tops[at] - top) * inverse)
            d_prob = dot(tile(1, plane, side), cot_rows[...], 1, 1)
            d_score = (w * (d_prob - delta)).astype(jnp.bfloat16)
            acc[...] += dot(tile(0, plane, side), d_score, 0, 0)
            dk_sum[at] += dot(d_score, q_rows[...], 1, 0)
            dv_sum[at] += dot(w.astype(jnp.bfloat16), cot_rows[...], 1, 0)

        if half == 0:
            pl.loop(0, z + 1)(lambda t: grad_turn(t, 0))
        else:
            pl.loop(0, depth)(lambda t: grad_turn(t, 0))
            pl.loop(z, depth)(lambda t: grad_turn(t, 1))
        dq_rows = (acc[...] * scale).T.astype(jnp.bfloat16)
        for h in range(group_size):
            q_at = slice(head * group_cols + h * HD, head * group_cols + (h + 1) * HD)
            attn_ref[token_at, q_at] = out_rows[h * half_rows : (h + 1) * half_rows]
            dq_ref[token_at, q_at] = dq_rows[h * half_rows : (h + 1) * half_rows]
        if half == 0:
            for side in range(2):
                key_at = slice(side * half_rows, (side + 1) * half_rows)

                @pl.loop(0, depth)
                def _(plane):
                    at = side * depth + plane
                    for c, (ref, by) in enumerate(((dk_sum, scale), (dv_sum, 1.0))):
                        block = (ref[at] * by).astype(jnp.bfloat16)
                        terms[plane, :, :, c, key_at, cols] = block.reshape(2, 2, half_rows, HD)

    stores = []

    def store(src, dst):
        copy = pltpu.make_async_copy(src, dst, store_sem.at[len(stores)])
        copy.start()
        stores.append(copy)

    @pl.loop(0, groups)
    def _(group):
        forward(group, 0)

    turn(gathers[0])

    @pl.loop(0, groups)
    def _(group):
        forward(groups - 1 - group, 1)

    back = spread(
        count, me, lambda p: mixed_all.at[p], lambda p: mixed_back.at[:, columns(p, own_cols)],
        b_send, b_recv,
    )
    turn(gathers[0], depth - 2)
    turn(gathers[1])
    finish(gathers[0])
    turn(gathers[1])
    for copy in loads.values():
        copy.wait()
    attend(0, 1)
    turn(gathers[1], depth - 1)
    settle(back)
    norm()
    d_mixed = spread(
        count, me, lambda p: dm_ref.at[:, columns(p, own_cols)], lambda p: dm_all.at[p],
        p_send, p_recv,
    )
    store(ssm_ref, ssm_out)
    store(gate_grad, gate_out)
    turn(gathers[1])
    attend(0, 0)
    turn(gathers[1])
    attend(1, 1)
    turn(gathers[1])
    attend(1, 0)
    turn(scatters[0])
    finish(gathers[1])
    settle(d_mixed)
    state[...] = jnp.zeros_like(state)

    @pl.loop(0, groups)
    def _(group):
        backward(group, 1)

    turn(scatters[0], 2)

    @pl.loop(0, groups)
    def _(group):
        backward(groups - 1 - group, 0)

    over = remote(map_terms.at[1 - core], map_in, t_send.at[1], t_recv.at[1], tp=1 - core)
    over.start()
    sent_back = spread(
        count, me, lambda p: mixed_all.at[p], lambda p: input_back.at[:, columns(p, own_cols)],
        i_send, i_recv,
    )
    turn(scatters[0], depth - 2)
    over.wait_recv()

    @pl.loop(0, count)
    def _(d):
        map_in[d] = (
            map_in[d].astype(jnp.float32) + map_terms[core, d].astype(jnp.float32)
        ).astype(jnp.bfloat16)

    map_pieces = spread(
        count, me, lambda p: map_in.at[p], lambda p: map_back.at[p], map_send, map_recv
    )
    attend(2, 1)
    turn(scatters[0], 2)
    attend(2, 0)
    turn(scatters[0], depth - 2)
    attend(3, 1)
    finish(scatters[0])
    attend(3, 0)
    turn(scatters[1])
    store(attn_ref, attn_out)
    store(dq_ref, query_out)
    settle(map_pieces)
    total = map_back[0].astype(jnp.float32)
    for d in range(1, count):
        total = total + map_back[d].astype(jnp.float32)
    map_mine[...] = total
    other = remote(map_mine, map_theirs, t_send.at[2], t_recv.at[2], tp=1 - core)
    other.start()
    turn(scatters[1], depth)
    settle(sent_back)

    @pl.loop(0, tok_rows // strip)
    def _(r):
        at = pl.ds(pl.multiple_of(r * strip, strip), strip)
        for c in range(channels // wide_cols):
            cols = slice(c * wide_cols, (c + 1) * wide_cols)
            input_ref[at, cols] = (
                input_back[at, cols].astype(jnp.float32) + dm_wide[at, cols]
            ).astype(jnp.bfloat16)

    store(input_ref, input_out)
    turn(scatters[1], depth)
    other.wait_recv()
    first = core == 0
    write_out[...] = jnp.where(first, map_mine[...], map_theirs[...])
    read_out[...] = jnp.where(first, map_theirs[...], map_mine[...])
    other.wait_send()
    over.wait_send()
    finish(scatters[1])
    for copy in stores:
        copy.wait()


def both_layers_direct(
    ssm_input, ssm_gate, state_write, state_read, log_decay, skip_gain, norm_gain, ssm_cotangent,
    queries, key_states, value_states, attn_cotangent,
):
    tok_rows, channel_count = ssm_input.shape
    head_count = log_decay.shape[1]
    head_dim = channel_count // head_count
    count = lax.axis_size("ctx")
    own_cols = channel_count // count
    size = state_write.shape[1]
    kv_cols = key_states.shape[1]
    depth = count // 4
    steps = count * tok_rows // CHUNK
    q_count = queries.shape[1] // (kv_cols // HD) // HD * tok_rows // 2
    decay_rows = jnp.repeat(log_decay.T, head_dim // own_cols, axis=0)
    skip = jnp.repeat(skip_gain, head_dim)[None, :]
    short, full = jnp.bfloat16, jnp.float32
    hbm = pl.BlockSpec(memory_space=pl.ANY)
    vmem = pl.BlockSpec(memory_space=pltpu.VMEM)
    dma = pltpu.SemaphoreType.DMA
    big = jax.ShapeDtypeStruct(ssm_input.shape, short)
    grad = jax.ShapeDtypeStruct(state_write.shape, full)
    small = jax.ShapeDtypeStruct(key_states.shape, short)
    wide = pltpu.VMEM(ssm_input.shape, short)
    by_channel = pltpu.VMEM((count, tok_rows, own_cols), short)
    map_shape = (count, tok_rows, size)
    square = pltpu.VMEM((tok_rows, size), full)
    pairs, part = 2, kv_cols // 2
    n_gather, n_scatter = gather_copies(depth), scatter_copies(depth)
    return pl.pallas_call(
        layers_kernel,
        in_specs=[hbm] * 5 + [vmem] * 2 + [hbm] * 5,
        out_specs=(hbm, hbm, hbm, vmem, vmem, hbm, hbm, vmem, vmem),
        out_shape=(big, big, big, grad, grad, big, big, small, small),
        scratch_shapes=[
            wide, wide, wide, wide, wide, pltpu.VMEM((tok_rows, size), short),
            pltpu.VMEM((count, tok_rows), full),
            pltpu.VMEM((steps, CHUNK), full),
            pltpu.VMEM((size, own_cols), full),
            pltpu.VMEM((steps, size, own_cols), short),
            by_channel,
            pltpu.VMEM((2, depth, 2, 2, tok_rows, size), short),
            by_channel, wide,
            pltpu.VMEM((2, tok_rows, HD), full),
            pltpu.VMEM((2, tok_rows, HD), full),
            wide,
            pltpu.VMEM(ssm_input.shape, full),
            by_channel, wide,
            pltpu.VMEM((2,) + map_shape, short),
            pltpu.VMEM(map_shape, short),
            pltpu.VMEM(map_shape, short),
            square, square,
            pltpu.VMEM((depth, 2, 2, 2, tok_rows, kv_cols), short),
            pltpu.VMEM((depth, 2, 2, 2, tok_rows, kv_cols), short),
            pltpu.VMEM((pairs, 2, depth, 2, tok_rows, part), short),
            pltpu.VMEM((pairs, 2, depth, tok_rows, part), short),
            pltpu.VMEM((pairs, 2, depth - 1, tok_rows, part), short),
            pltpu.VMEM((2 * depth, 2 * tok_rows, q_count), short),
            pltpu.VMEM((2 * depth, 1, q_count), full),
            pltpu.VMEM((2 * depth, 2 * tok_rows, HD), full),
            pltpu.VMEM((2 * depth, 2 * tok_rows, HD), full),
            pltpu.VMEM((q_count, HD), short),
            pltpu.VMEM((q_count, HD), short),
            pltpu.VMEM((HD, q_count), full),
            wide, wide, wide, wide, wide,
            dma((count,)), dma((count,)), dma((count,)), dma((count,)), dma((count,)),
            dma((count,)), dma((depth + 3,)), dma((depth + 3,)), dma((count,)), dma((count,)),
            dma((count,)), dma((count,)), dma((count,)), dma((count,)),
            dma((pairs, n_gather)), dma((pairs, n_gather)), dma((pairs, 2)),
            dma((pairs, n_scatter)), dma((pairs, n_scatter)),
            dma((3,)), dma((3,)), dma((6,)), dma((5,)),
        ],
        compiler_params=pltpu.CompilerParams(
            collective_id=0, has_side_effects=True, vmem_limit_bytes=VMEM_LARGE
        ),
        cost_estimate=pl.CostEstimate(
            flops=10**10, bytes_accessed=32 * 1024 * 1024, transcendentals=10**7
        ),
        name="both_layers",
    )(
        ssm_input, ssm_gate, state_write, state_read, decay_rows, skip, norm_gain[None, :],
        ssm_cotangent, queries, key_states, value_states, attn_cotangent,
    )


def direct(mesh):
    count = mesh.shape["ctx"]
    return mesh.shape["tp"] == 2 and count % 4 == 0 and count >= 8 and CH // 2 // count % HD == 0


def solution(mesh):
    placed = (
        P("ctx", "tp"),
        P("ctx", "tp"),
        P("ctx", None),
        P("ctx", None),
        P("ctx", "tp"),
        P("tp"),
        P("tp"),
        P("ctx", "tp"),
        P("ctx", "tp"),
        P("ctx", "tp"),
        P("ctx", "tp"),
        P("ctx", "tp"),
    )
    return jax.shard_map(
        both_layers_direct if direct(mesh) else both_layers,
        mesh=mesh,
        in_specs=placed,
        out_specs=(
            P("ctx", "tp"),
            P("ctx", "tp"),
            P("ctx", "tp"),
            P("ctx", None),
            P("ctx", None),
            P("ctx", "tp"),
            P("ctx", "tp"),
            P("ctx", "tp"),
            P("ctx", "tp"),
        ),
        check_vma=False,
    )
```

```python
import functools

import jax
import jax.numpy as jnp
from jax import lax
from jax.experimental import pallas as pl
from jax.experimental.pallas import tpu as pltpu
from jax.sharding import PartitionSpec as P

HD = 128
CH = 8192
PRECISE = lax.Precision.HIGHEST
NEGATIVE = -1e30
EPSILON = 1e-05
TILE_KEYS = 256
CHUNK = 256
VMEM_BYTES = 48 * 1024 * 1024
VMEM_LARGE = 58 * 1024 * 1024
GATHER_UNITS = ((0, 1), (2, 3))
SCATTER_UNITS = ((0, 1), (2,), (3,))


def dot(a, b, a_dim, b_dim):
    return lax.dot_general(
        a, b, (((a_dim,), (b_dim,)), ((), ())), preferred_element_type=jnp.float32
    )


def attention_kernel(
    place_ref, q_ref, kv_ref, cot_ref, out_ref, dq_ref, dkv_ref,
    keys, values, dk_sum, dv_sum, scores, q_rows, cot_rows, acc,
):
    count, _, _, half_rows, _ = kv_ref.shape
    group = q_ref.shape[1] // HD
    rows = group * half_rows
    scale = HD ** (-0.5)
    place = place_ref[0]
    for j in range(count):
        near = pl.ds(j * half_rows, half_rows)
        far = pl.ds((2 * count - 1 - j) * half_rows, half_rows)
        keys[near] = kv_ref[j, 0, 0]
        keys[far] = kv_ref[j, 0, 1]
        values[near] = kv_ref[j, 1, 0]
        values[far] = kv_ref[j, 1, 1]
    dk_sum[...] = jnp.zeros_like(dk_sum)
    dv_sum[...] = jnp.zeros_like(dv_sum)
    for half in range(2):
        block = place if half == 0 else 2 * count - 1 - place
        tiles = block // (TILE_KEYS // half_rows) + 1
        for h in range(group):
            there = (pl.ds(half * half_rows, half_rows), pl.ds(h * HD, HD))
            q_rows[pl.ds(h * half_rows, half_rows)] = q_ref[there]
            cot_rows[pl.ds(h * half_rows, half_rows)] = cot_ref[there]
        q_pos = block * half_rows + lax.broadcasted_iota(jnp.int32, (1, rows), 1) % half_rows

        def score_turn(tile, top):
            at = pl.ds(pl.multiple_of(tile * TILE_KEYS, TILE_KEYS), TILE_KEYS)
            s = dot(keys[at], q_rows[...], 1, 1) * scale
            key_pos = tile * TILE_KEYS + lax.broadcasted_iota(jnp.int32, s.shape, 0)
            s = jnp.where(key_pos <= q_pos, s, NEGATIVE)
            scores[at] = s
            return jnp.maximum(top, jnp.max(s, axis=0, keepdims=True))

        top = lax.fori_loop(0, tiles, score_turn, jnp.full((1, rows), NEGATIVE, jnp.float32))
        acc[...] = jnp.zeros_like(acc)

        def value_turn(tile, total):
            at = pl.ds(pl.multiple_of(tile * TILE_KEYS, TILE_KEYS), TILE_KEYS)
            p = jnp.exp(scores[at] - top)
            scores[at] = p
            acc[...] += dot(values[at], p.astype(jnp.bfloat16), 0, 0)
            return total + jnp.sum(p, axis=0, keepdims=True)

        total = lax.fori_loop(0, tiles, value_turn, jnp.zeros((1, rows), jnp.float32))
        inverse = 1.0 / total
        out_t = acc[...] * inverse
        out_rows = out_t.T.astype(jnp.bfloat16)
        cot_t = cot_rows[...].astype(jnp.float32).T
        delta = jnp.sum(
            cot_t * out_t.astype(jnp.bfloat16).astype(jnp.float32), axis=0, keepdims=True
        )
        acc[...] = jnp.zeros_like(acc)

        def grad_turn(tile, carry):
            at = pl.ds(pl.multiple_of(tile * TILE_KEYS, TILE_KEYS), TILE_KEYS)
            w = scores[at] * inverse
            d_prob = dot(values[at], cot_rows[...], 1, 1)
            d_score = (w * (d_prob - delta) * scale).astype(jnp.bfloat16)
            acc[...] += dot(keys[at], d_score, 0, 0)
            dk_sum[at] += dot(d_score, q_rows[...], 1, 0)
            dv_sum[at] += dot(w.astype(jnp.bfloat16), cot_rows[...], 1, 0)
            return carry

        lax.fori_loop(0, tiles, grad_turn, 0)
        dq_rows = acc[...].T.astype(jnp.bfloat16)
        for h in range(group):
            there = (pl.ds(half * half_rows, half_rows), pl.ds(h * HD, HD))
            out_ref[there] = out_rows[h * half_rows : (h + 1) * half_rows]
            dq_ref[there] = dq_rows[h * half_rows : (h + 1) * half_rows]
    for j in range(count):
        near = pl.ds(j * half_rows, half_rows)
        far = pl.ds((2 * count - 1 - j) * half_rows, half_rows)
        dkv_ref[j, 0, 0] = dk_sum[near].astype(jnp.bfloat16)
        dkv_ref[j, 0, 1] = dk_sum[far].astype(jnp.bfloat16)
        dkv_ref[j, 1, 0] = dv_sum[near].astype(jnp.bfloat16)
        dkv_ref[j, 1, 1] = dv_sum[far].astype(jnp.bfloat16)


def attention_core(queries, kv_all, attn_cotangent, place):
    tok_rows, q_cols = queries.shape
    count, _, _, half_rows, kv_cols = kv_all.shape
    kv_heads = kv_cols // HD
    width = q_cols // kv_heads
    rows = width // HD * half_rows
    total = count * tok_rows
    wide = pl.BlockSpec((tok_rows, width), lambda g, place: (0, g))
    pair = pl.BlockSpec((count, 2, 2, half_rows, HD), lambda g, place: (0, 0, 0, 0, g))
    like_q = jax.ShapeDtypeStruct(queries.shape, jnp.bfloat16)
    flops = 7 * 2 * tok_rows * q_cols * total // 2
    return pl.pallas_call(
        attention_kernel,
        out_shape=(like_q, like_q, jax.ShapeDtypeStruct(kv_all.shape, jnp.bfloat16)),
        grid_spec=pltpu.PrefetchScalarGridSpec(
            num_scalar_prefetch=1,
            grid=(kv_heads,),
            in_specs=[wide, pair, wide],
            out_specs=(wide, wide, pair),
            scratch_shapes=[
                pltpu.VMEM((total, HD), jnp.bfloat16),
                pltpu.VMEM((total, HD), jnp.bfloat16),
                pltpu.VMEM((total, HD), jnp.float32),
                pltpu.VMEM((total, HD), jnp.float32),
                pltpu.VMEM((total, rows), jnp.float32),
                pltpu.VMEM((rows, HD), jnp.bfloat16),
                pltpu.VMEM((rows, HD), jnp.bfloat16),
                pltpu.VMEM((HD, rows), jnp.float32),
            ],
        ),
        compiler_params=pltpu.CompilerParams(vmem_limit_bytes=VMEM_BYTES),
        cost_estimate=pl.CostEstimate(
            flops=3 * flops, bytes_accessed=16 * 1024 * 1024, transcendentals=total * q_cols // 2
        ),
        name="attention_both",
    )(place.reshape(1).astype(jnp.int32), queries, kv_all, attn_cotangent)


def gather_pair(kv):
    _, tok_rows, kv_cols = kv.shape
    return lax.all_gather(kv, "ctx", axis=0).reshape(
        lax.axis_size("ctx"), 2, 2, tok_rows // 2, kv_cols
    )


def scatter_pair(dkv):
    count, _, _, half_rows, kv_cols = dkv.shape
    mine = lax.psum_scatter(
        dkv.reshape(count, 2, 2 * half_rows, kv_cols), "ctx", scatter_dimension=0, tiled=False
    )
    return (mine[0], mine[1])


def in_order(ref, step, steps):
    pieces = ref.shape[0]
    early = step < steps // 2
    return [ref[jnp.where(early, j, pieces - 1 - j)] for j in range(pieces)]


def put_in_order(ref, value, step, steps):
    pieces, rows = ref.shape[0], ref.shape[1]
    early = step < steps // 2
    for j in range(pieces):
        ref[jnp.where(early, j, pieces - 1 - j)] = value[j * rows : (j + 1) * rows].astype(
            ref.dtype
        )


def whole(ref, step, steps):
    return jnp.concatenate(in_order(ref, step, steps), axis=0)


def causal_decay(col, row, flip):
    shape = (col.shape[0], row.shape[1])
    down = lax.broadcasted_iota(jnp.int32, shape, 0)
    across = lax.broadcasted_iota(jnp.int32, shape, 1)
    if flip:
        return jnp.exp(jnp.where(across >= down, row - col, NEGATIVE))
    return jnp.exp(jnp.where(down >= across, col - row, NEGATIVE))


def forward_kernel(steps, x_ref, b_ref, c_ref, col_ref, row_ref, mixed_ref, state_ref, state):
    step = pl.program_id(0)

    @pl.when(step == 0)
    def _():
        state[...] = jnp.zeros_like(state)

    x = whole(x_ref, step, steps)
    b = whole(b_ref, step, steps)
    c = whole(c_ref, step, steps)
    col, row = col_ref[...], row_ref[0]
    last = col[CHUNK - 1 : CHUNK]
    weights = (causal_decay(col, row, False) * dot(c, b, 1, 1)).astype(jnp.bfloat16)
    entering = state[...]
    entering_short = entering.astype(jnp.bfloat16)
    state_ref[0] = entering_short
    mixed = dot(weights, x, 1, 0) + jnp.exp(col) * dot(c, entering_short, 1, 0)
    put_in_order(mixed_ref, mixed, step, steps)
    shrunk = (b.astype(jnp.float32) * jnp.exp(last - col)).astype(jnp.bfloat16)
    state[...] = jnp.exp(last) * entering + dot(shrunk, x, 0, 0)


def backward_kernel(
    steps, x_ref, dm_ref, b_ref, c_ref, col_ref, row_ref, state_ref,
    input_ref, write_ref, read_ref, adjoint,
):
    step = steps - 1 - pl.program_id(0)

    @pl.when(pl.program_id(0) == 0)
    def _():
        adjoint[...] = jnp.zeros_like(adjoint)

    x = whole(x_ref, step, steps)
    dm = whole(dm_ref, step, steps)
    b = whole(b_ref, step, steps)
    c = whole(c_ref, step, steps)
    col, row = col_ref[...], row_ref[0]
    last = col[CHUNK - 1 : CHUNK]
    shrink, grow = jnp.exp(last - col), jnp.exp(col)
    entering = adjoint[...]
    entering_short = entering.astype(jnp.bfloat16)
    decay_t = causal_decay(col, row, True)
    weights_t = (decay_t * dot(b, c, 1, 1)).astype(jnp.bfloat16)
    input_g = dot(weights_t, dm, 1, 0) + shrink * dot(b, entering_short, 1, 0)
    put_in_order(input_ref, input_g, step, steps)
    pairs_t = (decay_t * dot(x, dm, 1, 1)).astype(jnp.bfloat16)
    write_g = dot(pairs_t, c, 1, 0) + shrink * dot(x, entering_short, 1, 1)
    pairs = (causal_decay(col, row, False) * dot(dm, x, 1, 1)).astype(jnp.bfloat16)
    read_g = dot(pairs, b, 1, 0) + grow * dot(dm, state_ref[0], 1, 1)
    put_in_order(write_ref, write_g, step, steps)
    put_in_order(read_ref, read_g, step, steps)
    grown = (c.astype(jnp.float32) * grow).astype(jnp.bfloat16)
    adjoint[...] = jnp.exp(last) * entering + dot(grown, dm, 0, 0)


def ssm_specs(count, half_rows, steps, order):
    per = CHUNK // half_rows

    def rows_spec(cols):
        def place(i):
            step = order(i)
            early = step < steps // 2
            return (
                jnp.where(early, step, steps - 1 - step), jnp.where(early, 0, 1), 0, 0
            )

        return pl.BlockSpec((per, pl.Squeezed(), half_rows, cols), place)

    return (
        rows_spec,
        pl.BlockSpec((CHUNK, 1), lambda i: (order(i), 0)),
        pl.BlockSpec((1, 1, CHUNK), lambda i: (order(i), 0, 0)),
    )


def scan_forward(x, b, c, col, row):
    count, _, half_rows, cols = x.shape
    states = b.shape[-1]
    steps = count * 2 * half_rows // CHUNK
    rows_spec, col_spec, row_spec = ssm_specs(count, half_rows, steps, lambda i: i)
    return pl.pallas_call(
        functools.partial(forward_kernel, steps),
        grid=(steps,),
        in_specs=[rows_spec(cols), rows_spec(states), rows_spec(states), col_spec, row_spec],
        out_specs=(rows_spec(cols), pl.BlockSpec((1, states, cols), lambda i: (i, 0, 0))),
        out_shape=(
            jax.ShapeDtypeStruct(x.shape, jnp.bfloat16),
            jax.ShapeDtypeStruct((steps, states, cols), jnp.bfloat16),
        ),
        scratch_shapes=[pltpu.VMEM((states, cols), jnp.float32)],
        compiler_params=pltpu.CompilerParams(vmem_limit_bytes=VMEM_BYTES),
        cost_estimate=pl.CostEstimate(
            flops=10**9, bytes_accessed=6 * 1024 * 1024, transcendentals=5 * 10**5
        ),
        name="scan_forward",
    )(x, b, c, col, row)


def scan_backward(x, dm, b, c, col, row, state):
    count, _, half_rows, cols = x.shape
    states = b.shape[-1]
    steps = count * 2 * half_rows // CHUNK
    rows_spec, col_spec, row_spec = ssm_specs(
        count, half_rows, steps, lambda i: steps - 1 - i
    )
    return pl.pallas_call(
        functools.partial(backward_kernel, steps),
        grid=(steps,),
        in_specs=[
            rows_spec(cols), rows_spec(cols), rows_spec(states), rows_spec(states),
            col_spec, row_spec,
            pl.BlockSpec((1, states, cols), lambda i: (steps - 1 - i, 0, 0)),
        ],
        out_specs=(rows_spec(cols), rows_spec(states), rows_spec(states)),
        out_shape=(
            jax.ShapeDtypeStruct(x.shape, jnp.bfloat16),
            jax.ShapeDtypeStruct(b.shape, jnp.bfloat16),
            jax.ShapeDtypeStruct(b.shape, jnp.bfloat16),
        ),
        scratch_shapes=[pltpu.VMEM((states, cols), jnp.float32)],
        compiler_params=pltpu.CompilerParams(vmem_limit_bytes=VMEM_BYTES),
        cost_estimate=pl.CostEstimate(
            flops=2 * 10**9, bytes_accessed=6 * 1024 * 1024, transcendentals=10**6
        ),
        name="scan_backward",
    )(x, dm, b, c, col, row, state)


def to_channels(values, extra=None):
    count = lax.axis_size("ctx")
    parts = values.reshape(values.shape[0], count, -1)
    if extra is not None:
        shape = (values.shape[0], count, extra.shape[1])
        parts = jnp.concatenate([parts, jnp.broadcast_to(extra[:, None, :], shape)], axis=2)
    blocks = jnp.transpose(parts, (1, 0, 2))
    return lax.all_to_all(blocks, "ctx", split_axis=0, concat_axis=0)


def to_owners(blocks):
    return lax.all_to_all(blocks, "ctx", split_axis=0, concat_axis=0)


def side_by_side(blocks):
    return jnp.transpose(blocks, (1, 0, 2)).reshape(blocks.shape[1], -1)


def from_other_core(values):
    return lax.ppermute(values, "tp", [(0, 1), (1, 0)])


def both_layers(
    ssm_input, ssm_gate, state_write, state_read, log_decay, skip_gain, norm_gain, ssm_cotangent,
    queries, key_states, value_states, attn_cotangent,
):
    tok_rows, channel_count = ssm_input.shape
    head_count = log_decay.shape[1]
    half_rows = tok_rows // 2
    head_dim = channel_count // head_count
    count = lax.axis_size("ctx")
    own_cols = channel_count // count
    states = state_write.shape[1]
    folded = (count, 2, half_rows)
    share_maps = lax.axis_size("tp") == 2
    kv = jnp.stack([key_states, value_states])
    kv, sent_input, log_decay = lax.optimization_barrier((kv, ssm_input, log_decay))
    kv_all = gather_pair(kv)
    if share_maps:
        first = lax.axis_index("tp") == 0
        arrived = to_channels(sent_input, jnp.where(first, state_write, state_read))
        own_map = arrived[:, :, own_cols:]
        other_map = from_other_core(own_map)
        b_all = jnp.where(first, own_map, other_map).reshape(*folded, states)
        c_all = jnp.where(first, other_map, own_map).reshape(*folded, states)
    else:
        arrived = to_channels(sent_input, jnp.concatenate([state_write, state_read], axis=1))
        b_all = arrived[:, :, own_cols : own_cols + states].reshape(*folded, states)
        c_all = arrived[:, :, own_cols + states :].reshape(*folded, states)
    x_all = arrived[:, :, :own_cols].reshape(*folded, own_cols)
    decay_rows = jnp.repeat(log_decay.T, head_dim // own_cols, axis=0)
    own_decay = to_owners(decay_rows[:, None, :]).reshape(*folded)
    ordered = jnp.concatenate([own_decay[:, 0], own_decay[::-1, 1]]).reshape(-1, CHUNK)
    upto = jnp.triu(jnp.ones((CHUNK, CHUNK), jnp.float32))
    log_total = jnp.dot(ordered, upto, precision=PRECISE)
    col = log_total.reshape(-1, 1)
    row = log_total[:, None, :]
    mixed_all, state_all = scan_forward(x_all, b_all, c_all, col, row)
    mixed_all, kv_all = lax.optimization_barrier((mixed_all, kv_all))
    attn_output, query_grad, dkv = attention_core(
        queries, kv_all, attn_cotangent, lax.axis_index("ctx")
    )
    mixed_back = to_owners(mixed_all.reshape(count, tok_rows, own_cols))
    dkv, mixed_back = lax.optimization_barrier((dkv, mixed_back))
    key_grad, value_grad = scatter_pair(dkv)
    skip = jnp.repeat(skip_gain, head_dim)[None, :]
    mixed = side_by_side(mixed_back)
    mixed = mixed.astype(jnp.float32) + skip * ssm_input.astype(jnp.float32)
    gate = ssm_gate.astype(jnp.float32)
    sigmoid = jax.nn.sigmoid(gate)
    gated = mixed * gate * sigmoid
    d_normed = ssm_cotangent.astype(jnp.float32) * norm_gain
    sums = lax.psum(
        jnp.stack([jnp.sum(gated * gated, axis=1), jnp.sum(d_normed * gated, axis=1)]), "tp"
    )
    root_mean = jnp.sqrt(sums[0] / CH + EPSILON)[:, None]
    inner_mean = (sums[1] / CH)[:, None] / root_mean
    normed = gated / root_mean
    ssm_output = (normed * norm_gain).astype(jnp.bfloat16)
    d_gated = (d_normed - normed * inner_mean) / root_mean
    d_mixed = d_gated * gate * sigmoid
    gate_grad = (d_gated * mixed * sigmoid * (1.0 + gate * (1.0 - sigmoid))).astype(jnp.bfloat16)
    dm_all = to_channels(d_mixed.astype(jnp.bfloat16)).reshape(*folded, own_cols)
    input_all, write_all, read_all = scan_backward(
        x_all, dm_all, b_all, c_all, col, row, state_all
    )
    blocks = (count, tok_rows)
    input_all = input_all.reshape(*blocks, own_cols)
    write_all, read_all = write_all.reshape(*blocks, states), read_all.reshape(*blocks, states)
    if share_maps:
        kept = jnp.where(first, write_all, read_all)
        passed = from_other_core(jnp.where(first, read_all, write_all))
        maps_all = (kept.astype(jnp.float32) + passed.astype(jnp.float32)).astype(jnp.bfloat16)
    else:
        maps_all = jnp.concatenate([write_all, read_all], axis=2)
    back = to_owners(jnp.concatenate([input_all, maps_all], axis=2))
    input_g = side_by_side(back[:, :, :own_cols]).astype(jnp.float32)
    input_grad = (input_g + skip * d_mixed).astype(jnp.bfloat16)
    maps = jnp.sum(back[:, :, own_cols:].astype(jnp.float32), axis=0)
    if share_maps:
        other = from_other_core(maps)
        write_grad, read_grad = jnp.where(first, maps, other), jnp.where(first, other, maps)
    else:
        maps = lax.psum(maps.astype(jnp.bfloat16), "tp").astype(jnp.float32)
        write_grad, read_grad = maps[:, :states], maps[:, states:]
    return (
        ssm_output, input_grad, gate_grad, write_grad, read_grad,
        attn_output, query_grad, key_grad, value_grad,
    )


MESH = pl.DeviceIdType.MESH


def remote(src, dst, send, recv, **to):
    return pltpu.make_async_remote_copy(
        src_ref=src, dst_ref=dst, send_sem=send, recv_sem=recv,
        device_id=to, device_id_type=MESH,
    )


def ring(at, step, size):
    return lax.rem(at + step, size)


def spot():
    me = lax.axis_index("ctx")
    return me, lax.div(me, 4), lax.rem(lax.div(me, 2), 2), lax.rem(me, 2)


def greet(count, me, core=None):
    barrier = pltpu.get_barrier_semaphore()
    for k in range(1, count):
        pl.semaphore_signal(
            barrier, inc=1, device_id={"ctx": ring(me, k, count)}, device_id_type=MESH
        )
    if core is not None:
        pl.semaphore_signal(barrier, inc=1, device_id={"tp": 1 - core}, device_id_type=MESH)
    pl.semaphore_wait(barrier, count - 1 if core is None else count)


def columns(p, width):
    return pl.ds(pl.multiple_of(p * width, width), width)


def cube_peer(k, cube):
    bits = [1 - at if k & bit else at for at, bit in zip(cube, (4, 2, 1))]
    return bits[0] * 4 + bits[1] * 2 + bits[2]


def spread(base, cube, pick, place, send, recv):
    mine = cube_peer(0, cube)
    copies = []
    for k in (7, 4, 2, 1, 6, 5, 3):
        p = cube_peer(k, cube)
        copy = remote(pick(p), place(mine), send.at[k], recv.at[k], ctx=base + p)
        copy.start()
        copies.append(copy)
    local = pltpu.make_async_copy(pick(mine), place(mine), send.at[0])
    local.start()
    return local, copies


def settle(pieces):
    local, copies = pieces
    for copy in copies:
        copy.wait_recv()
    for copy in copies:
        copy.wait_send()
    local.wait()


def index_of(z, y, x):
    return z * 4 + y * 2 + x


def gather_turns(own, dest, cols, where, send, recv, local):
    _, z, y, x = where
    depth = dest.shape[0]
    used = []

    def post(src, dst, to):
        copy = remote(src, dst, send.at[len(used)], recv.at[len(used)], ctx=to)
        copy.start()
        used.append(copy)
        return copy

    def block(at, c):
        return dest.at[at, y, x, c, :, cols]

    mine = [
        pltpu.make_async_copy(own[c].at[:, cols], block(z, c), local.at[c]) for c in range(2)
    ]
    for copy in mine:
        copy.start()
    over_x, over_y = index_of(z, y, 1 - x), index_of(z, 1 - y, x)
    first = [
        post(own[0].at[:, cols], block(z, 0), over_x),
        post(own[1].at[:, cols], block(z, 1), over_y),
    ]
    along = {}
    for k in range(1, depth):
        to = index_of(ring(z, k, depth), y, x)
        along[k] = [post(own[c].at[:, cols], block(z, c), to) for c in range(2)]
    yield
    for copy in mine:
        copy.wait()

    def pair(at, arrived):
        arrived[0].wait_recv()
        keys = dest.at[at, y, :, 0, :, cols]
        a = post(keys, keys, over_y)
        arrived[1].wait_recv()
        values = dest.at[at, :, x, 1, :, cols]
        return a, post(values, values, over_x)

    ends = list(pair(z, first))
    yield
    onward = {}
    for k in range(1, depth):
        at = ring(z, depth - k, depth)
        for copy in along[k]:
            copy.wait_recv()
        onward[k] = [post(block(at, 0), block(at, 0), over_x), post(block(at, 1), block(at, 1), over_y)]
        yield
    for k in range(1, depth):
        ends += pair(ring(z, depth - k, depth), onward[k])
        yield
    for copy in ends:
        copy.wait_recv()
    for copy in used:
        copy.wait_send()


def gather_copies(depth):
    return 2 + 2 * (depth - 1) * 3 + 2


def scatter_turns(terms, cols, out, half_way, next_way, last_way, where, send, recv):
    _, z, y, x = where
    depth = terms.shape[0]
    used = []

    def post(src, dst, to):
        copy = remote(src, dst, send.at[len(used)], recv.at[len(used)], ctx=to)
        copy.start()
        used.append(copy)
        return copy

    def wide(value):
        return value.astype(jnp.float32)

    over_x, over_y = index_of(z, y, 1 - x), index_of(z, 1 - y, x)
    order = list(range(1, depth)) + [0]
    first, second, third = {}, {}, []
    for k in order:
        at = ring(z, k, depth)
        first[k] = (
            post(terms.at[at, 1 - y, :, 0, :, cols], half_way.at[0, at, :, :, cols], over_y),
            post(terms.at[at, :, 1 - x, 1, :, cols], half_way.at[1, at, :, :, cols], over_x),
        )
    yield
    for k in order:
        at = ring(z, k, depth)
        first[k][0].wait_recv()
        half_way[0, at, 1 - x, :, cols] = (
            wide(half_way[0, at, 1 - x, :, cols]) + wide(terms[at, y, 1 - x, 0, :, cols])
        ).astype(jnp.bfloat16)
        a = post(half_way.at[0, at, 1 - x, :, cols], next_way.at[0, at, :, cols], over_x)
        first[k][1].wait_recv()
        half_way[1, at, 1 - y, :, cols] = (
            wide(half_way[1, at, 1 - y, :, cols]) + wide(terms[at, 1 - y, x, 1, :, cols])
        ).astype(jnp.bfloat16)
        second[k] = (a, post(half_way.at[1, at, 1 - y, :, cols], next_way.at[1, at, :, cols], over_y))
        yield
    for k in order:
        at = ring(z, k, depth)
        for c in range(2):
            second[k][c].wait_recv()
            total = (
                wide(next_way[c, at, :, cols]) + wide(half_way[c, at, y if c else x, :, cols])
                + wide(terms[at, y, x, c, :, cols])
            )
            next_way[c, at, :, cols] = total.astype(jnp.bfloat16)
            if k:
                there = last_way.at[c, k - 1, :, cols]
                third.append(post(next_way.at[c, at, :, cols], there, index_of(at, y, x)))
        yield
    for copy in third:
        copy.wait_recv()
    for c in range(2):
        total = wide(next_way[c, z, :, cols])
        for k in range(1, depth):
            total = total + wide(last_way[c, k - 1, :, cols])
        out[c][:, cols] = total.astype(jnp.bfloat16)
    for copy in used:
        copy.wait_send()


def scatter_copies(depth):
    return 4 * depth + 2 * (depth - 1)


def running_decay(decay, rows, first, half_rows):
    per = CHUNK // half_rows
    groups = decay.shape[0] // per
    width = 2 * half_rows
    side = jnp.concatenate(
        [
            jnp.concatenate([decay[g * per + j] for g in range(groups)], axis=0)
            for j in range(per)
        ],
        axis=1,
    )
    shape = (per * width, 2 * CHUNK)
    r = lax.broadcasted_iota(jnp.int32, shape, 0)
    u = lax.broadcasted_iota(jnp.int32, shape, 1)
    j, t = r // width, r % width
    near = (t < half_rows) & (u < CHUNK) & (j * half_rows + t <= u)
    far = (t >= half_rows) & (u >= CHUNK)
    far = far & ((per - 1 - j) * half_rows + t - half_rows <= u - CHUNK)
    ones = jnp.where(near | far, 1.0, 0.0)
    sums = lax.dot_general(
        side, ones, (((1,), (0,)), ((), ())), precision=PRECISE,
        preferred_element_type=jnp.float32,
    )
    for i in range(groups):
        rows[first + i] = sums[i : i + 1, :CHUNK]
        rows[first + groups + i] = sums[i : i + 1, CHUNK:]


def members(group, half, per):
    return [per * group + (j if half == 0 else per - 1 - j) for j in range(per)]


def put_chunk(ref, ids, half, half_rows, value):
    value = value.astype(ref.dtype)
    for j, d in enumerate(ids):
        ref[d, half * half_rows : (half + 1) * half_rows] = value[
            j * half_rows : (j + 1) * half_rows
        ]


def as_column(row):
    shape = (row.shape[1], row.shape[1])
    same = lax.broadcasted_iota(jnp.int32, shape, 0) == lax.broadcasted_iota(jnp.int32, shape, 1)
    return jnp.sum(jnp.where(same, row, 0.0), axis=1, keepdims=True)


def layers_kernel(
    x_hbm, gate_hbm, write_hbm, read_hbm, decay_hbm, skip_ref, gain_ref, up_hbm,
    q_hbm, k_hbm, v_hbm, cot_hbm,
    ssm_out, input_out, gate_out, write_out, read_out, attn_out, query_out, key_out, value_out,
    x_ref, gate_ref, up_ref, q_ref, cot_ref, own_map,
    decay, rows, sums, states, summary, summary_in, fade, fade_in, x_all, maps, mixed_all, mixed_back,
    sums_mine, sums_theirs, dm_ref, dm_wide, dm_all, input_back,
    map_terms, map_in, map_back, map_mine, map_theirs,
    kv_all, terms, half_way, next_way, last_way,
    adjoints, scores, tops, dk_sum, dv_sum, q_rows, cot_rows, acc,
    ssm_ref, input_ref, gate_grad, attn_ref, dq_ref,
    x_send, x_recv, d_send, d_recv, b_send, b_recv, m_send, m_recv, i_send, i_recv,
    p_send, p_recv, map_send, map_recv, g_send, g_recv, g_local, s_send, s_recv,
    t_send, t_recv, h_send, h_recv, load_sem, store_sem,
):
    where = spot()
    me, z, y, x = where
    core = lax.axis_index("tp")
    members_count, tok_rows, own_cols = x_all.shape
    heads = decay.shape[0]
    head_dim = own_cols // heads
    channels = x_ref.shape[1]
    half_rows = tok_rows // 2
    depth = kv_all.shape[0]
    count = depth * 4
    per = CHUNK // half_rows
    groups = members_count // per
    outer, inner_z = lax.div(z, 2), lax.rem(z, 2)
    base, cube = outer * members_count, (inner_z, y, x)
    early = outer == 0
    partner = index_of(ring(z, 2, depth), y, x)
    kv_cols = k_hbm.shape[1]
    kv_heads = kv_cols // HD
    group_cols = q_ref.shape[1] // kv_heads
    group_size = group_cols // HD
    q_count = group_size * half_rows

    def unit_cols(unit):
        return slice(unit[0] * HD, unit[-1] * HD + HD)

    scale = HD ** (-0.5)
    to_exp2 = scale * 1.4426950408889634

    loads = {}
    for i, (name, src, dst) in enumerate((
        ("q", q_hbm, q_ref), ("cot", cot_hbm, cot_ref), ("x", x_hbm, x_ref),
        ("gate", gate_hbm, gate_ref), ("up", up_hbm, up_ref),
    )):
        loads[name] = pltpu.make_async_copy(src, dst, load_sem.at[i])
        loads[name].start()
    own_map_sem = load_sem.at[len(loads)]

    @pl.when(core == 0)
    def _():
        pltpu.make_async_copy(write_hbm, own_map, own_map_sem).start()

    @pl.when(core != 0)
    def _():
        pltpu.make_async_copy(read_hbm, own_map, own_map_sem).start()

    greet(count, me, core)
    decays = spread(
        base, cube, lambda p: decay_hbm.at[:, p], lambda p: decay.at[:, p],
        d_send, d_recv,
    )
    pltpu.make_async_copy(write_hbm, own_map, own_map_sem).wait()
    copy_map = pltpu.make_async_copy(own_map, maps.at[core, inner_z, y, x], m_send.at[0])
    copy_map.start()
    used = []

    def post(src, dst, **to):
        copy = remote(src, dst, m_send.at[len(used) + 1], m_recv.at[len(used) + 1], **to)
        copy.start()
        used.append(copy)
        return copy

    post(own_map, maps.at[core, inner_z, y, x], ctx=base + cube_peer(4, cube))
    inputs = spread(
        base, cube, lambda p: x_hbm.at[:, columns(p, own_cols)], lambda p: x_all.at[p],
        x_send, x_recv,
    )
    gathers = [
        gather_turns(
            (k_hbm, v_hbm), kv_all, unit_cols(unit), where, g_send.at[i], g_recv.at[i],
            g_local.at[i],
        )
        for i, unit in enumerate(GATHER_UNITS)
    ]
    scatters = [
        scatter_turns(
            terms, unit_cols(unit), (key_out, value_out), half_way, next_way, last_way, where,
            s_send.at[i], s_recv.at[i],
        )
        for i, unit in enumerate(SCATTER_UNITS)
    ]

    def turn(turns, times=1):
        for _ in range(times):
            next(turns, None)

    def finish(turns):
        for _ in turns:
            pass

    turn(gathers[0])
    for copy in used:
        copy.wait_recv()
    copy_map.wait()
    part = maps.at[core, :, y, x]
    post(part, part, ctx=index_of(z, y, 1 - x)).wait_recv()
    part = maps.at[core, :, y]
    post(part, part, ctx=index_of(z, 1 - y, x)).wait_recv()
    part = maps.at[core]
    over = post(part, part, tp=1 - core)
    turn(gathers[0])
    settle(decays)
    for h in range(heads):
        running_decay(decay.at[h], rows, h * 2 * groups, half_rows)
    over.wait_recv()
    for copy in used:
        copy.wait_send()
    settle(inputs)
    turn(gathers[1])

    def chunk_map(which, group, half):
        js = range(per) if half == 0 else range(per - 1, -1, -1)
        at = slice(half * half_rows, (half + 1) * half_rows)
        return jnp.concatenate([maps[which, group, j // 2, j % 2, at] for j in js], axis=0)

    def logs(group, half, h):
        row = rows[(h * 2 + half) * groups + group]
        col = as_column(row)
        return row, col, col[CHUNK - 1 : CHUNK]

    def of_head(h):
        return slice(h * head_dim, (h + 1) * head_dim)

    def chunk_head(ref, group, half, h):
        ids = members(group, half, per)
        return jnp.concatenate(
            [ref[d, half * half_rows : (half + 1) * half_rows, of_head(h)] for d in ids], axis=0
        )

    def put_head(ref, group, half, h, value):
        value = value.astype(ref.dtype)
        for j, d in enumerate(members(group, half, per)):
            ref[d, half * half_rows : (half + 1) * half_rows, of_head(h)] = value[
                j * half_rows : (j + 1) * half_rows
            ]

    def total_log(group, half, h):
        return rows[(h * 2 + half) * groups + group][:, CHUNK - 1 : CHUNK]

    def run_order(half):
        return (0, 1) if half == 0 else (1, 0)

    def chunk_sums(which, grow):
        source = dm_all if grow else x_all

        @pl.loop(0, groups)
        def _(group):
            for half in range(2):
                maps_here = chunk_map(which, group, half).astype(jnp.float32)
                for h in range(heads):
                    _, col, last = logs(group, half, h)
                    scaled = (maps_here * jnp.exp(col if grow else last - col)).astype(
                        jnp.bfloat16
                    )
                    sums[half, group, :, of_head(h)] = dot(
                        scaled, chunk_head(source, group, half, h), 0, 0
                    )

    def run_sum(half, h, back):
        first, then = run_order(half)[::-1] if back else run_order(half)
        return (
            jnp.exp(total_log(then, half, h)) * sums[half, first, :, of_head(h)]
            + sums[half, then, :, of_head(h)]
        )

    def run_log(half, h):
        return total_log(0, half, h) + total_log(1, half, h)

    def send_summary(slot, back):
        near, far = (1, 0) if back else (0, 1)
        for h in range(heads):
            one, two = run_sum(near, h, back), run_sum(far, h, back)
            joined = jnp.exp(run_log(far, h)) * one + two
            summary[slot, :, of_head(h)] = jnp.where(early, one, joined).astype(jnp.bfloat16)
        copy = remote(
            summary.at[slot], summary_in.at[slot], h_send.at[slot], h_recv.at[slot], ctx=partner
        )
        copy.start()
        return copy

    def entering(slot, half, h, back):
        near, far = (1, 0) if back else (0, 1)
        there = summary_in[slot, :, of_head(h)].astype(jnp.float32)
        if half == near:
            return jnp.where(early, 0.0, there)
        other = fade_in[0:1, h * HD : h * HD + 1]
        own = run_sum(near, h, back)
        return jnp.where(
            early, jnp.exp(other) * own + there, jnp.exp(run_log(near, h)) * there + own
        )

    def chunk_entering(slot, half, h, back):
        first, then = run_order(half)[::-1] if back else run_order(half)
        value = entering(slot, half, h, back)
        later = jnp.exp(total_log(first, half, h)) * value + sums[half, first, :, of_head(h)]
        return {first: value, then: later}

    def forward_within(group):
        for half in range(2):
            b, c = chunk_map(0, group, half), chunk_map(1, group, half)
            pairs_cb = dot(c, b, 1, 1)
            for h in range(heads):
                row, col, _ = logs(group, half, h)
                weights = (causal_decay(col, row, False) * pairs_cb).astype(jnp.bfloat16)
                put_head(
                    dm_wide, group, half, h,
                    dot(weights, chunk_head(x_all, group, half, h), 1, 0),
                )

    def forward_across(group):
        for half in range(2):
            c = chunk_map(1, group, half)
            for h in range(heads):
                _, col, _ = logs(group, half, h)
                across = jnp.exp(col) * dot(c, states[half, group, :, of_head(h)], 1, 0)
                put_head(
                    mixed_all, group, half, h, chunk_head(dm_wide, group, half, h) + across
                )

    def backward(group):
        for half in range(2):
            b, c = chunk_map(0, group, half), chunk_map(1, group, half)
            pairs_bc = dot(b, c, 1, 1)
            write_g = read_g = 0.0
            for h in range(heads):
                value = chunk_head(x_all, group, half, h)
                dm = chunk_head(dm_all, group, half, h)
                row, col, last = logs(group, half, h)
                shrink, grow = jnp.exp(last - col), jnp.exp(col)
                later = adjoints[half, group, :, of_head(h)]
                decay_t = causal_decay(col, row, True)
                weights_t = (decay_t * pairs_bc).astype(jnp.bfloat16)
                input_g = dot(weights_t, dm, 1, 0) + shrink * dot(b, later, 1, 0)
                put_head(mixed_all, group, half, h, input_g)
                pairs_t = (decay_t * dot(value, dm, 1, 1)).astype(jnp.bfloat16)
                write_g = write_g + dot(pairs_t, c, 1, 0) + shrink * dot(value, later, 1, 1)
                pairs_f = (causal_decay(col, row, False) * dot(dm, value, 1, 1)).astype(
                    jnp.bfloat16
                )
                state = states[half, group, :, of_head(h)]
                read_g = read_g + dot(pairs_f, b, 1, 0) + grow * dot(dm, state, 1, 1)
            ids = members(group, half, per)
            put_chunk(map_terms.at[0], ids, half, half_rows, write_g)
            put_chunk(map_terms.at[1], ids, half, half_rows, read_g)

    wide_cols = own_cols
    strip = 16

    def pieces_of(r):
        at = pl.ds(pl.multiple_of(r * strip, strip), strip)
        for c in range(channels // wide_cols):
            cols = slice(c * wide_cols, (c + 1) * wide_cols)
            gate = gate_ref[at, cols].astype(jnp.float32)
            sigmoid = 0.5 * jnp.tanh(0.5 * gate) + 0.5
            mixed = mixed_back[at, cols].astype(jnp.float32) + skip_ref[:, cols] * x_ref[
                at, cols
            ].astype(jnp.float32)
            d_normed = up_ref[at, cols].astype(jnp.float32) * gain_ref[:, cols]
            yield at, cols, gate, sigmoid, mixed, d_normed

    def norm():
        @pl.loop(0, tok_rows // strip)
        def _(r):
            squares = jnp.zeros((strip, 1), jnp.float32)
            inner = jnp.zeros((strip, 1), jnp.float32)
            for at, cols, gate, sigmoid, mixed, d_normed in pieces_of(r):
                gated = mixed * gate * sigmoid
                squares = squares + jnp.sum(gated * gated, axis=1, keepdims=True)
                inner = inner + jnp.sum(d_normed * gated, axis=1, keepdims=True)
            sums_mine[0, at] = jnp.broadcast_to(squares, (strip, HD))
            sums_mine[1, at] = jnp.broadcast_to(inner, (strip, HD))

        swap = remote(sums_mine, sums_theirs, t_send.at[0], t_recv.at[0], tp=1 - core)
        swap.start()
        swap.wait()

        @pl.loop(0, tok_rows // strip)
        def _(r):
            at = pl.ds(pl.multiple_of(r * strip, strip), strip)
            squares = sums_mine[0, at] + sums_theirs[0, at]
            inner = sums_mine[1, at] + sums_theirs[1, at]
            inverse = 1.0 / jnp.sqrt(squares[:, :1] / CH + EPSILON)
            inner_mean = inner[:, :1] / CH * inverse
            for at, cols, gate, sigmoid, mixed, d_normed in pieces_of(r):
                silu = gate * sigmoid
                normed = mixed * silu * inverse
                ssm_ref[at, cols] = (normed * gain_ref[:, cols]).astype(jnp.bfloat16)
                d_gated = (d_normed - normed * inner_mean) * inverse
                d_mixed = d_gated * silu
                dm_ref[at, cols] = d_mixed.astype(jnp.bfloat16)
                dm_wide[cols.start // wide_cols, at] = skip_ref[:, cols] * d_mixed
                gate_grad[at, cols] = (
                    d_gated * mixed * sigmoid * (1.0 + gate * (1.0 - sigmoid))
                ).astype(jnp.bfloat16)

    def attend(head, half):
        cols = slice(head * HD, (head + 1) * HD)
        token_at = slice(half * half_rows, (half + 1) * half_rows)
        for h in range(group_size):
            q_at = slice(head * group_cols + h * HD, head * group_cols + (h + 1) * HD)
            q_rows[h * half_rows : (h + 1) * half_rows] = q_ref[token_at, q_at]
            cot_rows[h * half_rows : (h + 1) * half_rows] = cot_ref[token_at, q_at]
        if half == 1:
            dk_sum[...] = jnp.zeros_like(dk_sum)
            dv_sum[...] = jnp.zeros_like(dv_sum)

        def tile(c, plane, side):
            block = kv_all[
                plane, :, :, c, side * half_rows : (side + 1) * half_rows, cols
            ]
            return block.reshape(4 * half_rows, HD)

        def score_turn(plane, side, carry, edge):
            top, total = carry
            s = dot(tile(0, plane, side), q_rows[...], 1, 1) * to_exp2
            if edge:
                r = lax.broadcasted_iota(jnp.int32, s.shape, 0)
                q = lax.broadcasted_iota(jnp.int32, s.shape, 1) % half_rows
                j, mine = r // half_rows, 2 * y + x
                if side:
                    j, mine = 3 - j, 3 - mine
                s = jnp.where(j * half_rows + r % half_rows <= mine * half_rows + q, s, NEGATIVE)
            higher = jnp.maximum(top, jnp.max(s, axis=0, keepdims=True))
            p = jnp.exp2(s - higher)
            short = p.astype(jnp.bfloat16)
            at = side * depth + plane
            scores[at] = short
            tops[at] = higher
            fade = jnp.exp2(top - higher)
            acc[...] = acc[...] * fade + dot(tile(1, plane, side), short, 0, 0)
            return higher, total * fade + jnp.sum(p, axis=0, keepdims=True)

        acc[...] = jnp.zeros_like(acc)
        start = (jnp.full((1, q_count), NEGATIVE, jnp.float32), jnp.zeros((1, q_count), jnp.float32))
        carry = score_turn(z, half, start, True)
        if half == 0:
            carry = lax.fori_loop(0, z, lambda t, c: score_turn(t, 0, c, False), carry)
        else:
            carry = lax.fori_loop(0, depth, lambda t, c: score_turn(t, 0, c, False), carry)
            carry = lax.fori_loop(z + 1, depth, lambda t, c: score_turn(t, 1, c, False), carry)
        top, total = carry
        inverse = 1.0 / total
        out_t = acc[...] * inverse
        out_rows = out_t.T.astype(jnp.bfloat16)
        cot_t = cot_rows[...].astype(jnp.float32).T
        delta = jnp.sum(
            cot_t * out_t.astype(jnp.bfloat16).astype(jnp.float32), axis=0, keepdims=True
        )
        acc[...] = jnp.zeros_like(acc)

        def grad_turn(plane, side):
            at = side * depth + plane
            w = scores[at].astype(jnp.float32) * (jnp.exp2(tops[at] - top) * inverse)
            d_prob = dot(tile(1, plane, side), cot_rows[...], 1, 1)
            d_score = (w * (d_prob - delta)).astype(jnp.bfloat16)
            acc[...] += dot(tile(0, plane, side), d_score, 0, 0)
            dk_sum[at] += dot(d_score, q_rows[...], 1, 0)
            dv_sum[at] += dot(w.astype(jnp.bfloat16), cot_rows[...], 1, 0)

        if half == 0:
            pl.loop(0, z + 1)(lambda t: grad_turn(t, 0))
        else:
            pl.loop(0, depth)(lambda t: grad_turn(t, 0))
            pl.loop(z, depth)(lambda t: grad_turn(t, 1))
        dq_rows = (acc[...] * scale).T.astype(jnp.bfloat16)
        for h in range(group_size):
            q_at = slice(head * group_cols + h * HD, head * group_cols + (h + 1) * HD)
            attn_ref[token_at, q_at] = out_rows[h * half_rows : (h + 1) * half_rows]
            dq_ref[token_at, q_at] = dq_rows[h * half_rows : (h + 1) * half_rows]
        if half == 0:
            for side in range(2):
                key_at = slice(side * half_rows, (side + 1) * half_rows)

                @pl.loop(0, depth)
                def _(plane):
                    at = side * depth + plane
                    for c, (ref, by) in enumerate(((dk_sum, scale), (dv_sum, 1.0))):
                        block = (ref[at] * by).astype(jnp.bfloat16)
                        terms[plane, :, :, c, key_at, cols] = block.reshape(2, 2, half_rows, HD)

    stores = []

    def store(src, dst):
        copy = pltpu.make_async_copy(src, dst, store_sem.at[len(stores)])
        copy.start()
        stores.append(copy)

    for h in range(heads):
        fade[:, h * HD : (h + 1) * HD] = jnp.broadcast_to(run_log(0, h) + run_log(1, h), (8, HD))
    fades = remote(fade, fade_in, h_send.at[2], h_recv.at[2], ctx=partner)
    fades.start()
    chunk_sums(0, False)
    summaries = send_summary(0, False)
    turn(gathers[0], depth - 1)
    pl.loop(0, groups)(forward_within)
    turn(gathers[0], depth - 1)
    fades.wait()
    summaries.wait()
    for half in range(2):
        for h in range(heads):
            for group, value in chunk_entering(0, half, h, False).items():
                states[half, group, :, of_head(h)] = value.astype(jnp.bfloat16)
    pl.loop(0, groups)(forward_across)
    back = spread(
        base, cube, lambda p: mixed_all.at[p], lambda p: mixed_back.at[:, columns(p, own_cols)],
        b_send, b_recv,
    )
    turn(gathers[1])
    for copy in loads.values():
        copy.wait()
    finish(gathers[0])
    attend(0, 1)
    turn(gathers[1], depth - 1)
    settle(back)
    norm()
    d_mixed = spread(
        base, cube, lambda p: dm_ref.at[:, columns(p, own_cols)], lambda p: dm_all.at[p],
        p_send, p_recv,
    )
    store(ssm_ref, ssm_out)
    store(gate_grad, gate_out)
    turn(gathers[1], depth - 1)
    attend(0, 0)
    attend(1, 1)
    settle(d_mixed)
    chunk_sums(1, True)
    summaries = send_summary(1, True)
    attend(1, 0)
    turn(scatters[0])
    finish(gathers[1])
    summaries.wait()
    for half in range(2):
        for h in range(heads):
            for group, value in chunk_entering(1, half, h, True).items():
                adjoints[half, group, :, of_head(h)] = value.astype(jnp.bfloat16)
    turn(scatters[0], 2)
    pl.loop(0, groups)(backward)
    over = remote(map_terms.at[1 - core], map_in, t_send.at[1], t_recv.at[1], tp=1 - core)
    over.start()
    sent_back = spread(
        base, cube, lambda p: mixed_all.at[p], lambda p: input_back.at[:, columns(p, own_cols)],
        i_send, i_recv,
    )
    turn(scatters[0], depth - 2)
    over.wait_recv()

    @pl.loop(0, members_count)
    def _(d):
        map_in[d] = (
            map_in[d].astype(jnp.float32) + map_terms[core, d].astype(jnp.float32)
        ).astype(jnp.bfloat16)

    map_pieces = spread(
        base, cube, lambda p: map_in.at[p], lambda p: map_back.at[p], map_send, map_recv
    )
    attend(2, 1)
    turn(scatters[0], 2)
    attend(2, 0)
    turn(scatters[1])
    turn(scatters[0], depth - 2)
    attend(3, 1)
    finish(scatters[0])
    turn(scatters[1], depth)
    attend(3, 0)
    turn(scatters[2])
    store(attn_ref, attn_out)
    store(dq_ref, query_out)
    finish(scatters[1])
    settle(map_pieces)
    total = map_back[0].astype(jnp.float32)
    for d in range(1, members_count):
        total = total + map_back[d].astype(jnp.float32)
    map_mine[...] = total
    other = remote(map_mine, map_theirs, t_send.at[2], t_recv.at[2], tp=1 - core)
    other.start()
    settle(sent_back)
    turn(scatters[2], depth)

    @pl.loop(0, tok_rows // strip)
    def _(r):
        at = pl.ds(pl.multiple_of(r * strip, strip), strip)
        for c in range(channels // wide_cols):
            cols = slice(c * wide_cols, (c + 1) * wide_cols)
            input_ref[at, cols] = (
                input_back[at, cols].astype(jnp.float32) + dm_wide[c, at]
            ).astype(jnp.bfloat16)

    store(input_ref, input_out)
    turn(scatters[2], depth)
    other.wait_recv()
    first = core == 0
    write_out[...] = jnp.where(first, map_mine[...], map_theirs[...])
    read_out[...] = jnp.where(first, map_theirs[...], map_mine[...])
    other.wait_send()
    over.wait_send()
    finish(scatters[2])
    for copy in stores:
        copy.wait()


def both_layers_direct(
    ssm_input, ssm_gate, state_write, state_read, log_decay, skip_gain, norm_gain, ssm_cotangent,
    queries, key_states, value_states, attn_cotangent,
):
    tok_rows, channel_count = ssm_input.shape
    head_count = log_decay.shape[1]
    head_dim = channel_count // head_count
    count = lax.axis_size("ctx")
    group = count // 2
    own_cols = channel_count // group
    heads = own_cols // head_dim
    size = state_write.shape[1]
    kv_cols = key_states.shape[1]
    depth = count // 4
    chunks = group * tok_rows // 2 // CHUNK
    q_count = queries.shape[1] // (kv_cols // HD) // HD * tok_rows // 2
    decay_rows = jnp.transpose(log_decay.reshape(tok_rows, group, heads), (2, 1, 0))[:, :, None]
    skip = jnp.repeat(skip_gain, head_dim)[None, :]
    short, full = jnp.bfloat16, jnp.float32
    hbm = pl.BlockSpec(memory_space=pl.ANY)
    vmem = pl.BlockSpec(memory_space=pltpu.VMEM)
    dma = pltpu.SemaphoreType.DMA
    big = jax.ShapeDtypeStruct(ssm_input.shape, short)
    grad = jax.ShapeDtypeStruct(state_write.shape, full)
    small = jax.ShapeDtypeStruct(key_states.shape, short)
    wide = pltpu.VMEM(ssm_input.shape, short)
    by_channel = pltpu.VMEM((group, tok_rows, own_cols), short)
    map_shape = (group, tok_rows, size)
    square = pltpu.VMEM((tok_rows, size), full)
    n_g, n_s = len(GATHER_UNITS), len(SCATTER_UNITS)
    n_gather, n_scatter = gather_copies(depth), scatter_copies(depth)
    results = pl.pallas_call(
        layers_kernel,
        in_specs=[hbm] * 5 + [vmem] * 2 + [hbm] * 5,
        out_specs=(hbm, hbm, hbm, vmem, vmem, hbm, hbm, vmem, vmem),
        out_shape=(big, big, big, grad, grad, big, big, small, small),
        scratch_shapes=[
            wide, wide, wide, wide, wide, pltpu.VMEM((tok_rows, size), short),
            pltpu.VMEM((heads, group, 1, tok_rows), full),
            pltpu.VMEM((heads * 2 * chunks, 1, CHUNK), full),
            pltpu.VMEM((2, chunks, size, own_cols), full),
            pltpu.VMEM((2, chunks, size, own_cols), short),
            pltpu.VMEM((2, size, own_cols), short),
            pltpu.VMEM((2, size, own_cols), short),
            pltpu.VMEM((8, heads * HD), full),
            pltpu.VMEM((8, heads * HD), full),
            by_channel,
            pltpu.VMEM((2, 2, 2, 2, tok_rows, size), short),
            by_channel, wide,
            pltpu.VMEM((2, tok_rows, HD), full),
            pltpu.VMEM((2, tok_rows, HD), full),
            wide,
            pltpu.VMEM((group, tok_rows, own_cols), full),
            by_channel, wide,
            pltpu.VMEM((2,) + map_shape, short),
            pltpu.VMEM(map_shape, short),
            pltpu.VMEM(map_shape, short),
            square, square,
            pltpu.VMEM((depth, 2, 2, 2, tok_rows, kv_cols), short),
            pltpu.VMEM((depth, 2, 2, 2, tok_rows, kv_cols), short),
            pltpu.VMEM((2, depth, 2, tok_rows, kv_cols), short),
            pltpu.VMEM((2, depth, tok_rows, kv_cols), short),
            pltpu.VMEM((2, depth - 1, tok_rows, kv_cols), short),
            pltpu.VMEM((2, chunks, size, own_cols), short),
            pltpu.VMEM((2 * depth, 2 * tok_rows, q_count), short),
            pltpu.VMEM((2 * depth, 1, q_count), full),
            pltpu.VMEM((2 * depth, 2 * tok_rows, HD), full),
            pltpu.VMEM((2 * depth, 2 * tok_rows, HD), full),
            pltpu.VMEM((q_count, HD), short),
            pltpu.VMEM((q_count, HD), short),
            pltpu.VMEM((HD, q_count), full),
            wide, wide, wide, wide, wide,
            dma((group,)), dma((group,)), dma((group,)), dma((group,)), dma((group,)),
            dma((group,)), dma((5,)), dma((5,)), dma((group,)), dma((group,)),
            dma((group,)), dma((group,)), dma((group,)), dma((group,)),
            dma((n_g, n_gather)), dma((n_g, n_gather)), dma((n_g, 2)),
            dma((n_s, n_scatter)), dma((n_s, n_scatter)),
            dma((3,)), dma((3,)), dma((3,)), dma((3,)), dma((6,)), dma((5,)),
        ],
        compiler_params=pltpu.CompilerParams(
            collective_id=0, has_side_effects=True, vmem_limit_bytes=VMEM_LARGE
        ),
        cost_estimate=pl.CostEstimate(
            flops=10**10, bytes_accessed=32 * 1024 * 1024, transcendentals=10**7
        ),
        name="both_layers",
    )(
        ssm_input, ssm_gate, state_write, state_read, decay_rows, skip, norm_gain[None, :],
        ssm_cotangent, queries, key_states, value_states, attn_cotangent,
    )
    return hand_over(results)


def hand_over_kernel(*refs):
    n = len(refs) // 3
    sources, targets, held, sems = refs[:n], refs[n : 2 * n], refs[2 * n : 3 * n], refs[-1]
    ins = [pltpu.make_async_copy(sources[i], held[i], sems.at[0, i]) for i in range(n)]
    outs = [pltpu.make_async_copy(held[i], targets[i], sems.at[1, i]) for i in range(n)]
    for copy in ins:
        copy.start()
    for i in range(n):
        ins[i].wait()
        outs[i].start()
    for copy in outs:
        copy.wait()


def hand_over(results):
    n = len(results)
    hbm = pl.BlockSpec(memory_space=pl.ANY)
    return pl.pallas_call(
        hand_over_kernel,
        in_specs=[hbm] * n,
        out_specs=(hbm,) * n,
        out_shape=tuple(jax.ShapeDtypeStruct(r.shape, r.dtype) for r in results),
        scratch_shapes=[pltpu.VMEM(r.shape, r.dtype) for r in results]
        + [pltpu.SemaphoreType.DMA((2, n))],
        compiler_params=pltpu.CompilerParams(vmem_limit_bytes=VMEM_LARGE),
        name="hand_over",
    )(*results)


def direct(mesh):
    return mesh.shape["tp"] == 2 and mesh.shape["ctx"] == 16


def solution(mesh):
    placed = (
        P("ctx", "tp"),
        P("ctx", "tp"),
        P("ctx", None),
        P("ctx", None),
        P("ctx", "tp"),
        P("tp"),
        P("tp"),
        P("ctx", "tp"),
        P("ctx", "tp"),
        P("ctx", "tp"),
        P("ctx", "tp"),
        P("ctx", "tp"),
    )
    return jax.shard_map(
        both_layers_direct if direct(mesh) else both_layers,
        mesh=mesh,
        in_specs=placed,
        out_specs=(
            P("ctx", "tp"),
            P("ctx", "tp"),
            P("ctx", "tp"),
            P("ctx", None),
            P("ctx", None),
            P("ctx", "tp"),
            P("ctx", "tp"),
            P("ctx", "tp"),
            P("ctx", "tp"),
        ),
        check_vma=False,
    )
```

```python
import functools

import jax
import jax.numpy as jnp
from jax import lax
from jax.experimental import pallas as pl
from jax.experimental.pallas import tpu as pltpu
from jax.sharding import PartitionSpec as P

HD = 128
CH = 8192
PRECISE = lax.Precision.HIGHEST
NEGATIVE = -1e30
EPSILON = 1e-05
TILE_KEYS = 256
CHUNK = 256
VMEM_BYTES = 48 * 1024 * 1024
VMEM_LARGE = 58 * 1024 * 1024
GATHER_UNITS = ((0, 1), (2, 3))
SCATTER_UNITS = ((0, 1), (2,), (3,))


def dot(a, b, a_dim, b_dim):
    return lax.dot_general(
        a, b, (((a_dim,), (b_dim,)), ((), ())), preferred_element_type=jnp.float32
    )


def attention_kernel(
    place_ref, q_ref, kv_ref, cot_ref, out_ref, dq_ref, dkv_ref,
    keys, values, dk_sum, dv_sum, scores, q_rows, cot_rows, acc,
):
    count, _, _, half_rows, _ = kv_ref.shape
    group = q_ref.shape[1] // HD
    rows = group * half_rows
    scale = HD ** (-0.5)
    place = place_ref[0]
    for j in range(count):
        near = pl.ds(j * half_rows, half_rows)
        far = pl.ds((2 * count - 1 - j) * half_rows, half_rows)
        keys[near] = kv_ref[j, 0, 0]
        keys[far] = kv_ref[j, 0, 1]
        values[near] = kv_ref[j, 1, 0]
        values[far] = kv_ref[j, 1, 1]
    dk_sum[...] = jnp.zeros_like(dk_sum)
    dv_sum[...] = jnp.zeros_like(dv_sum)
    for half in range(2):
        block = place if half == 0 else 2 * count - 1 - place
        tiles = block // (TILE_KEYS // half_rows) + 1
        for h in range(group):
            there = (pl.ds(half * half_rows, half_rows), pl.ds(h * HD, HD))
            q_rows[pl.ds(h * half_rows, half_rows)] = q_ref[there]
            cot_rows[pl.ds(h * half_rows, half_rows)] = cot_ref[there]
        q_pos = block * half_rows + lax.broadcasted_iota(jnp.int32, (1, rows), 1) % half_rows

        def score_turn(tile, top):
            at = pl.ds(pl.multiple_of(tile * TILE_KEYS, TILE_KEYS), TILE_KEYS)
            s = dot(keys[at], q_rows[...], 1, 1) * scale
            key_pos = tile * TILE_KEYS + lax.broadcasted_iota(jnp.int32, s.shape, 0)
            s = jnp.where(key_pos <= q_pos, s, NEGATIVE)
            scores[at] = s
            return jnp.maximum(top, jnp.max(s, axis=0, keepdims=True))

        top = lax.fori_loop(0, tiles, score_turn, jnp.full((1, rows), NEGATIVE, jnp.float32))
        acc[...] = jnp.zeros_like(acc)

        def value_turn(tile, total):
            at = pl.ds(pl.multiple_of(tile * TILE_KEYS, TILE_KEYS), TILE_KEYS)
            p = jnp.exp(scores[at] - top)
            scores[at] = p
            acc[...] += dot(values[at], p.astype(jnp.bfloat16), 0, 0)
            return total + jnp.sum(p, axis=0, keepdims=True)

        total = lax.fori_loop(0, tiles, value_turn, jnp.zeros((1, rows), jnp.float32))
        inverse = 1.0 / total
        out_t = acc[...] * inverse
        out_rows = out_t.T.astype(jnp.bfloat16)
        cot_t = cot_rows[...].astype(jnp.float32).T
        delta = jnp.sum(
            cot_t * out_t.astype(jnp.bfloat16).astype(jnp.float32), axis=0, keepdims=True
        )
        acc[...] = jnp.zeros_like(acc)

        def grad_turn(tile, carry):
            at = pl.ds(pl.multiple_of(tile * TILE_KEYS, TILE_KEYS), TILE_KEYS)
            w = scores[at] * inverse
            d_prob = dot(values[at], cot_rows[...], 1, 1)
            d_score = (w * (d_prob - delta) * scale).astype(jnp.bfloat16)
            acc[...] += dot(keys[at], d_score, 0, 0)
            dk_sum[at] += dot(d_score, q_rows[...], 1, 0)
            dv_sum[at] += dot(w.astype(jnp.bfloat16), cot_rows[...], 1, 0)
            return carry

        lax.fori_loop(0, tiles, grad_turn, 0)
        dq_rows = acc[...].T.astype(jnp.bfloat16)
        for h in range(group):
            there = (pl.ds(half * half_rows, half_rows), pl.ds(h * HD, HD))
            out_ref[there] = out_rows[h * half_rows : (h + 1) * half_rows]
            dq_ref[there] = dq_rows[h * half_rows : (h + 1) * half_rows]
    for j in range(count):
        near = pl.ds(j * half_rows, half_rows)
        far = pl.ds((2 * count - 1 - j) * half_rows, half_rows)
        dkv_ref[j, 0, 0] = dk_sum[near].astype(jnp.bfloat16)
        dkv_ref[j, 0, 1] = dk_sum[far].astype(jnp.bfloat16)
        dkv_ref[j, 1, 0] = dv_sum[near].astype(jnp.bfloat16)
        dkv_ref[j, 1, 1] = dv_sum[far].astype(jnp.bfloat16)


def attention_core(queries, kv_all, attn_cotangent, place):
    tok_rows, q_cols = queries.shape
    count, _, _, half_rows, kv_cols = kv_all.shape
    kv_heads = kv_cols // HD
    width = q_cols // kv_heads
    rows = width // HD * half_rows
    total = count * tok_rows
    wide = pl.BlockSpec((tok_rows, width), lambda g, place: (0, g))
    pair = pl.BlockSpec((count, 2, 2, half_rows, HD), lambda g, place: (0, 0, 0, 0, g))
    like_q = jax.ShapeDtypeStruct(queries.shape, jnp.bfloat16)
    flops = 7 * 2 * tok_rows * q_cols * total // 2
    return pl.pallas_call(
        attention_kernel,
        out_shape=(like_q, like_q, jax.ShapeDtypeStruct(kv_all.shape, jnp.bfloat16)),
        grid_spec=pltpu.PrefetchScalarGridSpec(
            num_scalar_prefetch=1,
            grid=(kv_heads,),
            in_specs=[wide, pair, wide],
            out_specs=(wide, wide, pair),
            scratch_shapes=[
                pltpu.VMEM((total, HD), jnp.bfloat16),
                pltpu.VMEM((total, HD), jnp.bfloat16),
                pltpu.VMEM((total, HD), jnp.float32),
                pltpu.VMEM((total, HD), jnp.float32),
                pltpu.VMEM((total, rows), jnp.float32),
                pltpu.VMEM((rows, HD), jnp.bfloat16),
                pltpu.VMEM((rows, HD), jnp.bfloat16),
                pltpu.VMEM((HD, rows), jnp.float32),
            ],
        ),
        compiler_params=pltpu.CompilerParams(vmem_limit_bytes=VMEM_BYTES),
        cost_estimate=pl.CostEstimate(
            flops=3 * flops, bytes_accessed=16 * 1024 * 1024, transcendentals=total * q_cols // 2
        ),
        name="attention_both",
    )(place.reshape(1).astype(jnp.int32), queries, kv_all, attn_cotangent)


def gather_pair(kv):
    _, tok_rows, kv_cols = kv.shape
    return lax.all_gather(kv, "ctx", axis=0).reshape(
        lax.axis_size("ctx"), 2, 2, tok_rows // 2, kv_cols
    )


def scatter_pair(dkv):
    count, _, _, half_rows, kv_cols = dkv.shape
    mine = lax.psum_scatter(
        dkv.reshape(count, 2, 2 * half_rows, kv_cols), "ctx", scatter_dimension=0, tiled=False
    )
    return (mine[0], mine[1])


def in_order(ref, step, steps):
    pieces = ref.shape[0]
    early = step < steps // 2
    return [ref[jnp.where(early, j, pieces - 1 - j)] for j in range(pieces)]


def put_in_order(ref, value, step, steps):
    pieces, rows = ref.shape[0], ref.shape[1]
    early = step < steps // 2
    for j in range(pieces):
        ref[jnp.where(early, j, pieces - 1 - j)] = value[j * rows : (j + 1) * rows].astype(
            ref.dtype
        )


def whole(ref, step, steps):
    return jnp.concatenate(in_order(ref, step, steps), axis=0)


def causal_decay(col, row, flip):
    shape = (col.shape[0], row.shape[1])
    down = lax.broadcasted_iota(jnp.int32, shape, 0)
    across = lax.broadcasted_iota(jnp.int32, shape, 1)
    if flip:
        return jnp.exp(jnp.where(across >= down, row - col, NEGATIVE))
    return jnp.exp(jnp.where(down >= across, col - row, NEGATIVE))


def forward_kernel(steps, x_ref, b_ref, c_ref, col_ref, row_ref, mixed_ref, state_ref, state):
    step = pl.program_id(0)

    @pl.when(step == 0)
    def _():
        state[...] = jnp.zeros_like(state)

    x = whole(x_ref, step, steps)
    b = whole(b_ref, step, steps)
    c = whole(c_ref, step, steps)
    col, row = col_ref[...], row_ref[0]
    last = col[CHUNK - 1 : CHUNK]
    weights = (causal_decay(col, row, False) * dot(c, b, 1, 1)).astype(jnp.bfloat16)
    entering = state[...]
    entering_short = entering.astype(jnp.bfloat16)
    state_ref[0] = entering_short
    mixed = dot(weights, x, 1, 0) + jnp.exp(col) * dot(c, entering_short, 1, 0)
    put_in_order(mixed_ref, mixed, step, steps)
    shrunk = (b.astype(jnp.float32) * jnp.exp(last - col)).astype(jnp.bfloat16)
    state[...] = jnp.exp(last) * entering + dot(shrunk, x, 0, 0)


def backward_kernel(
    steps, x_ref, dm_ref, b_ref, c_ref, col_ref, row_ref, state_ref,
    input_ref, write_ref, read_ref, adjoint,
):
    step = steps - 1 - pl.program_id(0)

    @pl.when(pl.program_id(0) == 0)
    def _():
        adjoint[...] = jnp.zeros_like(adjoint)

    x = whole(x_ref, step, steps)
    dm = whole(dm_ref, step, steps)
    b = whole(b_ref, step, steps)
    c = whole(c_ref, step, steps)
    col, row = col_ref[...], row_ref[0]
    last = col[CHUNK - 1 : CHUNK]
    shrink, grow = jnp.exp(last - col), jnp.exp(col)
    entering = adjoint[...]
    entering_short = entering.astype(jnp.bfloat16)
    decay_t = causal_decay(col, row, True)
    weights_t = (decay_t * dot(b, c, 1, 1)).astype(jnp.bfloat16)
    input_g = dot(weights_t, dm, 1, 0) + shrink * dot(b, entering_short, 1, 0)
    put_in_order(input_ref, input_g, step, steps)
    pairs_t = (decay_t * dot(x, dm, 1, 1)).astype(jnp.bfloat16)
    write_g = dot(pairs_t, c, 1, 0) + shrink * dot(x, entering_short, 1, 1)
    pairs = (causal_decay(col, row, False) * dot(dm, x, 1, 1)).astype(jnp.bfloat16)
    read_g = dot(pairs, b, 1, 0) + grow * dot(dm, state_ref[0], 1, 1)
    put_in_order(write_ref, write_g, step, steps)
    put_in_order(read_ref, read_g, step, steps)
    grown = (c.astype(jnp.float32) * grow).astype(jnp.bfloat16)
    adjoint[...] = jnp.exp(last) * entering + dot(grown, dm, 0, 0)


def ssm_specs(count, half_rows, steps, order):
    per = CHUNK // half_rows

    def rows_spec(cols):
        def place(i):
            step = order(i)
            early = step < steps // 2
            return (
                jnp.where(early, step, steps - 1 - step), jnp.where(early, 0, 1), 0, 0
            )

        return pl.BlockSpec((per, pl.Squeezed(), half_rows, cols), place)

    return (
        rows_spec,
        pl.BlockSpec((CHUNK, 1), lambda i: (order(i), 0)),
        pl.BlockSpec((1, 1, CHUNK), lambda i: (order(i), 0, 0)),
    )


def scan_forward(x, b, c, col, row):
    count, _, half_rows, cols = x.shape
    states = b.shape[-1]
    steps = count * 2 * half_rows // CHUNK
    rows_spec, col_spec, row_spec = ssm_specs(count, half_rows, steps, lambda i: i)
    return pl.pallas_call(
        functools.partial(forward_kernel, steps),
        grid=(steps,),
        in_specs=[rows_spec(cols), rows_spec(states), rows_spec(states), col_spec, row_spec],
        out_specs=(rows_spec(cols), pl.BlockSpec((1, states, cols), lambda i: (i, 0, 0))),
        out_shape=(
            jax.ShapeDtypeStruct(x.shape, jnp.bfloat16),
            jax.ShapeDtypeStruct((steps, states, cols), jnp.bfloat16),
        ),
        scratch_shapes=[pltpu.VMEM((states, cols), jnp.float32)],
        compiler_params=pltpu.CompilerParams(vmem_limit_bytes=VMEM_BYTES),
        cost_estimate=pl.CostEstimate(
            flops=10**9, bytes_accessed=6 * 1024 * 1024, transcendentals=5 * 10**5
        ),
        name="scan_forward",
    )(x, b, c, col, row)


def scan_backward(x, dm, b, c, col, row, state):
    count, _, half_rows, cols = x.shape
    states = b.shape[-1]
    steps = count * 2 * half_rows // CHUNK
    rows_spec, col_spec, row_spec = ssm_specs(
        count, half_rows, steps, lambda i: steps - 1 - i
    )
    return pl.pallas_call(
        functools.partial(backward_kernel, steps),
        grid=(steps,),
        in_specs=[
            rows_spec(cols), rows_spec(cols), rows_spec(states), rows_spec(states),
            col_spec, row_spec,
            pl.BlockSpec((1, states, cols), lambda i: (steps - 1 - i, 0, 0)),
        ],
        out_specs=(rows_spec(cols), rows_spec(states), rows_spec(states)),
        out_shape=(
            jax.ShapeDtypeStruct(x.shape, jnp.bfloat16),
            jax.ShapeDtypeStruct(b.shape, jnp.bfloat16),
            jax.ShapeDtypeStruct(b.shape, jnp.bfloat16),
        ),
        scratch_shapes=[pltpu.VMEM((states, cols), jnp.float32)],
        compiler_params=pltpu.CompilerParams(vmem_limit_bytes=VMEM_BYTES),
        cost_estimate=pl.CostEstimate(
            flops=2 * 10**9, bytes_accessed=6 * 1024 * 1024, transcendentals=10**6
        ),
        name="scan_backward",
    )(x, dm, b, c, col, row, state)


def to_channels(values, extra=None):
    count = lax.axis_size("ctx")
    parts = values.reshape(values.shape[0], count, -1)
    if extra is not None:
        shape = (values.shape[0], count, extra.shape[1])
        parts = jnp.concatenate([parts, jnp.broadcast_to(extra[:, None, :], shape)], axis=2)
    blocks = jnp.transpose(parts, (1, 0, 2))
    return lax.all_to_all(blocks, "ctx", split_axis=0, concat_axis=0)


def to_owners(blocks):
    return lax.all_to_all(blocks, "ctx", split_axis=0, concat_axis=0)


def side_by_side(blocks):
    return jnp.transpose(blocks, (1, 0, 2)).reshape(blocks.shape[1], -1)


def from_other_core(values):
    return lax.ppermute(values, "tp", [(0, 1), (1, 0)])


def both_layers(
    ssm_input, ssm_gate, state_write, state_read, log_decay, skip_gain, norm_gain, ssm_cotangent,
    queries, key_states, value_states, attn_cotangent,
):
    tok_rows, channel_count = ssm_input.shape
    head_count = log_decay.shape[1]
    half_rows = tok_rows // 2
    head_dim = channel_count // head_count
    count = lax.axis_size("ctx")
    own_cols = channel_count // count
    states = state_write.shape[1]
    folded = (count, 2, half_rows)
    share_maps = lax.axis_size("tp") == 2
    kv = jnp.stack([key_states, value_states])
    kv, sent_input, log_decay = lax.optimization_barrier((kv, ssm_input, log_decay))
    kv_all = gather_pair(kv)
    if share_maps:
        first = lax.axis_index("tp") == 0
        arrived = to_channels(sent_input, jnp.where(first, state_write, state_read))
        own_map = arrived[:, :, own_cols:]
        other_map = from_other_core(own_map)
        b_all = jnp.where(first, own_map, other_map).reshape(*folded, states)
        c_all = jnp.where(first, other_map, own_map).reshape(*folded, states)
    else:
        arrived = to_channels(sent_input, jnp.concatenate([state_write, state_read], axis=1))
        b_all = arrived[:, :, own_cols : own_cols + states].reshape(*folded, states)
        c_all = arrived[:, :, own_cols + states :].reshape(*folded, states)
    x_all = arrived[:, :, :own_cols].reshape(*folded, own_cols)
    decay_rows = jnp.repeat(log_decay.T, head_dim // own_cols, axis=0)
    own_decay = to_owners(decay_rows[:, None, :]).reshape(*folded)
    ordered = jnp.concatenate([own_decay[:, 0], own_decay[::-1, 1]]).reshape(-1, CHUNK)
    upto = jnp.triu(jnp.ones((CHUNK, CHUNK), jnp.float32))
    log_total = jnp.dot(ordered, upto, precision=PRECISE)
    col = log_total.reshape(-1, 1)
    row = log_total[:, None, :]
    mixed_all, state_all = scan_forward(x_all, b_all, c_all, col, row)
    mixed_all, kv_all = lax.optimization_barrier((mixed_all, kv_all))
    attn_output, query_grad, dkv = attention_core(
        queries, kv_all, attn_cotangent, lax.axis_index("ctx")
    )
    mixed_back = to_owners(mixed_all.reshape(count, tok_rows, own_cols))
    dkv, mixed_back = lax.optimization_barrier((dkv, mixed_back))
    key_grad, value_grad = scatter_pair(dkv)
    skip = jnp.repeat(skip_gain, head_dim)[None, :]
    mixed = side_by_side(mixed_back)
    mixed = mixed.astype(jnp.float32) + skip * ssm_input.astype(jnp.float32)
    gate = ssm_gate.astype(jnp.float32)
    sigmoid = jax.nn.sigmoid(gate)
    gated = mixed * gate * sigmoid
    d_normed = ssm_cotangent.astype(jnp.float32) * norm_gain
    sums = lax.psum(
        jnp.stack([jnp.sum(gated * gated, axis=1), jnp.sum(d_normed * gated, axis=1)]), "tp"
    )
    root_mean = jnp.sqrt(sums[0] / CH + EPSILON)[:, None]
    inner_mean = (sums[1] / CH)[:, None] / root_mean
    normed = gated / root_mean
    ssm_output = (normed * norm_gain).astype(jnp.bfloat16)
    d_gated = (d_normed - normed * inner_mean) / root_mean
    d_mixed = d_gated * gate * sigmoid
    gate_grad = (d_gated * mixed * sigmoid * (1.0 + gate * (1.0 - sigmoid))).astype(jnp.bfloat16)
    dm_all = to_channels(d_mixed.astype(jnp.bfloat16)).reshape(*folded, own_cols)
    input_all, write_all, read_all = scan_backward(
        x_all, dm_all, b_all, c_all, col, row, state_all
    )
    blocks = (count, tok_rows)
    input_all = input_all.reshape(*blocks, own_cols)
    write_all, read_all = write_all.reshape(*blocks, states), read_all.reshape(*blocks, states)
    if share_maps:
        kept = jnp.where(first, write_all, read_all)
        passed = from_other_core(jnp.where(first, read_all, write_all))
        maps_all = (kept.astype(jnp.float32) + passed.astype(jnp.float32)).astype(jnp.bfloat16)
    else:
        maps_all = jnp.concatenate([write_all, read_all], axis=2)
    back = to_owners(jnp.concatenate([input_all, maps_all], axis=2))
    input_g = side_by_side(back[:, :, :own_cols]).astype(jnp.float32)
    input_grad = (input_g + skip * d_mixed).astype(jnp.bfloat16)
    maps = jnp.sum(back[:, :, own_cols:].astype(jnp.float32), axis=0)
    if share_maps:
        other = from_other_core(maps)
        write_grad, read_grad = jnp.where(first, maps, other), jnp.where(first, other, maps)
    else:
        maps = lax.psum(maps.astype(jnp.bfloat16), "tp").astype(jnp.float32)
        write_grad, read_grad = maps[:, :states], maps[:, states:]
    return (
        ssm_output, input_grad, gate_grad, write_grad, read_grad,
        attn_output, query_grad, key_grad, value_grad,
    )


MESH = pl.DeviceIdType.MESH


def remote(src, dst, send, recv, **to):
    return pltpu.make_async_remote_copy(
        src_ref=src, dst_ref=dst, send_sem=send, recv_sem=recv,
        device_id=to, device_id_type=MESH,
    )


def ring(at, step, size):
    return lax.rem(at + step, size)


def spot():
    me = lax.axis_index("ctx")
    return me, lax.div(me, 4), lax.rem(lax.div(me, 2), 2), lax.rem(me, 2)


def greet(count, me, core=None):
    barrier = pltpu.get_barrier_semaphore()
    for k in range(1, count):
        pl.semaphore_signal(
            barrier, inc=1, device_id={"ctx": ring(me, k, count)}, device_id_type=MESH
        )
    if core is not None:
        pl.semaphore_signal(barrier, inc=1, device_id={"tp": 1 - core}, device_id_type=MESH)
    pl.semaphore_wait(barrier, count - 1 if core is None else count)


def columns(p, width):
    return pl.ds(pl.multiple_of(p * width, width), width)


def cube_peer(k, cube):
    bits = [1 - at if k & bit else at for at, bit in zip(cube, (4, 2, 1))]
    return bits[0] * 4 + bits[1] * 2 + bits[2]


def spread(base, cube, pick, place, send, recv):
    mine = cube_peer(0, cube)
    copies = []
    for k in (7, 4, 2, 1, 6, 5, 3):
        p = cube_peer(k, cube)
        copy = remote(pick(p), place(mine), send.at[k], recv.at[k], ctx=base + p)
        copy.start()
        copies.append(copy)
    local = pltpu.make_async_copy(pick(mine), place(mine), send.at[0])
    local.start()
    return local, copies


def settle(pieces):
    local, copies = pieces
    for copy in copies:
        copy.wait_recv()
    for copy in copies:
        copy.wait_send()
    local.wait()


def index_of(z, y, x):
    return z * 4 + y * 2 + x


def gather_turns(own, dest, cols, where, send, recv, local):
    _, z, y, x = where
    depth = dest.shape[0]
    used = []

    def post(src, dst, to):
        copy = remote(src, dst, send.at[len(used)], recv.at[len(used)], ctx=to)
        copy.start()
        used.append(copy)
        return copy

    def block(at, c):
        return dest.at[at, y, x, c, :, cols]

    mine = [
        pltpu.make_async_copy(own[c].at[:, cols], block(z, c), local.at[c]) for c in range(2)
    ]
    for copy in mine:
        copy.start()
    over_x, over_y = index_of(z, y, 1 - x), index_of(z, 1 - y, x)
    first = [
        post(own[0].at[:, cols], block(z, 0), over_x),
        post(own[1].at[:, cols], block(z, 1), over_y),
    ]
    along = {}
    for k in (2, 3, 1):
        to = index_of(ring(z, k, depth), y, x)
        along[k] = [post(own[c].at[:, cols], block(z, c), to) for c in range(2)]
    yield
    for copy in mine:
        copy.wait()

    def pair(at, arrived):
        arrived[0].wait_recv()
        keys = dest.at[at, y, :, 0, :, cols]
        a = post(keys, keys, over_y)
        arrived[1].wait_recv()
        values = dest.at[at, :, x, 1, :, cols]
        return a, post(values, values, over_x)

    ends = list(pair(z, first))
    yield
    onward = {}
    for k in (2, 3, 1):
        at = ring(z, depth - k, depth)
        for copy in along[k]:
            copy.wait_recv()
        onward[k] = [post(block(at, 0), block(at, 0), over_x), post(block(at, 1), block(at, 1), over_y)]
        yield
    for k in (2, 3, 1):
        ends += pair(ring(z, depth - k, depth), onward[k])
        yield
    for copy in ends:
        copy.wait_recv()
    for copy in used:
        copy.wait_send()


def gather_copies(depth):
    return 2 + 2 * (depth - 1) * 3 + 2


def scatter_turns(terms, cols, out, half_way, next_way, last_way, where, send, recv):
    _, z, y, x = where
    depth = terms.shape[0]
    used = []

    def post(src, dst, to):
        copy = remote(src, dst, send.at[len(used)], recv.at[len(used)], ctx=to)
        copy.start()
        used.append(copy)
        return copy

    def wide(value):
        return value.astype(jnp.float32)

    over_x, over_y = index_of(z, y, 1 - x), index_of(z, 1 - y, x)
    order = list(range(1, depth)) + [0]
    first, second, third = {}, {}, []
    for k in order:
        at = ring(z, k, depth)
        first[k] = (
            post(terms.at[at, 1 - y, :, 0, :, cols], half_way.at[0, at, :, :, cols], over_y),
            post(terms.at[at, :, 1 - x, 1, :, cols], half_way.at[1, at, :, :, cols], over_x),
        )
    yield
    for k in order:
        at = ring(z, k, depth)
        first[k][0].wait_recv()
        half_way[0, at, 1 - x, :, cols] = (
            wide(half_way[0, at, 1 - x, :, cols]) + wide(terms[at, y, 1 - x, 0, :, cols])
        ).astype(jnp.bfloat16)
        a = post(half_way.at[0, at, 1 - x, :, cols], next_way.at[0, at, :, cols], over_x)
        first[k][1].wait_recv()
        half_way[1, at, 1 - y, :, cols] = (
            wide(half_way[1, at, 1 - y, :, cols]) + wide(terms[at, 1 - y, x, 1, :, cols])
        ).astype(jnp.bfloat16)
        second[k] = (a, post(half_way.at[1, at, 1 - y, :, cols], next_way.at[1, at, :, cols], over_y))
        yield
    for k in order:
        at = ring(z, k, depth)
        for c in range(2):
            second[k][c].wait_recv()
            total = (
                wide(next_way[c, at, :, cols]) + wide(half_way[c, at, y if c else x, :, cols])
                + wide(terms[at, y, x, c, :, cols])
            )
            next_way[c, at, :, cols] = total.astype(jnp.bfloat16)
            if k:
                there = last_way.at[c, k - 1, :, cols]
                third.append(post(next_way.at[c, at, :, cols], there, index_of(at, y, x)))
        yield
    for copy in third:
        copy.wait_recv()
    for c in range(2):
        total = wide(next_way[c, z, :, cols])
        for k in range(1, depth):
            total = total + wide(last_way[c, k - 1, :, cols])
        out[c][:, cols] = total.astype(jnp.bfloat16)
    for copy in used:
        copy.wait_send()


def scatter_copies(depth):
    return 4 * depth + 2 * (depth - 1)


def running_decay(decay, rows, first, half_rows):
    per = CHUNK // half_rows
    groups = decay.shape[0] // per
    width = 2 * half_rows
    side = jnp.concatenate(
        [
            jnp.concatenate([decay[g * per + j] for g in range(groups)], axis=0)
            for j in range(per)
        ],
        axis=1,
    )
    shape = (per * width, 2 * CHUNK)
    r = lax.broadcasted_iota(jnp.int32, shape, 0)
    u = lax.broadcasted_iota(jnp.int32, shape, 1)
    j, t = r // width, r % width
    near = (t < half_rows) & (u < CHUNK) & (j * half_rows + t <= u)
    far = (t >= half_rows) & (u >= CHUNK)
    far = far & ((per - 1 - j) * half_rows + t - half_rows <= u - CHUNK)
    ones = jnp.where(near | far, 1.0, 0.0)
    sums = lax.dot_general(
        side, ones, (((1,), (0,)), ((), ())), precision=PRECISE,
        preferred_element_type=jnp.float32,
    )
    for i in range(groups):
        rows[first + i] = sums[i : i + 1, :CHUNK]
        rows[first + groups + i] = sums[i : i + 1, CHUNK:]


def members(group, half, per):
    return [per * group + (j if half == 0 else per - 1 - j) for j in range(per)]


def put_chunk(ref, ids, half, half_rows, value):
    value = value.astype(ref.dtype)
    for j, d in enumerate(ids):
        ref[d, half * half_rows : (half + 1) * half_rows] = value[
            j * half_rows : (j + 1) * half_rows
        ]


def as_column(row):
    shape = (row.shape[1], row.shape[1])
    same = lax.broadcasted_iota(jnp.int32, shape, 0) == lax.broadcasted_iota(jnp.int32, shape, 1)
    return jnp.sum(jnp.where(same, row, 0.0), axis=1, keepdims=True)


def layers_kernel(
    x_hbm, gate_hbm, write_hbm, read_hbm, decay_hbm, skip_ref, gain_ref, up_hbm,
    q_hbm, k_hbm, v_hbm, cot_hbm,
    ssm_out, input_out, gate_out, write_out, read_out, attn_out, query_out, key_out, value_out,
    x_ref, gate_ref, up_ref, q_ref, cot_ref, own_map,
    decay, rows, cols_ref, sums, states, summary, summary_in, fade, fade_in, x_all, maps, mixed_all, mixed_back,
    sums_mine, sums_theirs, dm_ref, dm_wide, dm_all, input_back,
    map_terms, map_in, map_back, map_mine, map_theirs,
    kv_all, terms, half_way, next_way, last_way,
    adjoints, scores, tops, dk_sum, dv_sum, q_rows, cot_rows, acc,
    ssm_ref, input_ref, gate_grad, attn_ref, dq_ref,
    x_send, x_recv, d_send, d_recv, b_send, b_recv, m_send, m_recv, i_send, i_recv,
    p_send, p_recv, map_send, map_recv, g_send, g_recv, g_local, s_send, s_recv,
    t_send, t_recv, h_send, h_recv, load_sem, store_sem,
):
    where = spot()
    me, z, y, x = where
    core = lax.axis_index("tp")
    members_count, tok_rows, own_cols = x_all.shape
    heads = decay.shape[0]
    head_dim = own_cols // heads
    channels = x_ref.shape[1]
    half_rows = tok_rows // 2
    depth = kv_all.shape[0]
    count = depth * 4
    per = CHUNK // half_rows
    groups = members_count // per
    outer, inner_z = lax.div(z, 2), lax.rem(z, 2)
    base, cube = outer * members_count, (inner_z, y, x)
    early = outer == 0
    partner = index_of(ring(z, 2, depth), y, x)
    kv_cols = k_hbm.shape[1]
    kv_heads = kv_cols // HD
    group_cols = q_ref.shape[1] // kv_heads
    group_size = group_cols // HD
    q_count = group_size * half_rows

    def unit_cols(unit):
        return slice(unit[0] * HD, unit[-1] * HD + HD)

    scale = HD ** (-0.5)
    to_exp2 = scale * 1.4426950408889634

    loads = {}
    for i, (name, src, dst) in enumerate((
        ("q", q_hbm, q_ref), ("cot", cot_hbm, cot_ref), ("x", x_hbm, x_ref),
        ("gate", gate_hbm, gate_ref), ("up", up_hbm, up_ref),
    )):
        loads[name] = pltpu.make_async_copy(src, dst, load_sem.at[i])
        loads[name].start()
    own_map_sem = load_sem.at[len(loads)]

    @pl.when(core == 0)
    def _():
        pltpu.make_async_copy(write_hbm, own_map, own_map_sem).start()

    @pl.when(core != 0)
    def _():
        pltpu.make_async_copy(read_hbm, own_map, own_map_sem).start()

    greet(count, me, core)
    decays = spread(
        base, cube, lambda p: decay_hbm.at[:, p], lambda p: decay.at[:, p],
        d_send, d_recv,
    )
    pltpu.make_async_copy(write_hbm, own_map, own_map_sem).wait()
    copy_map = pltpu.make_async_copy(own_map, maps.at[core, inner_z, y, x], m_send.at[0])
    copy_map.start()
    used = []

    def post(src, dst, **to):
        copy = remote(src, dst, m_send.at[len(used) + 1], m_recv.at[len(used) + 1], **to)
        copy.start()
        used.append(copy)
        return copy

    post(own_map, maps.at[core, inner_z, y, x], ctx=base + cube_peer(4, cube))
    inputs = spread(
        base, cube, lambda p: x_hbm.at[:, columns(p, own_cols)], lambda p: x_all.at[p],
        x_send, x_recv,
    )
    gathers = [
        gather_turns(
            (k_hbm, v_hbm), kv_all, unit_cols(unit), where, g_send.at[i], g_recv.at[i],
            g_local.at[i],
        )
        for i, unit in enumerate(GATHER_UNITS)
    ]
    scatters = [
        scatter_turns(
            terms, unit_cols(unit), (key_out, value_out), half_way, next_way, last_way, where,
            s_send.at[i], s_recv.at[i],
        )
        for i, unit in enumerate(SCATTER_UNITS)
    ]

    def turn(turns, times=1):
        for _ in range(times):
            next(turns, None)

    def finish(turns):
        for _ in turns:
            pass

    turn(gathers[0])
    for copy in used:
        copy.wait_recv()
    copy_map.wait()
    part = maps.at[core, :, y, x]
    post(part, part, ctx=index_of(z, y, 1 - x)).wait_recv()
    part = maps.at[core, :, y]
    post(part, part, ctx=index_of(z, 1 - y, x)).wait_recv()
    part = maps.at[core]
    over = post(part, part, tp=1 - core)
    turn(gathers[0])
    settle(decays)
    for h in range(heads):
        running_decay(decay.at[h], rows, h * 2 * groups, half_rows)

    @pl.loop(0, 2 * heads * groups)
    def _(i):
        cols_ref[i] = jnp.broadcast_to(as_column(rows[i]), (CHUNK, HD))

    over.wait_recv()
    for copy in used:
        copy.wait_send()
    settle(inputs)
    turn(gathers[1])

    def chunk_map(which, group, half):
        js = range(per) if half == 0 else range(per - 1, -1, -1)
        at = slice(half * half_rows, (half + 1) * half_rows)
        return jnp.concatenate([maps[which, group, j // 2, j % 2, at] for j in js], axis=0)

    def logs(group, half, h):
        row = rows[(h * 2 + half) * groups + group]
        col = cols_ref[(h * 2 + half) * groups + group][:, :1]
        return row, col, col[CHUNK - 1 : CHUNK]

    def of_head(h):
        return slice(h * head_dim, (h + 1) * head_dim)

    def chunk_head(ref, group, half, h):
        ids = members(group, half, per)
        return jnp.concatenate(
            [ref[d, half * half_rows : (half + 1) * half_rows, of_head(h)] for d in ids], axis=0
        )

    def put_head(ref, group, half, h, value):
        value = value.astype(ref.dtype)
        for j, d in enumerate(members(group, half, per)):
            ref[d, half * half_rows : (half + 1) * half_rows, of_head(h)] = value[
                j * half_rows : (j + 1) * half_rows
            ]

    def total_log(group, half, h):
        return rows[(h * 2 + half) * groups + group][:, CHUNK - 1 : CHUNK]

    def run_order(half):
        return (0, 1) if half == 0 else (1, 0)

    def chunk_sums(which, grow):
        source = dm_all if grow else x_all

        @pl.loop(0, groups)
        def _(group):
            for half in range(2):
                maps_here = chunk_map(which, group, half).astype(jnp.float32)
                for h in range(heads):
                    _, col, last = logs(group, half, h)
                    scaled = (maps_here * jnp.exp(col if grow else last - col)).astype(
                        jnp.bfloat16
                    )
                    sums[half, group, :, of_head(h)] = dot(
                        scaled, chunk_head(source, group, half, h), 0, 0
                    )

    def run_sum(half, h, back):
        first, then = run_order(half)[::-1] if back else run_order(half)
        return (
            jnp.exp(total_log(then, half, h)) * sums[half, first, :, of_head(h)]
            + sums[half, then, :, of_head(h)]
        )

    def run_log(half, h):
        return total_log(0, half, h) + total_log(1, half, h)

    def send_summary(slot, back):
        near, far = (1, 0) if back else (0, 1)
        for h in range(heads):
            one, two = run_sum(near, h, back), run_sum(far, h, back)
            joined = jnp.exp(run_log(far, h)) * one + two
            summary[slot, :, of_head(h)] = jnp.where(early, one, joined).astype(jnp.bfloat16)
        copy = remote(
            summary.at[slot], summary_in.at[slot], h_send.at[slot], h_recv.at[slot], ctx=partner
        )
        copy.start()
        return copy

    def entering(slot, half, h, back):
        near, far = (1, 0) if back else (0, 1)
        there = summary_in[slot, :, of_head(h)].astype(jnp.float32)
        if half == near:
            return jnp.where(early, 0.0, there)
        other = fade_in[0:1, h * HD : h * HD + 1]
        own = run_sum(near, h, back)
        return jnp.where(
            early, jnp.exp(other) * own + there, jnp.exp(run_log(near, h)) * there + own
        )

    def chunk_entering(slot, half, h, back):
        first, then = run_order(half)[::-1] if back else run_order(half)
        value = entering(slot, half, h, back)
        later = jnp.exp(total_log(first, half, h)) * value + sums[half, first, :, of_head(h)]
        return {first: value, then: later}

    def forward_within(group):
        for half in range(2):
            b, c = chunk_map(0, group, half), chunk_map(1, group, half)
            pairs_cb = dot(c, b, 1, 1)
            for h in range(heads):
                row, col, _ = logs(group, half, h)
                weights = (causal_decay(col, row, False) * pairs_cb).astype(jnp.bfloat16)
                put_head(
                    dm_wide, group, half, h,
                    dot(weights, chunk_head(x_all, group, half, h), 1, 0),
                )

    def forward_across(group):
        for half in range(2):
            c = chunk_map(1, group, half)
            for h in range(heads):
                _, col, _ = logs(group, half, h)
                across = jnp.exp(col) * dot(c, states[half, group, :, of_head(h)], 1, 0)
                put_head(
                    mixed_all, group, half, h, chunk_head(dm_wide, group, half, h) + across
                )

    def backward(group):
        for half in range(2):
            b, c = chunk_map(0, group, half), chunk_map(1, group, half)
            pairs_bc = dot(b, c, 1, 1)
            write_g = read_g = 0.0
            for h in range(heads):
                value = chunk_head(x_all, group, half, h)
                dm = chunk_head(dm_all, group, half, h)
                row, col, last = logs(group, half, h)
                shrink, grow = jnp.exp(last - col), jnp.exp(col)
                later = adjoints[half, group, :, of_head(h)]
                decay_t = causal_decay(col, row, True)
                weights_t = (decay_t * pairs_bc).astype(jnp.bfloat16)
                input_g = dot(weights_t, dm, 1, 0) + shrink * dot(b, later, 1, 0)
                put_head(mixed_all, group, half, h, input_g)
                pairs_t = (decay_t * dot(value, dm, 1, 1)).astype(jnp.bfloat16)
                write_g = write_g + dot(pairs_t, c, 1, 0) + shrink * dot(value, later, 1, 1)
                pairs_f = (causal_decay(col, row, False) * dot(dm, value, 1, 1)).astype(
                    jnp.bfloat16
                )
                state = states[half, group, :, of_head(h)]
                read_g = read_g + dot(pairs_f, b, 1, 0) + grow * dot(dm, state, 1, 1)
            ids = members(group, half, per)
            put_chunk(map_terms.at[0], ids, half, half_rows, write_g)
            put_chunk(map_terms.at[1], ids, half, half_rows, read_g)

    wide_cols = own_cols
    strip = 16

    def pieces_of(r):
        at = pl.ds(pl.multiple_of(r * strip, strip), strip)
        for c in range(channels // wide_cols):
            cols = slice(c * wide_cols, (c + 1) * wide_cols)
            gate = gate_ref[at, cols].astype(jnp.float32)
            sigmoid = 0.5 * jnp.tanh(0.5 * gate) + 0.5
            mixed = mixed_back[at, cols].astype(jnp.float32) + skip_ref[:, cols] * x_ref[
                at, cols
            ].astype(jnp.float32)
            d_normed = up_ref[at, cols].astype(jnp.float32) * gain_ref[:, cols]
            yield at, cols, gate, sigmoid, mixed, d_normed

    def norm():
        @pl.loop(0, tok_rows // strip)
        def _(r):
            squares = jnp.zeros((strip, 1), jnp.float32)
            inner = jnp.zeros((strip, 1), jnp.float32)
            for at, cols, gate, sigmoid, mixed, d_normed in pieces_of(r):
                gated = mixed * gate * sigmoid
                squares = squares + jnp.sum(gated * gated, axis=1, keepdims=True)
                inner = inner + jnp.sum(d_normed * gated, axis=1, keepdims=True)
            sums_mine[0, at] = jnp.broadcast_to(squares, (strip, HD))
            sums_mine[1, at] = jnp.broadcast_to(inner, (strip, HD))

        swap = remote(sums_mine, sums_theirs, t_send.at[0], t_recv.at[0], tp=1 - core)
        swap.start()
        swap.wait()

        @pl.loop(0, tok_rows // strip)
        def _(r):
            at = pl.ds(pl.multiple_of(r * strip, strip), strip)
            squares = sums_mine[0, at] + sums_theirs[0, at]
            inner = sums_mine[1, at] + sums_theirs[1, at]
            inverse = 1.0 / jnp.sqrt(squares[:, :1] / CH + EPSILON)
            inner_mean = inner[:, :1] / CH * inverse
            for at, cols, gate, sigmoid, mixed, d_normed in pieces_of(r):
                silu = gate * sigmoid
                normed = mixed * silu * inverse
                ssm_ref[at, cols] = (normed * gain_ref[:, cols]).astype(jnp.bfloat16)
                d_gated = (d_normed - normed * inner_mean) * inverse
                d_mixed = d_gated * silu
                dm_ref[at, cols] = d_mixed.astype(jnp.bfloat16)
                dm_wide[cols.start // wide_cols, at] = skip_ref[:, cols] * d_mixed
                gate_grad[at, cols] = (
                    d_gated * mixed * sigmoid * (1.0 + gate * (1.0 - sigmoid))
                ).astype(jnp.bfloat16)

    def attend(head, half):
        cols = slice(head * HD, (head + 1) * HD)
        token_at = slice(half * half_rows, (half + 1) * half_rows)
        for h in range(group_size):
            q_at = slice(head * group_cols + h * HD, head * group_cols + (h + 1) * HD)
            q_rows[h * half_rows : (h + 1) * half_rows] = q_ref[token_at, q_at]
            cot_rows[h * half_rows : (h + 1) * half_rows] = cot_ref[token_at, q_at]
        if half == 1:
            dk_sum[...] = jnp.zeros_like(dk_sum)
            dv_sum[...] = jnp.zeros_like(dv_sum)

        def tile(c, plane, side):
            block = kv_all[
                plane, :, :, c, side * half_rows : (side + 1) * half_rows, cols
            ]
            return block.reshape(4 * half_rows, HD)

        def score_turn(plane, side, carry, edge):
            top, total = carry
            s = dot(tile(0, plane, side), q_rows[...], 1, 1) * to_exp2
            if edge:
                r = lax.broadcasted_iota(jnp.int32, s.shape, 0)
                q = lax.broadcasted_iota(jnp.int32, s.shape, 1) % half_rows
                j, mine = r // half_rows, 2 * y + x
                if side:
                    j, mine = 3 - j, 3 - mine
                s = jnp.where(j * half_rows + r % half_rows <= mine * half_rows + q, s, NEGATIVE)
            higher = jnp.maximum(top, jnp.max(s, axis=0, keepdims=True))
            p = jnp.exp2(s - higher)
            short = p.astype(jnp.bfloat16)
            at = side * depth + plane
            scores[at] = short
            tops[at] = higher
            fade = jnp.exp2(top - higher)
            acc[...] = acc[...] * fade + dot(tile(1, plane, side), short, 0, 0)
            return higher, total * fade + jnp.sum(p, axis=0, keepdims=True)

        acc[...] = jnp.zeros_like(acc)
        start = (jnp.full((1, q_count), NEGATIVE, jnp.float32), jnp.zeros((1, q_count), jnp.float32))
        carry = score_turn(z, half, start, True)
        if half == 0:
            carry = lax.fori_loop(0, z, lambda t, c: score_turn(t, 0, c, False), carry)
        else:
            carry = lax.fori_loop(0, depth, lambda t, c: score_turn(t, 0, c, False), carry)
            carry = lax.fori_loop(z + 1, depth, lambda t, c: score_turn(t, 1, c, False), carry)
        top, total = carry
        inverse = 1.0 / total
        out_t = acc[...] * inverse
        out_rows = out_t.T.astype(jnp.bfloat16)
        cot_t = cot_rows[...].astype(jnp.float32).T
        delta = jnp.sum(
            cot_t * out_t.astype(jnp.bfloat16).astype(jnp.float32), axis=0, keepdims=True
        )
        acc[...] = jnp.zeros_like(acc)

        def grad_turn(plane, side):
            at = side * depth + plane
            w = scores[at].astype(jnp.float32) * (jnp.exp2(tops[at] - top) * inverse)
            d_prob = dot(tile(1, plane, side), cot_rows[...], 1, 1)
            d_score = (w * (d_prob - delta)).astype(jnp.bfloat16)
            acc[...] += dot(tile(0, plane, side), d_score, 0, 0)
            dk_sum[at] += dot(d_score, q_rows[...], 1, 0)
            dv_sum[at] += dot(w.astype(jnp.bfloat16), cot_rows[...], 1, 0)

        if half == 0:
            pl.loop(0, z + 1)(lambda t: grad_turn(t, 0))
        else:
            pl.loop(0, depth)(lambda t: grad_turn(t, 0))
            pl.loop(z, depth)(lambda t: grad_turn(t, 1))
        dq_rows = (acc[...] * scale).T.astype(jnp.bfloat16)
        for h in range(group_size):
            q_at = slice(head * group_cols + h * HD, head * group_cols + (h + 1) * HD)
            attn_ref[token_at, q_at] = out_rows[h * half_rows : (h + 1) * half_rows]
            dq_ref[token_at, q_at] = dq_rows[h * half_rows : (h + 1) * half_rows]
        if half == 0:
            for side in range(2):
                key_at = slice(side * half_rows, (side + 1) * half_rows)

                @pl.loop(0, depth)
                def _(plane):
                    at = side * depth + plane
                    for c, (ref, by) in enumerate(((dk_sum, scale), (dv_sum, 1.0))):
                        block = (ref[at] * by).astype(jnp.bfloat16)
                        terms[plane, :, :, c, key_at, cols] = block.reshape(2, 2, half_rows, HD)

    stores = []

    def store(src, dst):
        copy = pltpu.make_async_copy(src, dst, store_sem.at[len(stores)])
        copy.start()
        stores.append(copy)

    for h in range(heads):
        fade[:, h * HD : (h + 1) * HD] = jnp.broadcast_to(run_log(0, h) + run_log(1, h), (8, HD))
    fades = remote(fade, fade_in, h_send.at[2], h_recv.at[2], ctx=partner)
    fades.start()
    chunk_sums(0, False)
    summaries = send_summary(0, False)
    turn(gathers[0], depth - 1)
    pl.loop(0, groups)(forward_within)
    turn(gathers[0], depth - 1)
    fades.wait()
    summaries.wait()
    for half in range(2):
        for h in range(heads):
            for group, value in chunk_entering(0, half, h, False).items():
                states[half, group, :, of_head(h)] = value.astype(jnp.bfloat16)
    pl.loop(0, groups)(forward_across)
    back = spread(
        base, cube, lambda p: mixed_all.at[p], lambda p: mixed_back.at[:, columns(p, own_cols)],
        b_send, b_recv,
    )
    turn(gathers[1])
    for copy in loads.values():
        copy.wait()
    finish(gathers[0])
    attend(0, 1)
    turn(gathers[1], depth - 1)
    settle(back)
    norm()
    d_mixed = spread(
        base, cube, lambda p: dm_ref.at[:, columns(p, own_cols)], lambda p: dm_all.at[p],
        p_send, p_recv,
    )
    store(ssm_ref, ssm_out)
    store(gate_grad, gate_out)
    turn(gathers[1], depth - 1)
    attend(0, 0)
    attend(1, 1)
    settle(d_mixed)
    chunk_sums(1, True)
    summaries = send_summary(1, True)
    attend(1, 0)
    turn(scatters[0])
    finish(gathers[1])
    summaries.wait()
    for half in range(2):
        for h in range(heads):
            for group, value in chunk_entering(1, half, h, True).items():
                adjoints[half, group, :, of_head(h)] = value.astype(jnp.bfloat16)
    turn(scatters[0], 2)
    pl.loop(0, groups)(backward)
    over = remote(map_terms.at[1 - core], map_in, t_send.at[1], t_recv.at[1], tp=1 - core)
    over.start()
    sent_back = spread(
        base, cube, lambda p: mixed_all.at[p], lambda p: input_back.at[:, columns(p, own_cols)],
        i_send, i_recv,
    )
    turn(scatters[0], depth - 2)
    over.wait_recv()

    @pl.loop(0, members_count)
    def _(d):
        map_in[d] = (
            map_in[d].astype(jnp.float32) + map_terms[core, d].astype(jnp.float32)
        ).astype(jnp.bfloat16)

    map_pieces = spread(
        base, cube, lambda p: map_in.at[p], lambda p: map_back.at[p], map_send, map_recv
    )
    attend(2, 1)
    turn(scatters[0], 2)
    attend(2, 0)
    turn(scatters[1])
    turn(scatters[0], depth - 2)
    attend(3, 1)
    finish(scatters[0])
    turn(scatters[1], depth)
    attend(3, 0)
    turn(scatters[2])
    store(attn_ref, attn_out)
    store(dq_ref, query_out)
    finish(scatters[1])
    settle(map_pieces)
    total = map_back[0].astype(jnp.float32)
    for d in range(1, members_count):
        total = total + map_back[d].astype(jnp.float32)
    map_mine[...] = total
    other = remote(map_mine, map_theirs, t_send.at[2], t_recv.at[2], tp=1 - core)
    other.start()
    settle(sent_back)
    turn(scatters[2], depth)

    @pl.loop(0, tok_rows // strip)
    def _(r):
        at = pl.ds(pl.multiple_of(r * strip, strip), strip)
        for c in range(channels // wide_cols):
            cols = slice(c * wide_cols, (c + 1) * wide_cols)
            input_ref[at, cols] = (
                input_back[at, cols].astype(jnp.float32) + dm_wide[c, at]
            ).astype(jnp.bfloat16)

    store(input_ref, input_out)
    turn(scatters[2], depth)
    other.wait_recv()
    first = core == 0
    write_out[...] = jnp.where(first, map_mine[...], map_theirs[...])
    read_out[...] = jnp.where(first, map_theirs[...], map_mine[...])
    other.wait_send()
    over.wait_send()
    finish(scatters[2])
    for copy in stores:
        copy.wait()


def both_layers_direct(
    ssm_input, ssm_gate, state_write, state_read, log_decay, skip_gain, norm_gain, ssm_cotangent,
    queries, key_states, value_states, attn_cotangent,
):
    tok_rows, channel_count = ssm_input.shape
    head_count = log_decay.shape[1]
    head_dim = channel_count // head_count
    count = lax.axis_size("ctx")
    group = count // 2
    own_cols = channel_count // group
    heads = own_cols // head_dim
    size = state_write.shape[1]
    kv_cols = key_states.shape[1]
    depth = count // 4
    chunks = group * tok_rows // 2 // CHUNK
    q_count = queries.shape[1] // (kv_cols // HD) // HD * tok_rows // 2
    decay_rows = jnp.transpose(log_decay.reshape(tok_rows, group, heads), (2, 1, 0))[:, :, None]
    skip = jnp.repeat(skip_gain, head_dim)[None, :]
    short, full = jnp.bfloat16, jnp.float32
    hbm = pl.BlockSpec(memory_space=pl.ANY)
    vmem = pl.BlockSpec(memory_space=pltpu.VMEM)
    dma = pltpu.SemaphoreType.DMA
    big = jax.ShapeDtypeStruct(ssm_input.shape, short)
    grad = jax.ShapeDtypeStruct(state_write.shape, full)
    small = jax.ShapeDtypeStruct(key_states.shape, short)
    wide = pltpu.VMEM(ssm_input.shape, short)
    by_channel = pltpu.VMEM((group, tok_rows, own_cols), short)
    map_shape = (group, tok_rows, size)
    square = pltpu.VMEM((tok_rows, size), full)
    n_g, n_s = len(GATHER_UNITS), len(SCATTER_UNITS)
    n_gather, n_scatter = gather_copies(depth), scatter_copies(depth)
    results = pl.pallas_call(
        layers_kernel,
        in_specs=[hbm] * 5 + [vmem] * 2 + [hbm] * 5,
        out_specs=(hbm, hbm, hbm, vmem, vmem, hbm, hbm, vmem, vmem),
        out_shape=(big, big, big, grad, grad, big, big, small, small),
        scratch_shapes=[
            wide, wide, wide, wide, wide, pltpu.VMEM((tok_rows, size), short),
            pltpu.VMEM((heads, group, 1, tok_rows), full),
            pltpu.VMEM((heads * 2 * chunks, 1, CHUNK), full),
            pltpu.VMEM((heads * 2 * chunks, CHUNK, HD), full),
            pltpu.VMEM((2, chunks, size, own_cols), full),
            pltpu.VMEM((2, chunks, size, own_cols), short),
            pltpu.VMEM((2, size, own_cols), short),
            pltpu.VMEM((2, size, own_cols), short),
            pltpu.VMEM((8, heads * HD), full),
            pltpu.VMEM((8, heads * HD), full),
            by_channel,
            pltpu.VMEM((2, 2, 2, 2, tok_rows, size), short),
            by_channel, wide,
            pltpu.VMEM((2, tok_rows, HD), full),
            pltpu.VMEM((2, tok_rows, HD), full),
            wide,
            pltpu.VMEM((group, tok_rows, own_cols), full),
            by_channel, wide,
            pltpu.VMEM((2,) + map_shape, short),
            pltpu.VMEM(map_shape, short),
            pltpu.VMEM(map_shape, short),
            square, square,
            pltpu.VMEM((depth, 2, 2, 2, tok_rows, kv_cols), short),
            pltpu.VMEM((depth, 2, 2, 2, tok_rows, kv_cols), short),
            pltpu.VMEM((2, depth, 2, tok_rows, kv_cols), short),
            pltpu.VMEM((2, depth, tok_rows, kv_cols), short),
            pltpu.VMEM((2, depth - 1, tok_rows, kv_cols), short),
            pltpu.VMEM((2, chunks, size, own_cols), short),
            pltpu.VMEM((2 * depth, 2 * tok_rows, q_count), short),
            pltpu.VMEM((2 * depth, 1, q_count), full),
            pltpu.VMEM((2 * depth, 2 * tok_rows, HD), full),
            pltpu.VMEM((2 * depth, 2 * tok_rows, HD), full),
            pltpu.VMEM((q_count, HD), short),
            pltpu.VMEM((q_count, HD), short),
            pltpu.VMEM((HD, q_count), full),
            wide, wide, wide, wide, wide,
            dma((group,)), dma((group,)), dma((group,)), dma((group,)), dma((group,)),
            dma((group,)), dma((5,)), dma((5,)), dma((group,)), dma((group,)),
            dma((group,)), dma((group,)), dma((group,)), dma((group,)),
            dma((n_g, n_gather)), dma((n_g, n_gather)), dma((n_g, 2)),
            dma((n_s, n_scatter)), dma((n_s, n_scatter)),
            dma((3,)), dma((3,)), dma((3,)), dma((3,)), dma((6,)), dma((5,)),
        ],
        compiler_params=pltpu.CompilerParams(
            collective_id=0, has_side_effects=True, vmem_limit_bytes=VMEM_LARGE
        ),
        cost_estimate=pl.CostEstimate(
            flops=10**10, bytes_accessed=32 * 1024 * 1024, transcendentals=10**7
        ),
        name="both_layers",
    )(
        ssm_input, ssm_gate, state_write, state_read, decay_rows, skip, norm_gain[None, :],
        ssm_cotangent, queries, key_states, value_states, attn_cotangent,
    )
    return hand_over(results)


def hand_over_kernel(*refs):
    n = len(refs) // 3
    sources, targets, held, sems = refs[:n], refs[n : 2 * n], refs[2 * n : 3 * n], refs[-1]
    ins = [pltpu.make_async_copy(sources[i], held[i], sems.at[0, i]) for i in range(n)]
    outs = [pltpu.make_async_copy(held[i], targets[i], sems.at[1, i]) for i in range(n)]
    for copy in ins:
        copy.start()
    for i in range(n):
        ins[i].wait()
        outs[i].start()
    for copy in outs:
        copy.wait()


def hand_over(results):
    n = len(results)
    hbm = pl.BlockSpec(memory_space=pl.ANY)
    return pl.pallas_call(
        hand_over_kernel,
        in_specs=[hbm] * n,
        out_specs=(hbm,) * n,
        out_shape=tuple(jax.ShapeDtypeStruct(r.shape, r.dtype) for r in results),
        scratch_shapes=[pltpu.VMEM(r.shape, r.dtype) for r in results]
        + [pltpu.SemaphoreType.DMA((2, n))],
        compiler_params=pltpu.CompilerParams(vmem_limit_bytes=VMEM_LARGE),
        name="hand_over",
    )(*results)


def direct(mesh):
    return mesh.shape["tp"] == 2 and mesh.shape["ctx"] == 16


def solution(mesh):
    placed = (
        P("ctx", "tp"),
        P("ctx", "tp"),
        P("ctx", None),
        P("ctx", None),
        P("ctx", "tp"),
        P("tp"),
        P("tp"),
        P("ctx", "tp"),
        P("ctx", "tp"),
        P("ctx", "tp"),
        P("ctx", "tp"),
        P("ctx", "tp"),
    )
    return jax.shard_map(
        both_layers_direct if direct(mesh) else both_layers,
        mesh=mesh,
        in_specs=placed,
        out_specs=(
            P("ctx", "tp"),
            P("ctx", "tp"),
            P("ctx", "tp"),
            P("ctx", None),
            P("ctx", None),
            P("ctx", "tp"),
            P("ctx", "tp"),
            P("ctx", "tp"),
            P("ctx", "tp"),
        ),
        check_vma=False,
    )
```
